32 devices in a mesh: dp: 4 (over y, x), sp: 8 (over z, core).
Axes of the slice: x: 2, y: 2, z: 4, core: 2. Of those that a mesh axis runs over, the one named last changes fastest.
Arguments:
- tokens: bfloat16 [2, 4, 1024, 768], P(None, 'dp', 'sp'), may hold values from -6 to 6
- doc_ids: int32 [2, 4, 1024], P(None, 'dp', 'sp'), may hold values from 0 to 7, as said below
- cotangent: bfloat16 [2, 4, 1024, 768], P(None, 'dp', 'sp'), may hold values from -6 to 6
- query_weight: bfloat16 [768, 768], P(('dp', 'sp')), may hold values from -0.21875 to 0.21875
- key_weight: bfloat16 [768, 768], P(('dp', 'sp')), may hold values from -0.21875 to 0.21875
- value_weight: bfloat16 [768, 768], P(('dp', 'sp')), may hold values from -0.21875 to 0.21875
- output_weight: bfloat16 [768, 768], P(('dp', 'sp')), may hold values from -1.25 to 1.25
- query_bias: bfloat16 [768], P(('dp', 'sp')), may hold values from -1.1953125 to 1.1953125
- value_bias: bfloat16 [768], P(('dp', 'sp')), may hold values from -1.796875 to 1.796875
- output_bias: bfloat16 [768], P(('dp', 'sp')), may hold values from -1.796875 to 1.796875
- first_gain: bfloat16 [768], P(('dp', 'sp')), may hold values from 0.5 to 1.5
- first_shift: bfloat16 [768], P(('dp', 'sp')), may hold values from -1.1953125 to 1.1953125
- inner_weight: bfloat16 [768, 3072], P(('dp', 'sp')), may hold values from -0.21875 to 0.21875
- inner_bias: bfloat16 [3072], P(('dp', 'sp')), may hold values from -1.796875 to 1.796875
- outer_weight: bfloat16 [3072, 768], P(('dp', 'sp')), may hold values from -0.21875 to 0.21875
- outer_bias: bfloat16 [768], P(('dp', 'sp')), may hold values from -1.796875 to 1.796875
- second_gain: bfloat16 [768], P(('dp', 'sp')), may hold values from 0.5 to 1.5
- second_shift: bfloat16 [768], P(('dp', 'sp')), may hold values from -1.1953125 to 1.1953125
Outputs:
- outputs: bfloat16 [2, 4, 1024, 768], P(None, 'dp', 'sp')
- tokens_grad: float32 [2, 4, 1024, 768], P(None, 'dp', 'sp')
- query_weight_grad: float32 [768, 768], P(('dp', 'sp'))
- key_weight_grad: float32 [768, 768], P(('dp', 'sp'))
- value_weight_grad: float32 [768, 768], P(('dp', 'sp'))
- output_weight_grad: float32 [768, 768], P(('dp', 'sp'))
- query_bias_grad: float32 [768], P(('dp', 'sp'))
- value_bias_grad: float32 [768], P(('dp', 'sp'))
- output_bias_grad: float32 [768], P(('dp', 'sp'))
- first_gain_grad: float32 [768], P(('dp', 'sp'))
- first_shift_grad: float32 [768], P(('dp', 'sp'))
- inner_weight_grad: float32 [768, 3072], P(('dp', 'sp'))
- inner_bias_grad: float32 [3072], P(('dp', 'sp'))
- outer_weight_grad: float32 [3072, 768], P(('dp', 'sp'))
- outer_bias_grad: float32 [768], P(('dp', 'sp'))
- second_gain_grad: float32 [768], P(('dp', 'sp'))
- second_shift_grad: float32 [768], P(('dp', 'sp'))
The draws below stay inside these ranges and needn't reach their ends.
Inputs may be any that keep to these rules, and one draw needn't show every extreme that they name: `doc_ids`: along each of the 2 x 4 sequences the ids never fall; each sequence begins with id 0 and ends with id 7. For each of the 4 sequence positions of a micro-batch, one of the 2 micro-batches holds a document that begins among the first 128 tokens and ends among the last 128.
All inputs are finite; a program needn't handle non-finite values.
Results may differ from the reference program's by a relative error of at most 0.02.
Values may be sent and summed in bfloat16 or wider, within the bound.
No kernel may reach another device: no remote copies, remote signals or barrier semaphores. Data moves between devices by JAX's collectives and lax.ppermute only.
A program may use at most 384 MiB of HBM per device.

```python
import jax
import jax.numpy as jnp
from jax import lax

D = 768
HEADS = 12
HEAD = 64
FF = 3072
TOK_DEV = 128
MB = 2
SEQS = 4
LEN = 1024


def draw_doc_ids(key, part):
    subkeys = jax.random.split(key, 5)
    top_exponent = max(1, (LEN // 16).bit_length() - 1)
    exponent = jax.random.randint(subkeys[0], (MB, SEQS, 7), 0, top_exponent + 1)
    base_length = jnp.left_shift(jnp.ones_like(exponent), exponent)
    extra_length = jax.random.randint(subkeys[1], (MB, SEQS, 7), 0, 1 << 30) % base_length
    starts = jnp.cumsum(base_length + extra_length, axis=-1)
    position = jnp.arange(LEN, dtype=jnp.int32)
    doc_index = jnp.sum((position[None, None, :, None] >= starts[:, :, None, :]).astype(jnp.int32), axis=-1)
    doc_index = jnp.where(position[None, None, :] == LEN - 1, 7, doc_index)
    span_start = jax.random.randint(subkeys[2], (1, SEQS, 1), 1, max(2, TOK_DEV))
    span_end = jax.random.randint(subkeys[3], (1, SEQS, 1), LEN - TOK_DEV + 1, LEN)
    spanning = jnp.where(position[None, None, :] >= span_end, 7, jnp.where(position[None, None, :] >= span_start, 3, 0))
    chosen = jax.random.randint(subkeys[4], (1, SEQS, 1), 0, MB)
    picked = jnp.arange(MB, dtype=jnp.int32)[:, None, None] == chosen
    return jnp.where(picked, spanning, doc_index).astype(jnp.int32)


def levels(stream_key, shape, shards, smallest, high):
    level = 1.0
    for axis_at, parts in shards:
        draws = jax.random.uniform(jax.random.fold_in(jax.random.fold_in(stream_key, 6), axis_at), (parts,), jnp.float32, smallest / len(shards), high / len(shards))
        level = level * jnp.repeat(jnp.exp(draws), shape[axis_at] // parts).reshape((-1,) + (1,) * (len(shape) - 1 - axis_at))
    return level


def gaussian(rng, shape, deviation, bound, pieces=(), kind=jnp.bfloat16):
    level = levels(rng, shape, pieces, -0.22, 0.18) if pieces else 1.0
    values = jax.random.normal(rng, shape, jnp.float32) * deviation * level
    return jnp.minimum(jnp.maximum(values, -bound), bound).astype(kind)


def setup_inputs(seed: int = 0) -> dict:
    seeds = jax.random.split(jax.random.key(seed), 19)
    return {
        "tokens": gaussian(seeds[0], (MB, SEQS, LEN, D), 1.0, 6.0, ((1, 4), (2, 8))),
        "doc_ids": draw_doc_ids(jax.random.fold_in(seeds[18], 71), 0),
        "cotangent": gaussian(seeds[2], (MB, SEQS, LEN, D), 1.0, 6.0, ((1, 4), (2, 8))),
        "query_weight": gaussian(seeds[3], (D, D), D ** -0.5, 0.21875, ((0, 32),)),
        "key_weight": gaussian(seeds[4], (D, D), D ** -0.5, 0.21875, ((0, 32),)),
        "value_weight": gaussian(seeds[5], (D, D), D ** -0.5, 0.21875, ((0, 32),)),
        "output_weight": gaussian(seeds[6], (D, D), (D // 32) ** -0.5, 1.25, ((0, 32),)),
        "query_bias": gaussian(seeds[7], (D,), 0.2, 1.1953125, ((0, 32),)),
        "value_bias": gaussian(seeds[8], (D,), 0.3, 1.796875, ((0, 32),)),
        "output_bias": gaussian(seeds[9], (D,), 0.3, 1.796875, ((0, 32),)),
        "first_gain": jnp.clip(1.0 + 0.1 * jax.random.normal(seeds[10], (D,), jnp.float32), 0.5, 1.5).astype(jnp.bfloat16),
        "first_shift": gaussian(seeds[11], (D,), 0.2, 1.1953125, ((0, 32),)),
        "inner_weight": gaussian(seeds[12], (D, FF), D ** -0.5, 0.21875, ((0, 32),)),
        "inner_bias": gaussian(seeds[13], (FF,), 0.3, 1.796875, ((0, 32),)),
        "outer_weight": gaussian(seeds[14], (FF, D), (FF // 4) ** -0.5, 0.21875, ((0, 32),)),
        "outer_bias": gaussian(seeds[15], (D,), 0.3, 1.796875, ((0, 32),)),
        "second_gain": jnp.clip(1.0 + 0.1 * jax.random.normal(seeds[16], (D,), jnp.float32), 0.5, 1.5).astype(jnp.bfloat16),
        "second_shift": gaussian(seeds[17], (D,), 0.2, 1.1953125, ((0, 32),)),
    }


EPS = 1e-12
HIGHEST = lax.Precision.HIGHEST

@jax.custom_vjp
def low(v):
    return lax.optimization_barrier(v.astype(jnp.bfloat16)).astype(jnp.float32)

@jax.custom_vjp
def low_back(v):
    return v

def low_keep(v):
    return (low(v), None)

def low_pass(kept, grad):
    return (grad,)

def back_keep(v):
    return (v, None)

def back_low(kept, grad):
    return (low(grad),)
low.defvjp(low_keep, low_pass)
low_back.defvjp(back_keep, back_low)

def product(left_matrix, right_matrix):
    return jnp.dot(left_matrix, right_matrix, precision=HIGHEST, preferred_element_type=jnp.float32)

def layer_norm(summed, gain, shift):
    center = summed - lax.optimization_barrier(jnp.mean(summed, axis=-1, keepdims=True))
    variance = lax.optimization_barrier(jnp.mean(center * center, axis=-1, keepdims=True))
    return center * lax.rsqrt(variance + EPS) * gain + shift

def attend(queries, key_rows, value_rows, segments):
    block_rows = min(512, LEN)
    key_heads = key_rows.reshape(LEN, HEADS, HEAD)
    value_heads = value_rows.reshape(LEN, HEADS, HEAD)
    scaling = HEAD ** (-0.5)

    def block(element):
        query_block, seg_block = element
        scores = jnp.einsum('qhd,khd->hqk', query_block.reshape(block_rows, HEADS, HEAD), key_heads, precision=HIGHEST) * scaling
        scores = low_back(scores)
        same_doc = (seg_block[:, None] == segments[None, :])[None]
        weights = jax.nn.softmax(jnp.where(same_doc, scores, -1e+30), axis=-1)
        context = jnp.einsum('hqk,khd->qhd', low(weights), value_heads, precision=HIGHEST)
        return context.reshape(block_rows, HEADS * HEAD)
    blocks = lax.map(jax.checkpoint(block), (queries.reshape(LEN // block_rows, block_rows, HEADS * HEAD), segments.reshape(LEN // block_rows, block_rows)))
    return blocks.reshape(LEN, HEADS * HEAD)

def sequence(inputs, segments, params):
    w_query, w_key, w_value, w_output, b_query, b_value, b_output, g_first, s_first, w_inner, b_inner, w_outer, b_outer, g_second, s_second = params
    queries = low(low_back(product(inputs, w_query) + b_query))
    key_rows = low(low_back(product(inputs, w_key)))
    value_rows = low(low_back(product(inputs, w_value) + b_value))
    context = low(low_back(attend(queries, key_rows, value_rows, segments)))
    attended = low_back(product(context, w_output) + b_output)
    first_out = layer_norm(inputs + attended, g_first, s_first)
    inner = low_back(product(low(first_out), w_inner) + b_inner)
    active = low(jax.nn.gelu(inner, approximate=False))
    outer = low_back(product(active, w_outer) + b_outer)
    return layer_norm(first_out + outer, g_second, s_second)

def forward(inputs, doc_ids, params):
    flattened = inputs.reshape(MB * SEQS, LEN, D)
    segments = doc_ids.reshape(MB * SEQS, LEN)

    def advance(running, element):
        return (running, sequence(element[0], element[1], params))
    _, stacked = lax.scan(advance, jnp.zeros((), jnp.float32), (flattened, segments))
    return stacked.reshape(MB, SEQS, LEN, D)

def reference(tokens, doc_ids, cotangent, query_weight, key_weight, value_weight, output_weight, query_bias, value_bias, output_bias, first_gain, first_shift, inner_weight, inner_bias, outer_weight, outer_bias, second_gain, second_shift):
    params = tuple((weight.astype(jnp.float32) for weight in (query_weight, key_weight, value_weight, output_weight, query_bias, value_bias, output_bias, first_gain, first_shift, inner_weight, inner_bias, outer_weight, outer_bias, second_gain, second_shift)))
    inputs = tokens.astype(jnp.float32)

    def apply_layer(values_in, weights_in):
        return forward(values_in, doc_ids, weights_in)
    result, pullback = jax.vjp(apply_layer, inputs, params)
    input_grad, weight_grads = pullback(cotangent.astype(jnp.float32))
    return (result.astype(jnp.bfloat16), input_grad, weight_grads[0], weight_grads[1], weight_grads[2], weight_grads[3], weight_grads[4], weight_grads[5], weight_grads[6], weight_grads[7], weight_grads[8], weight_grads[9], weight_grads[10], weight_grads[11], weight_grads[12], weight_grads[13], weight_grads[14])
```

```python
import jax
import jax.numpy as jnp
from jax import lax
from jax.sharding import PartitionSpec as P

HEADS = 12
HEAD = 64


EPS = 1e-12
NEG = -1e30


def product(left_matrix, right_matrix):
    return jnp.dot(left_matrix, right_matrix, preferred_element_type=jnp.float32)


def left_product(left_matrix, right_matrix):
    return lax.dot_general(
        left_matrix, right_matrix, (((0,), (0,)), ((), ())), preferred_element_type=jnp.float32
    )


def right_product(left_matrix, right_matrix):
    return lax.dot_general(
        left_matrix, right_matrix, (((1,), (1,)), ((), ())), preferred_element_type=jnp.float32
    )


def by_heads(matrix):
    return matrix.reshape(matrix.shape[0], HEADS, HEAD)


def norm_forward(summed, gain, shift):
    center = summed - jnp.mean(summed, -1, keepdims=True)
    inverse = lax.rsqrt(jnp.mean(center * center, -1, keepdims=True) + EPS)
    normed = center * inverse
    return (normed * gain + shift, normed, inverse)


def norm_backward(gradient, normed, inverse, gain):
    scaled = gradient * gain
    plain_mean = jnp.mean(scaled, -1, keepdims=True)
    cross_mean = jnp.mean(scaled * normed, -1, keepdims=True)
    return (
        (scaled - plain_mean - normed * cross_mean) * inverse,
        jnp.sum(gradient * normed, 0),
        jnp.sum(gradient, 0),
    )


def attend_forward(queries, key_rows, value_rows, seg_local, seg_all):
    row_count = queries.shape[0]
    scaling = HEAD ** (-0.5)
    query_heads = by_heads(queries)
    key_piece = lax.all_gather(key_rows, "sp", axis=0, tiled=True)
    value_piece = lax.all_gather(value_rows, "sp", axis=0, tiled=True)
    row_peak = jnp.full((HEADS, row_count), NEG, jnp.float32)
    same_doc = (seg_local[:, None] == seg_all[None, :])[None]
    scores = (
        jnp.einsum(
            "qhd,khd->hqk", query_heads, by_heads(key_piece), preferred_element_type=jnp.float32
        )
        * scaling
    )
    scores = jnp.where(same_doc, scores, NEG)
    new_peak = jnp.maximum(row_peak, jnp.max(scores, -1))
    weights = jnp.where(same_doc, jnp.exp(scores - new_peak[..., None]), 0.0)
    row_total = jnp.sum(weights, -1)
    summed = jnp.einsum(
        "hqk,khd->hqd",
        weights.astype(jnp.bfloat16),
        by_heads(value_piece),
        preferred_element_type=jnp.float32,
    )
    return (new_peak, row_total, summed)


def keys_backward(
    queries, key_rows, value_rows, context_grad, log_total, row_delta, seg_local, seg_all
):
    row_count, width = queries.shape
    scaling = HEAD ** (-0.5)
    query_heads = by_heads(queries)
    grad_heads = by_heads(context_grad)
    key_piece = lax.all_gather(key_rows, "sp", axis=0, tiled=True)
    value_piece = lax.all_gather(value_rows, "sp", axis=0, tiled=True)
    piece_rows = key_piece.shape[0]
    key_heads = by_heads(key_piece)
    same_doc = (seg_local[:, None] == seg_all[None, :])[None]
    scores = (
        jnp.einsum("qhd,khd->hqk", query_heads, key_heads, preferred_element_type=jnp.float32)
        * scaling
    )
    weights = jnp.where(same_doc, jnp.exp(scores - log_total[..., None]), 0.0)
    prob_grad = jnp.einsum(
        "qhd,khd->hqk", grad_heads, by_heads(value_piece), preferred_element_type=jnp.float32
    )
    score_grad = (weights * (prob_grad - row_delta[..., None])).astype(jnp.bfloat16)
    query_sum = jnp.einsum(
        "hqk,khd->hqd", score_grad, key_heads, preferred_element_type=jnp.float32
    )
    key_term = jnp.einsum(
        "hqk,qhd->khd", score_grad, query_heads, preferred_element_type=jnp.float32
    ).reshape(piece_rows, width)
    value_term = jnp.einsum(
        "hqk,qhd->khd", weights.astype(jnp.bfloat16), grad_heads, preferred_element_type=jnp.float32
    ).reshape(piece_rows, width)
    pair_sum = jnp.concatenate([key_term, value_term], 1)
    query_sum, pair_sum = (query_sum, pair_sum)
    pair_mine = lax.psum_scatter(pair_sum, "sp", scatter_dimension=0, tiled=True)
    query_sum = jnp.transpose(query_sum, (1, 0, 2)).reshape(row_count, width)
    return (query_sum, pair_mine[:, :width], pair_mine[:, width:])


def body_general(
    tokens,
    doc_ids,
    cotangent,
    query_weight,
    key_weight,
    value_weight,
    output_weight,
    query_bias,
    value_bias,
    output_bias,
    first_gain,
    first_shift,
    inner_weight,
    inner_bias,
    outer_weight,
    outer_bias,
    second_gain,
    second_shift,
):
    shards = (
        query_weight,
        key_weight,
        value_weight,
        output_weight,
        query_bias,
        value_bias,
        output_bias,
        first_gain,
        first_shift,
        inner_weight,
        inner_bias,
        outer_weight,
        outer_bias,
        second_gain,
        second_shift,
    )
    scaling = HEAD ** (-0.5)
    results = []
    input_grads = []
    totals = ()
    for micro in range(tokens.shape[0]):
        loaded = (
            lax.all_gather(shards[0], ("dp", "sp"), axis=0, tiled=True),
            lax.all_gather(shards[1], ("dp", "sp"), axis=0, tiled=True),
            lax.all_gather(shards[2], ("dp", "sp"), axis=0, tiled=True),
            lax.all_gather(shards[3], ("dp", "sp"), axis=0, tiled=True),
            lax.all_gather(shards[4], ("dp", "sp"), axis=0, tiled=True),
            lax.all_gather(shards[5], ("dp", "sp"), axis=0, tiled=True),
            lax.all_gather(shards[6], ("dp", "sp"), axis=0, tiled=True),
            lax.all_gather(shards[7], ("dp", "sp"), axis=0, tiled=True),
            lax.all_gather(shards[8], ("dp", "sp"), axis=0, tiled=True),
            lax.all_gather(shards[9], ("dp", "sp"), axis=0, tiled=True),
            lax.all_gather(shards[10], ("dp", "sp"), axis=0, tiled=True),
            lax.all_gather(shards[11], ("dp", "sp"), axis=0, tiled=True),
            lax.all_gather(shards[12], ("dp", "sp"), axis=0, tiled=True),
            lax.all_gather(shards[13], ("dp", "sp"), axis=0, tiled=True),
            lax.all_gather(shards[14], ("dp", "sp"), axis=0, tiled=True),
        )
        (
            w_query,
            w_key,
            w_value,
            w_output,
            b_query,
            b_value,
            b_output,
            g_first,
            s_first,
            w_inner,
            b_inner,
            w_outer,
            b_outer,
            g_second,
            s_second,
        ) = loaded
        inputs = tokens[micro, 0]
        seg_local = doc_ids[micro, 0]
        seg_all = lax.all_gather(seg_local, "sp", axis=0, tiled=True)
        row_count, width = inputs.shape
        queries = (product(inputs, w_query) + b_query).astype(jnp.bfloat16)
        key_rows = product(inputs, w_key).astype(jnp.bfloat16)
        value_rows = (product(inputs, w_value) + b_value).astype(jnp.bfloat16)
        row_peak, row_total, summed = attend_forward(
            queries, key_rows, value_rows, seg_local, seg_all
        )
        context_heads = summed / row_total[..., None]
        log_total = row_peak + jnp.log(row_total)
        context_low = (
            jnp.transpose(context_heads, (1, 0, 2)).reshape(row_count, width).astype(jnp.bfloat16)
        )
        attended = product(context_low, w_output) + b_output
        first_out, first_normed, first_inverse = norm_forward(
            inputs.astype(jnp.float32) + attended, g_first, s_first
        )
        first_low = first_out.astype(jnp.bfloat16)
        inner = product(first_low, w_inner) + b_inner
        active = jax.nn.gelu(inner, approximate=False).astype(jnp.bfloat16)
        outer = product(active, w_outer) + b_outer
        second_out, second_normed, second_inverse = norm_forward(
            first_out + outer, g_second, s_second
        )
        results.append(second_out.astype(jnp.bfloat16))
        loaded = (
            lax.all_gather(shards[0], ("dp", "sp"), axis=0, tiled=True),
            lax.all_gather(shards[1], ("dp", "sp"), axis=0, tiled=True),
            lax.all_gather(shards[2], ("dp", "sp"), axis=0, tiled=True),
            lax.all_gather(shards[3], ("dp", "sp"), axis=0, tiled=True),
            lax.all_gather(shards[4], ("dp", "sp"), axis=0, tiled=True),
            lax.all_gather(shards[5], ("dp", "sp"), axis=0, tiled=True),
            lax.all_gather(shards[6], ("dp", "sp"), axis=0, tiled=True),
            lax.all_gather(shards[7], ("dp", "sp"), axis=0, tiled=True),
            lax.all_gather(shards[8], ("dp", "sp"), axis=0, tiled=True),
            lax.all_gather(shards[9], ("dp", "sp"), axis=0, tiled=True),
            lax.all_gather(shards[10], ("dp", "sp"), axis=0, tiled=True),
            lax.all_gather(shards[11], ("dp", "sp"), axis=0, tiled=True),
            lax.all_gather(shards[12], ("dp", "sp"), axis=0, tiled=True),
            lax.all_gather(shards[13], ("dp", "sp"), axis=0, tiled=True),
            lax.all_gather(shards[14], ("dp", "sp"), axis=0, tiled=True),
        )
        (
            w_query,
            w_key,
            w_value,
            w_output,
            b_query,
            b_value,
            b_output,
            g_first,
            s_first,
            w_inner,
            b_inner,
            w_outer,
            b_outer,
            g_second,
            s_second,
        ) = loaded
        upstream = cotangent[micro, 0].astype(jnp.float32)
        second_grad, second_gain_grad, second_shift_grad = norm_backward(
            upstream, second_normed, second_inverse, g_second
        )
        outer_grad = second_grad.astype(jnp.bfloat16)
        outer_bias_grad = jnp.sum(outer_grad.astype(jnp.float32), 0)
        outer_weight_grad = left_product(active, outer_grad)
        active_grad = right_product(outer_grad, w_outer)
        _, gelu_pull = jax.vjp(lambda hidden: jax.nn.gelu(hidden, approximate=False), inner)
        inner_grad = gelu_pull(active_grad)[0].astype(jnp.bfloat16)
        inner_bias_grad = jnp.sum(inner_grad.astype(jnp.float32), 0)
        inner_weight_grad = left_product(first_low, inner_grad)
        first_incoming = second_grad + right_product(inner_grad, w_inner)
        first_grad, first_gain_grad, first_shift_grad = norm_backward(
            first_incoming, first_normed, first_inverse, g_first
        )
        attended_grad = first_grad.astype(jnp.bfloat16)
        output_bias_grad = jnp.sum(attended_grad.astype(jnp.float32), 0)
        output_weight_grad = left_product(context_low, attended_grad)
        context_grad = right_product(attended_grad, w_output).astype(jnp.bfloat16)
        row_delta = jnp.sum(jnp.transpose(by_heads(context_grad), (1, 0, 2)) * context_heads, -1)
        query_sum, key_sum, value_sum = keys_backward(
            queries, key_rows, value_rows, context_grad, log_total, row_delta, seg_local, seg_all
        )
        query_grad = (query_sum * scaling).astype(jnp.bfloat16)
        key_grad = (key_sum * scaling).astype(jnp.bfloat16)
        value_grad = value_sum.astype(jnp.bfloat16)
        query_bias_grad = jnp.sum(query_grad.astype(jnp.float32), 0)
        value_bias_grad = jnp.sum(value_grad.astype(jnp.float32), 0)
        query_weight_grad = left_product(inputs, query_grad)
        key_weight_grad = left_product(inputs, key_grad)
        value_weight_grad = left_product(inputs, value_grad)
        input_grads.append(
            first_grad
            + right_product(query_grad, w_query)
            + right_product(key_grad, w_key)
            + right_product(value_grad, w_value)
        )
        terms = (
            query_weight_grad,
            key_weight_grad,
            value_weight_grad,
            output_weight_grad,
            query_bias_grad,
            value_bias_grad,
            output_bias_grad,
            first_gain_grad,
            first_shift_grad,
            inner_weight_grad,
            inner_bias_grad,
            outer_weight_grad,
            outer_bias_grad,
            second_gain_grad,
            second_shift_grad,
        )
        if micro == 0:
            totals = terms
        else:
            totals = tuple((earlier + latest for earlier, latest in zip(totals, terms)))
    owned = lax.psum_scatter(totals, ("dp", "sp"), scatter_dimension=0, tiled=True)
    return (
        jnp.stack(results)[:, None],
        jnp.stack(input_grads)[:, None],
        owned[0],
        owned[1],
        owned[2],
        owned[3],
        owned[4],
        owned[5],
        owned[6],
        owned[7],
        owned[8],
        owned[9],
        owned[10],
        owned[11],
        owned[12],
        owned[13],
        owned[14],
    )


BIT_Y, BIT_X, BIT_ZH, BIT_ZL, BIT_C = 16, 8, 4, 2, 1
AXES = ("dp", "sp")


def swap(array, mask):
    return lax.ppermute(array, AXES, [(i, i ^ mask) for i in range(32)])


def join(bit, own, other, axis=0):
    return jnp.where(
        bit == 0, jnp.concatenate([own, other], axis), jnp.concatenate([other, own], axis)
    )


def halves(array, bit, axis=0):
    size = array.shape[axis] // 2
    low = lax.slice_in_dim(array, 0, size, axis=axis)
    high = lax.slice_in_dim(array, size, 2 * size, axis=axis)
    return (jnp.where(bit == 0, low, high), jnp.where(bit == 0, high, low))


def gather_weight(shard, bits, first, second):
    y, x, zh, zl, c = bits
    keep, give = halves(shard, c, 1)
    block = join(c, keep, swap(give, BIT_C))
    block = join(zl, block, swap(block, BIT_ZL))
    block = join(zh, block, swap(block, BIT_ZH))
    pieces = {0: block, second: swap(block, second), first: swap(block, first)}
    pieces[first | second] = swap(pieces[first], second)
    whole = []
    for mask in (0, BIT_X, BIT_Y, BIT_X | BIT_Y):
        other = swap(pieces[mask], BIT_C)
        whole.append(join(c, pieces[mask], other, 1))
    return join(y, join(x, whole[0], whole[1]), join(x, whole[2], whole[3]))


def low(array):
    return array.astype(jnp.bfloat16)


def add_low(own, other):
    return own.astype(jnp.float32) + other.astype(jnp.float32)


def scatter_weight(grad, bits, first, second):
    y, x, zh, zl, c = bits
    rows, cols = grad.shape
    keep, give = halves(grad, c, 1)
    total = add_low(keep, swap(low(give), BIT_C))
    total = total.reshape(2, 2, rows // 4, cols // 2)
    x_axis = 1
    order = [(first, y), (second, x)] if second == BIT_X else [(first, x), (second, y)]
    near_bit, far_bit = order[0][1], order[1][1]
    if second == BIT_X:
        keep, give = halves(total, x, 1)
        keep, give = keep[:, 0], give[:, 0]
    else:
        keep, give = halves(total, y, 0)
        keep, give = keep[0], give[0]
    keep_near, keep_far = halves(keep, near_bit, 0)
    give_near, give_far = halves(give, near_bit, 0)
    far = add_low(keep_far[0], swap(low(give_far[0]), second))
    near = add_low(keep_near[0], swap(low(give_near[0]), second))
    total = add_low(near, swap(low(far), first))
    for bit, mask in ((zh, BIT_ZH), (zl, BIT_ZL)):
        keep, give = halves(total, bit)
        total = add_low(keep, swap(low(give), mask))
    keep, give = halves(total, c)
    return join(c, keep, swap(low(give), BIT_C).astype(jnp.float32), 1)


def pick(blocks, index):
    return lax.dynamic_index_in_dim(blocks, index, 0, keepdims=False)


def body_fast(
    tokens,
    doc_ids,
    cotangent,
    query_weight,
    key_weight,
    value_weight,
    output_weight,
    query_bias,
    value_bias,
    output_bias,
    first_gain,
    first_shift,
    inner_weight,
    inner_bias,
    outer_weight,
    outer_bias,
    second_gain,
    second_shift,
):
    dp, sp = lax.axis_index("dp"), lax.axis_index("sp")
    bits = (dp // 2, dp % 2, sp // 4, (sp // 2) % 2, sp % 2)
    y, x, zh, zl, c = bits
    group = sp % 4
    scaling = HEAD ** (-0.5)
    width = tokens.shape[-1]
    rows = tokens.shape[2]
    cut = width // 4
    heads = HEADS // 4
    shard_rows = query_weight.shape[0]

    smalls = (
        query_bias, value_bias, output_bias, first_gain, first_shift,
        outer_bias, second_gain, second_shift, inner_bias,
    )
    packed = jnp.concatenate([*smalls, low(doc_ids.reshape(-1))])[None]
    packed = lax.all_gather(packed, AXES, axis=0, tiled=True)
    vectors, at = [], 0
    for small in smalls:
        vectors.append(packed[:, at : at + small.shape[0]].reshape(-1))
        at += small.shape[0]
    b_query, b_value, b_output, g_first, s_first, b_outer, g_second, s_second, b_inner = vectors
    docs = pick(packed[:, at:].reshape(4, 8, 2, rows), dp)[:, :]
    docs = pick(jnp.transpose(docs, (1, 0, 2)), zh)
    order = jnp.array([0, 4, 1, 5, 2, 6, 3, 7]) ^ sp
    docs = jnp.take(docs, order, axis=0).reshape(-1)

    def to_micro(array):
        keep, give = halves(array[:, 0], zh)
        return jnp.concatenate([keep[0], swap(give[0], BIT_ZH)], 0)

    mine = to_micro(tokens)
    second_tokens = swap(mine, BIT_ZL)
    inputs = jnp.concatenate(
        [mine, swap(mine, BIT_C), second_tokens, swap(second_tokens, BIT_C)], 0
    )

    blocks = jnp.stack([query_weight, key_weight, value_weight], 1)
    blocks = jnp.transpose(blocks.reshape(shard_rows, 3, 4, cut), (2, 0, 1, 3))
    blocks = blocks.reshape(4, shard_rows, 3 * cut)
    got = [pick(blocks, group)]
    got += [swap(pick(blocks, group ^ i), i) for i in (1, 2, 3)]
    block = join(zl, join(c, got[0], got[1]), join(c, got[2], got[3]))
    block = join(zh, block, swap(block, BIT_ZH))
    block = join(x, block, swap(block, BIT_X))
    w_attend = join(y, block, swap(block, BIT_Y))

    w_output = gather_weight(output_weight, bits, BIT_Y, BIT_X)
    w_inner = gather_weight(inner_weight, bits, BIT_Y, BIT_X)
    w_outer = gather_weight(outer_weight, bits, BIT_X, BIT_Y)
    upstream = to_micro(cotangent).astype(jnp.float32)

    projected = product(inputs, w_attend)
    b_query_cut = pick(b_query.reshape(4, cut), group)
    b_value_cut = pick(b_value.reshape(4, cut), group)
    queries = low(projected[:, :cut] + b_query_cut)
    keys = low(projected[:, cut : 2 * cut])
    values = low(projected[:, 2 * cut :] + b_value_cut)
    total_rows = inputs.shape[0]
    query_heads = queries.reshape(total_rows, heads, HEAD)
    key_heads = keys.reshape(total_rows, heads, HEAD)
    value_heads = values.reshape(total_rows, heads, HEAD)
    same_doc = (docs[:, None] == docs[None, :])[None]
    scores = jnp.einsum("qhd,khd->hqk", query_heads, key_heads, preferred_element_type=jnp.float32)
    scores = jnp.where(same_doc, scores * scaling, NEG)
    peak = jnp.max(scores, -1, keepdims=True)
    weights = jnp.where(same_doc, jnp.exp(scores - peak), 0.0)
    probs = weights / jnp.sum(weights, -1, keepdims=True)
    context = jnp.einsum(
        "hqk,khd->qhd", low(probs), value_heads, preferred_element_type=jnp.float32
    ).reshape(total_rows, cut)

    def to_rows(array):
        parts = low(array).reshape(4, -1, cut)
        got = [parts[0]] + [swap(parts[i], i) for i in (1, 2, 3)]
        return join(zl, join(c, got[0], got[1], 1), join(c, got[2], got[3], 1), 1)

    def to_heads(array):
        parts = jnp.transpose(array.reshape(-1, 4, cut), (1, 0, 2))
        got = [pick(parts, group)] + [swap(pick(parts, group ^ i), i) for i in (1, 2, 3)]
        return jnp.concatenate(got, 0)

    context_low = to_rows(context)
    attended = product(context_low, w_output) + b_output
    first_out, first_normed, first_inverse = norm_forward(
        mine.astype(jnp.float32) + attended, g_first, s_first
    )
    first_low = low(first_out)
    inner = product(first_low, w_inner) + b_inner
    active = low(jax.nn.gelu(inner, approximate=False))
    outer = product(active, w_outer) + b_outer
    second_out, second_normed, second_inverse = norm_forward(first_out + outer, g_second, s_second)

    def to_place(array):
        own, other = array[:rows], swap(low(array[rows:]), BIT_ZH).astype(array.dtype)
        return join(zh, own[None], other[None])[:, None]

    outputs = to_place(low(second_out))

    second_grad, second_gain_grad, second_shift_grad = norm_backward(
        upstream, second_normed, second_inverse, g_second
    )
    outer_grad = low(second_grad)
    outer_bias_grad = jnp.sum(outer_grad.astype(jnp.float32), 0)
    outer_owned = scatter_weight(left_product(active, outer_grad), bits, BIT_X, BIT_Y)
    active_grad = right_product(outer_grad, w_outer)
    _, gelu_pull = jax.vjp(lambda hidden: jax.nn.gelu(hidden, approximate=False), inner)
    inner_grad = low(gelu_pull(active_grad)[0])
    inner_bias_grad = jnp.sum(inner_grad.astype(jnp.float32), 0)
    inner_owned = scatter_weight(left_product(first_low, inner_grad), bits, BIT_Y, BIT_X)
    first_incoming = second_grad + right_product(inner_grad, w_inner)
    first_grad, first_gain_grad, first_shift_grad = norm_backward(
        first_incoming, first_normed, first_inverse, g_first
    )
    attended_grad = low(first_grad)
    output_bias_grad = jnp.sum(attended_grad.astype(jnp.float32), 0)
    output_owned = scatter_weight(left_product(context_low, attended_grad), bits, BIT_Y, BIT_X)
    context_grad = to_heads(low(right_product(attended_grad, w_output)))
    grad_heads = context_grad.reshape(total_rows, heads, HEAD)
    delta = jnp.sum(
        grad_heads * context.reshape(total_rows, heads, HEAD), -1
    )
    delta = jnp.transpose(delta, (1, 0))[..., None]
    prob_grad = jnp.einsum("qhd,khd->hqk", grad_heads, value_heads, preferred_element_type=jnp.float32)
    score_grad = low(probs * (prob_grad - delta))
    query_grad = low(jnp.einsum(
        "hqk,khd->qhd", score_grad, key_heads, preferred_element_type=jnp.float32
    ) * scaling).reshape(total_rows, cut)
    key_grad = low(jnp.einsum(
        "hqk,qhd->khd", score_grad, query_heads, preferred_element_type=jnp.float32
    ) * scaling).reshape(total_rows, cut)
    value_grad = low(jnp.einsum(
        "hqk,qhd->khd", low(probs), grad_heads, preferred_element_type=jnp.float32
    )).reshape(total_rows, cut)
    grads = jnp.concatenate([query_grad, key_grad, value_grad], 1)
    attend_grad = left_product(inputs, grads)
    total = attend_grad.reshape(2, 2, 2, 4 * shard_rows, 3 * cut)
    for bit, mask in ((x, BIT_X), (y, BIT_Y), (zh, BIT_ZH)):
        axis = {BIT_X: 1, BIT_Y: 0, BIT_ZH: 0}[mask]
        keep, give = halves(total, bit, axis)
        total = jnp.squeeze(add_low(keep, swap(low(give), mask)), axis)
    parts = total.reshape(4, shard_rows, 3 * cut)
    got = [pick(parts, group)] + [
        swap(low(pick(parts, group ^ i)), i).astype(jnp.float32) for i in (1, 2, 3)
    ]
    got = [part.reshape(shard_rows, 3, cut) for part in got]
    attend_owned = join(zl, join(c, got[0], got[1], 2), join(c, got[2], got[3], 2), 2)

    parts = right_product(grads, w_attend).reshape(4, 2 * rows, width)
    near = add_low(parts[0], swap(low(parts[1]), BIT_C))
    far = add_low(parts[2], swap(low(parts[3]), BIT_C))
    input_grad = to_place(first_grad + add_low(near, swap(low(far), BIT_ZL)))

    def spread(vector):
        return lax.dynamic_update_slice(jnp.zeros((width,), jnp.float32), vector, (group * cut,))

    grads_small = grads.astype(jnp.float32)
    vectors = (
        spread(jnp.sum(grads_small[:, :cut], 0)),
        spread(jnp.sum(grads_small[:, 2 * cut :], 0)),
        output_bias_grad,
        first_gain_grad,
        first_shift_grad,
        outer_bias_grad,
        second_gain_grad,
        second_shift_grad,
        inner_bias_grad,
    )
    packed = jnp.concatenate([vector.reshape(32, -1) for vector in vectors], 1)
    for bit, mask in ((y, BIT_Y), (x, BIT_X), (zh, BIT_ZH), (zl, BIT_ZL), (c, BIT_C)):
        keep, give = halves(packed, bit)
        packed = keep + swap(give, mask)
    owned, at = [], 0
    for vector in vectors:
        size = vector.shape[0] // 32
        owned.append(packed[0, at : at + size])
        at += size
    return (
        outputs,
        input_grad,
        attend_owned[:, 0],
        attend_owned[:, 1],
        attend_owned[:, 2],
        output_owned,
        owned[0],
        owned[1],
        owned[2],
        owned[3],
        owned[4],
        inner_owned,
        owned[8],
        outer_owned,
        owned[5],
        owned[6],
        owned[7],
    )


def solution(mesh):
    fast = mesh.shape["dp"] == 4 and mesh.shape["sp"] == 8
    body = body_fast if fast else body_general
    in_specs = (
        P(None, "dp", "sp", None),
        P(None, "dp", "sp"),
        P(None, "dp", "sp", None),
        P(("dp", "sp"), None),
        P(("dp", "sp"), None),
        P(("dp", "sp"), None),
        P(("dp", "sp"), None),
        P(("dp", "sp")),
        P(("dp", "sp")),
        P(("dp", "sp")),
        P(("dp", "sp")),
        P(("dp", "sp")),
        P(("dp", "sp"), None),
        P(("dp", "sp")),
        P(("dp", "sp"), None),
        P(("dp", "sp")),
        P(("dp", "sp")),
        P(("dp", "sp")),
    )
    out_specs = (
        P(None, "dp", "sp", None),
        P(None, "dp", "sp", None),
        P(("dp", "sp"), None),
        P(("dp", "sp"), None),
        P(("dp", "sp"), None),
        P(("dp", "sp"), None),
        P(("dp", "sp")),
        P(("dp", "sp")),
        P(("dp", "sp")),
        P(("dp", "sp")),
        P(("dp", "sp")),
        P(("dp", "sp"), None),
        P(("dp", "sp")),
        P(("dp", "sp"), None),
        P(("dp", "sp")),
        P(("dp", "sp")),
        P(("dp", "sp")),
    )
    return jax.shard_map(body, mesh=mesh, in_specs=in_specs, out_specs=out_specs, check_vma=False)
```

```python
import functools

import jax
import jax.numpy as jnp
from jax import lax
from jax.experimental import pallas as pl
from jax.experimental.pallas import tpu as pltpu
from jax.sharding import PartitionSpec as P

HEADS = 12
HEAD = 64


EPS = 1e-12
NEG = -1e30


def product(left_matrix, right_matrix):
    return jnp.dot(left_matrix, right_matrix, preferred_element_type=jnp.float32)


def left_product(left_matrix, right_matrix):
    return lax.dot_general(
        left_matrix, right_matrix, (((0,), (0,)), ((), ())), preferred_element_type=jnp.float32
    )


def right_product(left_matrix, right_matrix):
    return lax.dot_general(
        left_matrix, right_matrix, (((1,), (1,)), ((), ())), preferred_element_type=jnp.float32
    )


def by_heads(matrix):
    return matrix.reshape(matrix.shape[0], HEADS, HEAD)


def norm_forward(summed, gain, shift):
    center = summed - jnp.mean(summed, -1, keepdims=True)
    inverse = lax.rsqrt(jnp.mean(center * center, -1, keepdims=True) + EPS)
    normed = center * inverse
    return (normed * gain + shift, normed, inverse)


def norm_backward(gradient, normed, inverse, gain):
    scaled = gradient * gain
    plain_mean = jnp.mean(scaled, -1, keepdims=True)
    cross_mean = jnp.mean(scaled * normed, -1, keepdims=True)
    return (
        (scaled - plain_mean - normed * cross_mean) * inverse,
        jnp.sum(gradient * normed, 0),
        jnp.sum(gradient, 0),
    )


def attend_forward(queries, key_rows, value_rows, seg_local, seg_all):
    row_count = queries.shape[0]
    scaling = HEAD ** (-0.5)
    query_heads = by_heads(queries)
    key_piece = lax.all_gather(key_rows, "sp", axis=0, tiled=True)
    value_piece = lax.all_gather(value_rows, "sp", axis=0, tiled=True)
    row_peak = jnp.full((HEADS, row_count), NEG, jnp.float32)
    same_doc = (seg_local[:, None] == seg_all[None, :])[None]
    scores = (
        jnp.einsum(
            "qhd,khd->hqk", query_heads, by_heads(key_piece), preferred_element_type=jnp.float32
        )
        * scaling
    )
    scores = jnp.where(same_doc, scores, NEG)
    new_peak = jnp.maximum(row_peak, jnp.max(scores, -1))
    weights = jnp.where(same_doc, jnp.exp(scores - new_peak[..., None]), 0.0)
    row_total = jnp.sum(weights, -1)
    summed = jnp.einsum(
        "hqk,khd->hqd",
        weights.astype(jnp.bfloat16),
        by_heads(value_piece),
        preferred_element_type=jnp.float32,
    )
    return (new_peak, row_total, summed)


def keys_backward(
    queries, key_rows, value_rows, context_grad, log_total, row_delta, seg_local, seg_all
):
    row_count, width = queries.shape
    scaling = HEAD ** (-0.5)
    query_heads = by_heads(queries)
    grad_heads = by_heads(context_grad)
    key_piece = lax.all_gather(key_rows, "sp", axis=0, tiled=True)
    value_piece = lax.all_gather(value_rows, "sp", axis=0, tiled=True)
    piece_rows = key_piece.shape[0]
    key_heads = by_heads(key_piece)
    same_doc = (seg_local[:, None] == seg_all[None, :])[None]
    scores = (
        jnp.einsum("qhd,khd->hqk", query_heads, key_heads, preferred_element_type=jnp.float32)
        * scaling
    )
    weights = jnp.where(same_doc, jnp.exp(scores - log_total[..., None]), 0.0)
    prob_grad = jnp.einsum(
        "qhd,khd->hqk", grad_heads, by_heads(value_piece), preferred_element_type=jnp.float32
    )
    score_grad = (weights * (prob_grad - row_delta[..., None])).astype(jnp.bfloat16)
    query_sum = jnp.einsum(
        "hqk,khd->hqd", score_grad, key_heads, preferred_element_type=jnp.float32
    )
    key_term = jnp.einsum(
        "hqk,qhd->khd", score_grad, query_heads, preferred_element_type=jnp.float32
    ).reshape(piece_rows, width)
    value_term = jnp.einsum(
        "hqk,qhd->khd", weights.astype(jnp.bfloat16), grad_heads, preferred_element_type=jnp.float32
    ).reshape(piece_rows, width)
    pair_sum = jnp.concatenate([key_term, value_term], 1)
    query_sum, pair_sum = (query_sum, pair_sum)
    pair_mine = lax.psum_scatter(pair_sum, "sp", scatter_dimension=0, tiled=True)
    query_sum = jnp.transpose(query_sum, (1, 0, 2)).reshape(row_count, width)
    return (query_sum, pair_mine[:, :width], pair_mine[:, width:])


def body_general(
    tokens,
    doc_ids,
    cotangent,
    query_weight,
    key_weight,
    value_weight,
    output_weight,
    query_bias,
    value_bias,
    output_bias,
    first_gain,
    first_shift,
    inner_weight,
    inner_bias,
    outer_weight,
    outer_bias,
    second_gain,
    second_shift,
):
    shards = (
        query_weight,
        key_weight,
        value_weight,
        output_weight,
        query_bias,
        value_bias,
        output_bias,
        first_gain,
        first_shift,
        inner_weight,
        inner_bias,
        outer_weight,
        outer_bias,
        second_gain,
        second_shift,
    )
    scaling = HEAD ** (-0.5)
    results = []
    input_grads = []
    totals = ()
    for micro in range(tokens.shape[0]):
        loaded = (
            lax.all_gather(shards[0], ("dp", "sp"), axis=0, tiled=True),
            lax.all_gather(shards[1], ("dp", "sp"), axis=0, tiled=True),
            lax.all_gather(shards[2], ("dp", "sp"), axis=0, tiled=True),
            lax.all_gather(shards[3], ("dp", "sp"), axis=0, tiled=True),
            lax.all_gather(shards[4], ("dp", "sp"), axis=0, tiled=True),
            lax.all_gather(shards[5], ("dp", "sp"), axis=0, tiled=True),
            lax.all_gather(shards[6], ("dp", "sp"), axis=0, tiled=True),
            lax.all_gather(shards[7], ("dp", "sp"), axis=0, tiled=True),
            lax.all_gather(shards[8], ("dp", "sp"), axis=0, tiled=True),
            lax.all_gather(shards[9], ("dp", "sp"), axis=0, tiled=True),
            lax.all_gather(shards[10], ("dp", "sp"), axis=0, tiled=True),
            lax.all_gather(shards[11], ("dp", "sp"), axis=0, tiled=True),
            lax.all_gather(shards[12], ("dp", "sp"), axis=0, tiled=True),
            lax.all_gather(shards[13], ("dp", "sp"), axis=0, tiled=True),
            lax.all_gather(shards[14], ("dp", "sp"), axis=0, tiled=True),
        )
        (
            w_query,
            w_key,
            w_value,
            w_output,
            b_query,
            b_value,
            b_output,
            g_first,
            s_first,
            w_inner,
            b_inner,
            w_outer,
            b_outer,
            g_second,
            s_second,
        ) = loaded
        inputs = tokens[micro, 0]
        seg_local = doc_ids[micro, 0]
        seg_all = lax.all_gather(seg_local, "sp", axis=0, tiled=True)
        row_count, width = inputs.shape
        queries = (product(inputs, w_query) + b_query).astype(jnp.bfloat16)
        key_rows = product(inputs, w_key).astype(jnp.bfloat16)
        value_rows = (product(inputs, w_value) + b_value).astype(jnp.bfloat16)
        row_peak, row_total, summed = attend_forward(
            queries, key_rows, value_rows, seg_local, seg_all
        )
        context_heads = summed / row_total[..., None]
        log_total = row_peak + jnp.log(row_total)
        context_low = (
            jnp.transpose(context_heads, (1, 0, 2)).reshape(row_count, width).astype(jnp.bfloat16)
        )
        attended = product(context_low, w_output) + b_output
        first_out, first_normed, first_inverse = norm_forward(
            inputs.astype(jnp.float32) + attended, g_first, s_first
        )
        first_low = first_out.astype(jnp.bfloat16)
        inner = product(first_low, w_inner) + b_inner
        active = jax.nn.gelu(inner, approximate=False).astype(jnp.bfloat16)
        outer = product(active, w_outer) + b_outer
        second_out, second_normed, second_inverse = norm_forward(
            first_out + outer, g_second, s_second
        )
        results.append(second_out.astype(jnp.bfloat16))
        loaded = (
            lax.all_gather(shards[0], ("dp", "sp"), axis=0, tiled=True),
            lax.all_gather(shards[1], ("dp", "sp"), axis=0, tiled=True),
            lax.all_gather(shards[2], ("dp", "sp"), axis=0, tiled=True),
            lax.all_gather(shards[3], ("dp", "sp"), axis=0, tiled=True),
            lax.all_gather(shards[4], ("dp", "sp"), axis=0, tiled=True),
            lax.all_gather(shards[5], ("dp", "sp"), axis=0, tiled=True),
            lax.all_gather(shards[6], ("dp", "sp"), axis=0, tiled=True),
            lax.all_gather(shards[7], ("dp", "sp"), axis=0, tiled=True),
            lax.all_gather(shards[8], ("dp", "sp"), axis=0, tiled=True),
            lax.all_gather(shards[9], ("dp", "sp"), axis=0, tiled=True),
            lax.all_gather(shards[10], ("dp", "sp"), axis=0, tiled=True),
            lax.all_gather(shards[11], ("dp", "sp"), axis=0, tiled=True),
            lax.all_gather(shards[12], ("dp", "sp"), axis=0, tiled=True),
            lax.all_gather(shards[13], ("dp", "sp"), axis=0, tiled=True),
            lax.all_gather(shards[14], ("dp", "sp"), axis=0, tiled=True),
        )
        (
            w_query,
            w_key,
            w_value,
            w_output,
            b_query,
            b_value,
            b_output,
            g_first,
            s_first,
            w_inner,
            b_inner,
            w_outer,
            b_outer,
            g_second,
            s_second,
        ) = loaded
        upstream = cotangent[micro, 0].astype(jnp.float32)
        second_grad, second_gain_grad, second_shift_grad = norm_backward(
            upstream, second_normed, second_inverse, g_second
        )
        outer_grad = second_grad.astype(jnp.bfloat16)
        outer_bias_grad = jnp.sum(outer_grad.astype(jnp.float32), 0)
        outer_weight_grad = left_product(active, outer_grad)
        active_grad = right_product(outer_grad, w_outer)
        _, gelu_pull = jax.vjp(lambda hidden: jax.nn.gelu(hidden, approximate=False), inner)
        inner_grad = gelu_pull(active_grad)[0].astype(jnp.bfloat16)
        inner_bias_grad = jnp.sum(inner_grad.astype(jnp.float32), 0)
        inner_weight_grad = left_product(first_low, inner_grad)
        first_incoming = second_grad + right_product(inner_grad, w_inner)
        first_grad, first_gain_grad, first_shift_grad = norm_backward(
            first_incoming, first_normed, first_inverse, g_first
        )
        attended_grad = first_grad.astype(jnp.bfloat16)
        output_bias_grad = jnp.sum(attended_grad.astype(jnp.float32), 0)
        output_weight_grad = left_product(context_low, attended_grad)
        context_grad = right_product(attended_grad, w_output).astype(jnp.bfloat16)
        row_delta = jnp.sum(jnp.transpose(by_heads(context_grad), (1, 0, 2)) * context_heads, -1)
        query_sum, key_sum, value_sum = keys_backward(
            queries, key_rows, value_rows, context_grad, log_total, row_delta, seg_local, seg_all
        )
        query_grad = (query_sum * scaling).astype(jnp.bfloat16)
        key_grad = (key_sum * scaling).astype(jnp.bfloat16)
        value_grad = value_sum.astype(jnp.bfloat16)
        query_bias_grad = jnp.sum(query_grad.astype(jnp.float32), 0)
        value_bias_grad = jnp.sum(value_grad.astype(jnp.float32), 0)
        query_weight_grad = left_product(inputs, query_grad)
        key_weight_grad = left_product(inputs, key_grad)
        value_weight_grad = left_product(inputs, value_grad)
        input_grads.append(
            first_grad
            + right_product(query_grad, w_query)
            + right_product(key_grad, w_key)
            + right_product(value_grad, w_value)
        )
        terms = (
            query_weight_grad,
            key_weight_grad,
            value_weight_grad,
            output_weight_grad,
            query_bias_grad,
            value_bias_grad,
            output_bias_grad,
            first_gain_grad,
            first_shift_grad,
            inner_weight_grad,
            inner_bias_grad,
            outer_weight_grad,
            outer_bias_grad,
            second_gain_grad,
            second_shift_grad,
        )
        if micro == 0:
            totals = terms
        else:
            totals = tuple((earlier + latest for earlier, latest in zip(totals, terms)))
    owned = lax.psum_scatter(totals, ("dp", "sp"), scatter_dimension=0, tiled=True)
    return (
        jnp.stack(results)[:, None],
        jnp.stack(input_grads)[:, None],
        owned[0],
        owned[1],
        owned[2],
        owned[3],
        owned[4],
        owned[5],
        owned[6],
        owned[7],
        owned[8],
        owned[9],
        owned[10],
        owned[11],
        owned[12],
        owned[13],
        owned[14],
    )


BIT_Y, BIT_X, BIT_ZH, BIT_ZL, BIT_C = 16, 8, 4, 2, 1
AXES = ("dp", "sp")
GAUSS = 0.3989422804014327
LIMITS = {
    "first": 2, "query": 2, "attend": 16, "forward": 20, "outer_grad": 12, "middle": 20, "inner_grad": 12,
    "attend_back": 20, "attend_weight": 14,
}
SIDE = 64
SCALE = 0.0
DOC_ROWS = 16
BF16, F32 = jnp.bfloat16, jnp.float32


def low(array):
    return array.astype(BF16)


def swap(array, mask):
    return lax.ppermute(array, AXES, [(i, i ^ mask) for i in range(32)])


class Turns:
    def __init__(self):
        self.last = None

    def __call__(self, array):
        if self.last is not None:
            array, _ = lax.optimization_barrier((array, self.last))
        self.last = array
        return array


def tie(array, other):
    return lax.optimization_barrier((array, other))[0]


def join(bit, own, other, axis=0):
    return jnp.where(
        bit == 0, jnp.concatenate([own, other], axis), jnp.concatenate([other, own], axis)
    )


def pair(own, other):
    return jnp.concatenate([own, other], 0)


def add_low(own, other):
    return low(own.astype(F32) + other.astype(F32))


def call(kernel, outs, operands, spaces=None, scratch=(), flops=0, traffic=0, name=None):
    whole = pl.BlockSpec(memory_space=pltpu.VMEM)
    specs = [pl.BlockSpec(memory_space=pltpu.SMEM)]
    operands = list(operands)
    for n, kind in enumerate(spaces or ["vmem"] * (len(operands) - 1), 1):
        specs.append(whole if kind == "vmem" else pl.BlockSpec(memory_space=pltpu.HBM))
        if kind == "hbm":
            operands[n] = pltpu.with_memory_space_constraint(operands[n], pltpu.HBM)
    return pl.pallas_call(
        kernel,
        out_shape=tuple(jax.ShapeDtypeStruct(shape, dtype) for shape, dtype in outs),
        in_specs=specs,
        out_specs=tuple(whole for _ in outs),
        scratch_shapes=list(scratch),
        compiler_params=pltpu.CompilerParams(vmem_limit_bytes=LIMITS[name] * 1024 * 1024),
        cost_estimate=pl.CostEstimate(flops=int(flops * SCALE) + 1, transcendentals=0, bytes_accessed=int(traffic * SCALE) + 1),
        name=name,
    )(*operands)


def block_at(place, k):
    return (place[0] ^ (k // 2)) * 2 + (place[1] ^ (k % 2))


def unit_at(place, u):
    return (place[2] ^ (u // 2)) * 2 + (place[3] ^ (u % 2))


def first_kernel(place, tokens, docs, inner, outer, output, x_keep, x_give, keep, give, ids, sems):
    zh, c = place[2], place[4]
    rows, width = tokens.shape[1:]
    shard, cols = keep.shape[1:]
    started = [pltpu.make_async_copy(docs, ids, sems.at[0])]
    for flip in range(2):
        x_out, out = (x_keep, x_give)[flip], (keep, give)[flip]
        moves = [(tokens.at[zh ^ flip], x_out.at[pl.ds(0, rows), :])]
        half = c ^ flip
        for j in range(4):
            at = pl.ds(pl.multiple_of(half * (4 * cols) + j * cols, 128), cols)
            moves.append((inner.at[:, at], out.at[j]))
        at = pl.ds(pl.multiple_of(half * cols, 128), cols)
        for j in range(4):
            moves.append((outer.at[pl.ds(shard * j, shard), at], out.at[4 + j]))
        moves.append((output.at[:, at], out.at[8]))
        for source, target in moves:
            started.append(pltpu.make_async_copy(source, target, sems.at[len(started)]))
    for copy in started:
        copy.start()
    for copy in started:
        copy.wait()
    for flip, out in ((0, x_keep), (1, x_give)):
        line = ids[pl.ds(zh ^ flip, 1), :].astype(F32)
        line = jnp.concatenate([line, jnp.zeros((1, width - rows), F32)], 1)
        out[rows : rows + DOC_ROWS, :] = low(jnp.broadcast_to(line, (DOC_ROWS, width)))


def query_kernel(place, wq, wk, wv, smalls, q_keep, q_give, weights, blocks, side, sems):
    zl, c = place[3], place[4]
    shard, width = wq.shape
    cut = width // 4
    started = [
        pltpu.make_async_copy(w, weights.at[n], sems.at[n]) for n, w in enumerate((wq, wk, wv))
    ]
    for copy in started:
        copy.start()
    side[...] = jnp.zeros_like(side)
    side[SIDE : SIDE + 16, :] = smalls[...]
    columns = low(jnp.transpose(side[...]))[:shard, SIDE:]
    for copy in started:
        copy.wait()
    for p in range(4):
        at = slice(cut * p, cut * (p + 1))
        blocks[p] = jnp.concatenate([weights[0, :, at], weights[1, :, at], weights[2, :, at], columns], 1)
    for r in range(2):
        q_keep[r] = blocks[2 * (zl ^ r) + c]
        q_give[r] = blocks[2 * (zl ^ r) + (1 - c)]


def attend_kernel(place, w0, w1, w2, w3, x_own, x_other, *refs):
    outs, (w, doc_col) = refs[:-2], refs[-2:]
    context_out, (queries_out, keys_out, values_out, wide_out, lse_out, vec_out, doc_out) = (
        outs[:2], outs[2:],
    )
    cut = queries_out.shape[1]
    heads = cut // HEAD
    size = w0.shape[1]
    for k, part in enumerate((w0, w1, w2, w3)):
        for u in range(4):
            at = block_at(place, k) * (4 * size) + unit_at(place, u) * size
            w[pl.ds(pl.multiple_of(at, 16), size), :] = part[u]
    group = place[5]
    tile = slice(3 * cut - SIDE, 3 * cut + SIDE)
    vec_out[...] = jnp.transpose(w[:, tile].astype(F32))[SIDE : SIDE + 16, :]
    biases = w[pl.ds(pl.multiple_of(group * cut, 64), cut), tile].astype(F32)
    biases = jnp.transpose(jnp.concatenate([biases, jnp.zeros((64, 2 * SIDE), F32)], 0))
    bq, bv = biases[SIDE : SIDE + 1, :cut], biases[SIDE + 1 : SIDE + 2, :cut]
    rows = x_own.shape[1] - DOC_ROWS
    ids = []
    for n in range(8):
        source = (x_own, x_other)[n // 4]
        part = product(source[n % 4, 0:rows, :], w[:, : 3 * cut])
        at = pl.ds(rows * n, rows)
        queries_out[at, :] = low(part[:, :cut] + bq)
        keys_out[at, :] = low(part[:, cut : 2 * cut])
        values_out[at, :] = low(part[:, 2 * cut :] + bv)
        ids.append(source[n % 4, rows : rows + 1, 0:128].astype(F32))
    doc_row = jnp.concatenate(ids, 1)
    doc_out[...] = jnp.broadcast_to(doc_row, doc_out.shape)
    turned = jnp.transpose(jnp.concatenate(ids + [jnp.zeros((120, 128), F32)], 0))
    for n in range(8):
        doc_col[pl.ds(rows * n, rows), :] = jnp.broadcast_to(turned[:, n : n + 1], (rows, 128))
    rows = 2 * rows
    lane = lax.broadcasted_iota(jnp.int32, (rows, 128), 1)
    for i in (2, 3, 0, 1):
        at = pl.ds(rows * i, rows)
        same = doc_col[at, 0:1] == doc_row
        pieces = []
        logs = jnp.zeros((rows, 128), F32)
        for h in range(heads):
            cols = slice(HEAD * h, HEAD * (h + 1))
            query = queries_out[at, cols] * BF16(HEAD**-0.5)
            scores = right_product(query, keys_out[:, cols])
            scores = jnp.where(same, scores, NEG)
            peak = jnp.max(scores, -1, keepdims=True)
            weights = jnp.exp(scores - peak)
            denom = jnp.sum(weights, -1, keepdims=True)
            summed = product(low(weights), values_out[:, cols])
            pieces.append(summed / denom)
            logs = jnp.where(lane == h, peak + jnp.log(denom), logs)
        context = jnp.concatenate(pieces, 1)
        wide_out[at, :] = context
        context_out[i // 2][i % 2] = low(context)
        lse_out[:, at] = jnp.transpose(logs)[:8, :]


def attend_back_kernel(
    place, q, k, v, wide, lse, g0, g1, g2, g3, docs, grads, sums, dq_acc, delta_ref, dc, doc_col
):
    total, cut = q.shape
    heads = cut // HEAD
    rows = total // 4
    scaling = HEAD**-0.5
    lane = lax.broadcasted_iota(jnp.int32, (rows, 128), 1)
    doc_row = docs[0:1, :]
    for n in range(total // 128):
        at = slice(128 * n, 128 * (n + 1))
        turned = jnp.transpose(jnp.broadcast_to(docs[0:1, at], (128, 128)))
        doc_col[at, :] = turned
    for i, g in enumerate((g0, g1, g2, g3)):
        at = pl.ds(rows * i, rows)
        grad = g[...]
        dc[at, :] = grad
        prod = grad.astype(F32) * wide[at, :]
        cols = jnp.zeros((rows, 128), F32)
        for h in range(heads):
            piece = jnp.sum(prod[:, HEAD * h : HEAD * (h + 1)], -1, keepdims=True)
            cols = jnp.where(lane == h, piece, cols)
        delta_ref[:, at] = jnp.transpose(cols)[:8, :]
    for h in range(heads):
        cols = slice(HEAD * h, HEAD * (h + 1))
        query = q[:, cols]
        scaled = query * BF16(scaling)
        grad_rows = dc[:, cols]
        for i in range(4):
            at = pl.ds(rows * i, rows)
            key = k[at, cols]
            value = v[at, cols]
            same = doc_col[at, 0:1] == doc_row
            scores = jnp.where(same, right_product(key, scaled), NEG)
            probs = jnp.exp(scores - lse[h : h + 1, :])
            prob_grad = right_product(value, grad_rows)
            score_grad = low(probs * (prob_grad - delta_ref[h : h + 1, :]))
            grads[at, cut + HEAD * h : cut + HEAD * (h + 1)] = low(product(score_grad, query) * scaling)
            grads[at, 2 * cut + HEAD * h : 2 * cut + HEAD * (h + 1)] = low(product(low(probs), grad_rows))
            piece = left_product(key, score_grad)
            if i == 0:
                dq_acc[...] = piece
            else:
                dq_acc[...] += piece
        grads[:, cols] = low(jnp.transpose(dq_acc[...]) * scaling)
    grads[:, 3 * cut :] = jnp.zeros((total, SIDE), BF16)
    sums[0:1, :] = jnp.sum(grads[...].astype(F32), 0, keepdims=True)


def attend_weight_kernel(order, place, x_own, x_other, grads, w0, w1, w2, w3, sums, extra, *refs):
    outs, input_outs, (turned, w, side) = refs[:4], refs[4:7], refs[7:]
    rows = x_own.shape[1] - DOC_ROWS
    group = place[5]
    cut = extra.shape[1] // 4
    for n in range(8):
        source = (x_own, x_other)[n // 4]
        turned[:, pl.ds(rows * n, rows)] = jnp.transpose(source[n % 4, 0:rows, :])
    size = w0.shape[1]
    for k, part in enumerate((w0, w1, w2, w3)):
        for u in range(4):
            at = block_at(place, k) * (4 * size) + unit_at(place, u) * size
            w[pl.ds(pl.multiple_of(at, 16), size), :] = part[u]
    width = extra.shape[1]
    pad = jnp.concatenate([jnp.zeros((SIDE + 2, width), F32), extra[...], jnp.zeros((SIDE - 18, width), F32)], 0)
    side[...] = jnp.transpose(pad)
    own = jnp.concatenate([sums[0:1, :cut], sums[0:1, 2 * cut : 3 * cut]], 0)
    own = jnp.concatenate([own, jnp.zeros((2, 256 - cut), F32)], 1)
    own = jnp.concatenate([jnp.zeros((SIDE, 256), F32), own, jnp.zeros((SIDE - 2, 256), F32)], 0)
    at = pl.ds(pl.multiple_of(group * cut, 64), cut)
    side[at, :] += jnp.transpose(own)[:cut, :]
    for n, k in enumerate(order):
        at = pl.ds(pl.multiple_of(block_at(place, k) * (4 * size), 64), 4 * size)
        piece = product(turned[at, :], grads[...])
        piece = jnp.concatenate([piece[:, : 3 * cut - SIDE], piece[:, 3 * cut - SIDE :] + side[at, :]], 1)
        for a in range(4):
            outs[n][unit_at(place, a)] = low(piece[size * a : size * (a + 1), :])
    for n in (2, 3, 1, 0):
        at = pl.ds(2 * rows * n, 2 * rows)
        part = right_product(grads[at, : 3 * cut], w[:, : 3 * cut])
        if n == 0:
            input_outs[0][...] = part
        elif n == 1:
            input_outs[1][...] = low(part)
        else:
            input_outs[2][n - 2] = low(part)


def copies(pieces, whole, place, sems, base, column_blocks, first, row_count):
    c = place[4]
    started = []
    for half in range(2):
        for k in range(4):
            for u in range(4):
                for j in range(column_blocks):
                    source = pieces[half * 4 + k]
                    cols = source.shape[-1]
                    row = block_at(place, k) * (4 * row_count) + unit_at(place, u) * row_count
                    col = (c ^ half) * (column_blocks * cols) + j * cols
                    target = whole.at[
                        pl.ds(pl.multiple_of(row, 16), row_count), pl.ds(pl.multiple_of(col, 128), cols)
                    ]
                    if column_blocks > 1:
                        source = source.at[u, j]
                    else:
                        source = source.at[u, pl.ds(first, row_count), :]
                    started.append(pltpu.make_async_copy(source, target, sems.at[base + len(started)]))
    return started


def forward_kernel(place, c0, c1, c2, c3, x_ref, vec, b_inner, *refs):
    a_p, b_p = refs[:8], refs[8:16]
    (out, n2_out, r2_out, h1b_out, n1_out, r1_out, g_out, gp_out) = refs[16:24]
    wo, wi, wu, sems = refs[24:]
    unit = wo.shape[0] // 16
    copy_o = copies(b_p, wo, place, sems, 0, 1, 4 * unit, unit)
    copy_i = copies(a_p, wi, place, sems, 32, 4, 0, unit)
    copy_u = copies(b_p, wu, place, sems, 160, 1, 0, 4 * unit)
    for copy in copy_o + copy_i + copy_u:
        copy.start()
    group = place[5]
    rows = x_ref.shape[1] - DOC_ROWS
    cut = c0.shape[-1]
    for copy in copy_o:
        copy.wait()
    attended = vec[2:3, :]
    for mask, part in enumerate((c0, c1, c2, c3)):
        at = pl.ds(pl.multiple_of((group ^ mask) * cut, 64), cut)
        attended = attended + product(part[...], wo[at, :])
    tokens = jnp.concatenate([x_ref[0, 0:rows, :], x_ref[1, 0:rows, :]], 0)
    first_out, normed, inverse = norm_forward(tokens.astype(F32) + attended, vec[3:4, :], vec[4:5, :])
    n1_out[...] = normed
    r1_out[...] = jnp.broadcast_to(inverse, r1_out.shape)
    h1b_out[...] = low(first_out)
    for copy in copy_i + copy_u:
        copy.wait()
    outer = vec[5:6, :]
    step = 512
    for j in range(wi.shape[1] // step):
        at = slice(step * j, step * (j + 1))
        hidden = product(h1b_out[...], wi[:, at]) + b_inner[:, at]
        half = 0.5 + 0.5 * lax.erf(hidden * (0.5**0.5))
        active = low(hidden * half)
        g_out[:, at] = active
        gp_out[:, at] = half + hidden * jnp.exp(hidden * hidden * -0.5) * GAUSS
        outer = outer + product(active, wu[at, :])
    second_out, normed, inverse = norm_forward(first_out + outer, vec[6:7, :], vec[7:8, :])
    out[...] = low(second_out)
    n2_out[...] = normed
    r2_out[...] = jnp.broadcast_to(inverse, r2_out.shape)


def outer_grad_kernel(
    place, cot_own, cot_other, n2, r2, vec, g_ref, give, keep, dz2_out, df_ref, sums
):
    c = place[4]
    upstream = jnp.concatenate([cot_own[...], cot_other[...]], 0).astype(F32)
    grad, gain_grad, shift_grad = norm_backward(upstream, n2[...], r2[:, 0:1], vec[6:7, :])
    dz2_out[...] = grad
    grad_low = low(grad)
    df_ref[...] = grad_low
    sums[0:1, :] = gain_grad[None]
    sums[1:2, :] = shift_grad[None]
    sums[2:3, :] = jnp.sum(grad_low.astype(F32), 0, keepdims=True)
    unit, cols = give.shape[2:]
    give_part = df_ref[:, pl.ds(pl.multiple_of((1 - c) * cols, 128), cols)]
    keep_part = df_ref[:, pl.ds(pl.multiple_of(c * cols, 128), cols)]
    both = jnp.concatenate([give_part, keep_part], 1)
    for k in range(4):
        at = pl.ds(pl.multiple_of(block_at(place, k) * (4 * unit), 128), 4 * unit)
        piece = low(left_product(g_ref[:, at], both))
        for a in range(4):
            at = slice(unit * a, unit * (a + 1))
            give[k, unit_at(place, a)] = piece[at, :cols]
            keep[k, unit_at(place, a)] = piece[at, cols:]


def middle_kernel(place, df_ref, gp_ref, dz2, n1, r1, vec, *refs):
    a_p, b_p = refs[:8], refs[8:16]
    du, grad_out, da, dc0, dc1, dc_give, sums, sums_b = refs[16:24]
    wo, wi, wu, sems = refs[24:]
    unit = wo.shape[0] // 16
    copy_o = copies(b_p, wo, place, sems, 0, 1, 4 * unit, unit)
    copy_i = copies(a_p, wi, place, sems, 32, 4, 0, unit)
    copy_u = copies(b_p, wu, place, sems, 160, 1, 0, 4 * unit)
    for copy in copy_u + copy_i + copy_o:
        copy.start()
    group = place[5]
    for copy in copy_u + copy_i:
        copy.wait()
    step = 512
    incoming = dz2[...]
    for j in range(wu.shape[0] // step):
        at = slice(step * j, step * (j + 1))
        grad = low(right_product(df_ref[...], wu[at, :]) * gp_ref[:, at])
        du[:, at] = grad
        sums_b[0:1, at] = jnp.sum(grad.astype(F32), 0, keepdims=True)
        incoming = incoming + right_product(grad, wi[:, at])
    for copy in copy_o:
        copy.wait()
    grad, gain_grad, shift_grad = norm_backward(incoming, n1[...], r1[:, 0:1], vec[3:4, :])
    grad_out[...] = grad
    grad_low = low(grad)
    da[...] = grad_low
    sums[0:1, :] = gain_grad[None]
    sums[1:2, :] = shift_grad[None]
    sums[2:3, :] = jnp.sum(grad_low.astype(F32), 0, keepdims=True)
    cut = dc0.shape[1]
    for mask in (1, 3, 0, 2):
        at = pl.ds(pl.multiple_of((group ^ mask) * cut, 64), cut)
        part = low(right_product(grad_low, wo[at, :]))
        if mask % 2:
            dc_give[mask // 2] = part
        else:
            (dc0, dc1)[mask // 2][...] = part


def inner_grad_kernel(place, h1b_ref, du, da, c0, c1, c2, c3, give, keep, turned, cs):
    c, group = place[4], place[5]
    turned[...] = jnp.transpose(h1b_ref[...])
    for mask, part in enumerate((c0, c1, c2, c3)):
        cs[mask] = part[...]
    unit, cols = give.shape[2] // 5, give.shape[3]
    blocks = 5
    wide = (blocks - 1) * cols
    for half in range(2):
        side = c ^ 1 ^ half
        right = du[:, pl.ds(pl.multiple_of(side * wide, 128), wide)]
        right_low = da[:, pl.ds(pl.multiple_of(side * cols, 128), cols)]
        for k in range(4):
            block = block_at(place, k)
            at = pl.ds(pl.multiple_of(block * (4 * unit), 64), 4 * unit)
            piece = low(product(turned[at, :], right))
            tail = low(left_product(cs[block ^ group], right_low))
            for a in range(4):
                u = unit_at(place, a)
                rows = slice(unit * a, unit * (a + 1))
                for j in range(blocks):
                    part = piece[rows, cols * j : cols * (j + 1)] if j < blocks - 1 else tail[rows, :]
                    (give, keep)[half][k, u, unit * j : unit * (j + 1), :] = part


def body_fast(
    tokens,
    doc_ids,
    cotangent,
    query_weight,
    key_weight,
    value_weight,
    output_weight,
    query_bias,
    value_bias,
    output_bias,
    first_gain,
    first_shift,
    inner_weight,
    inner_bias,
    outer_weight,
    outer_bias,
    second_gain,
    second_shift,
):
    dp, sp = lax.axis_index("dp"), lax.axis_index("sp")
    y, x, zh, zl, c = dp // 2, dp % 2, sp // 4, (sp // 2) % 2, sp % 2
    place = jnp.stack([y, x, zh, zl, c, sp % 4]).astype(jnp.int32)
    width, hidden, rows = tokens.shape[-1], inner_weight.shape[1], tokens.shape[2]
    cut, shard = width // 4, query_weight.shape[0]
    unit = 2 * shard
    wide = 3 * cut + SIDE
    own, total = 2 * rows, 8 * rows
    turn = Turns()

    x_rows = rows + DOC_ROWS
    cols = hidden // 8
    x_keep, x_give, w_keep, w_give = call(
        first_kernel,
        [((x_rows, width), BF16)] * 2 + [((9, shard, cols), BF16)] * 2,
        [place, tokens[:, 0], doc_ids[:, 0], inner_weight, outer_weight, output_weight],
        ["hbm"] * 5,
        scratch=[pltpu.VMEM((2, rows), jnp.int32), pltpu.SemaphoreType.DMA((24,))],
        name="first",
    )
    from_xzh = swap(x_give, BIT_ZH)
    got = turn(swap(w_give, BIT_C))

    def zl_half(array):
        half = array.shape[1] // 2
        return lax.dynamic_slice_in_dim(array, zl * half, half, 1)

    def far_pair(own_half, other_half):
        turned = pair(other_half[1:], other_half[:1])
        return join(zl, own_half, turned, 1)

    a_unit = join(c, w_keep[:4], got[:4], 1)
    b_unit = jnp.concatenate(
        [
            join(c, w_keep[4:8].reshape(4 * shard, cols), got[4:8].reshape(4 * shard, cols)),
            join(c, w_keep[8], got[8]),
        ]
    )
    from_a2 = swap(a_unit[None], BIT_ZL)

    a_pair = pair(a_unit[None], turn(from_a2))
    from_a4 = swap(zl_half(a_pair), BIT_ZH)
    from_b2 = swap(tie(b_unit, a_pair)[None], BIT_ZL)
    smalls = [
        query_bias, value_bias, output_bias, first_gain, first_shift,
        outer_bias, second_gain, second_shift,
    ] + [inner_bias[shard * q : shard * (q + 1)] for q in range(4)]
    smalls = list(lax.optimization_barrier((*smalls, a_pair))[:-1])
    row = lax.broadcasted_iota(jnp.int32, (16, 128), 0)
    packed = jnp.zeros((16, 128), F32)
    for n, small in enumerate(smalls):
        wide_small = jnp.pad(small.astype(F32), (0, 128 - shard))
        packed = jnp.where(row == n, wide_small[None], packed)
    q_keep, q_give = call(
        query_kernel,
        [((2, shard, wide), BF16)] * 2,
        [place, tie(query_weight, a_pair), key_weight, value_weight, packed],
        ["hbm"] * 3 + ["vmem"],
        scratch=[
            pltpu.VMEM((3, shard, width), BF16),
            pltpu.VMEM((4, shard, wide), BF16),
            pltpu.VMEM((128, 128), F32),
            pltpu.SemaphoreType.DMA((3,)),
        ],
        name="query",
    )
    from_qc = swap(turn(q_give), BIT_C)
    b_pair = pair(b_unit[None], turn(from_b2))
    q_unit = join(c, q_keep, turn(from_qc), 1)
    from_qzl = swap(q_unit[1], BIT_ZL)
    mine = jnp.stack([x_keep, turn(from_xzh)])
    a_half = turn(from_a4)
    from_a5 = swap(a_half, BIT_ZL)
    from_b4 = swap(zl_half(tie(b_pair, a_half)), BIT_ZH)
    q_pair = jnp.stack([q_unit[0], turn(from_qzl)])
    a_own = pair(a_pair, far_pair(a_half, turn(from_a5)))
    from_ax = swap(a_own, BIT_X)
    from_ay = swap(a_own, BIT_Y)
    from_xzl = swap(tie(mine, a_own), BIT_ZL)
    b_half = turn(from_b4)
    from_b5 = swap(b_half, BIT_ZL)
    from_qzh = swap(tie(q_pair, b_half), BIT_ZH)
    a_y = turn(from_ay)
    a_x = turn(from_ax)
    b_own = pair(b_pair, far_pair(b_half, turn(from_b5)))
    x_own = pair(mine, turn(from_xzl))
    from_xc = swap(x_own, BIT_C)
    q_own = pair(q_pair, turn(from_qzh))
    from_qy = swap(tie(q_own, a_y), BIT_Y)
    from_qx = swap(tie(q_own, a_x), BIT_X)
    x_other = turn(from_xc)
    from_a0c = swap(tie(a_own, x_other), BIT_C)
    q_y = turn(from_qy)
    from_qxy = swap(q_y, BIT_X)
    from_by = swap(tie(b_own, q_y), BIT_Y)
    q_x = turn(from_qx)
    a_c = [turn(from_a0c)]
    from_a1c = swap(tie(a_x, a_c[0]), BIT_C)
    a_c.append(turn(from_a1c))
    q_xy = turn(from_qxy)
    from_bx = swap(tie(b_own, q_xy), BIT_X)
    w_attend = [q_own, q_x, q_y, q_xy]

    results = call(
        attend_kernel,
        [((2, own, cut), BF16)] * 2
        + [((total, cut), BF16)] * 3
        + [((total, cut), F32), ((8, total), F32), ((16, width), F32), ((8, total), F32)],
        [place, *w_attend, x_own, x_other],
        scratch=[pltpu.VMEM((width, wide), BF16), pltpu.VMEM((total, 128), F32)],
        flops=2 * total * width * 3 * cut + 4 * total * total * cut * 4,
        traffic=8 * total * width,
        name="attend",
    )
    context_keep, context_give, queries, keys, values, context_wide, lse, vec, docs = results
    context_give = turn(context_give)
    b_y = turn(from_by)
    b_x = turn(from_bx)
    from_axy = swap(tie(a_y, b_x), BIT_X)
    from_bxy = swap(tie(b_x, b_y), BIT_Y)
    from_cc = swap(tie(context_give, b_x), BIT_C)
    from_a2c = swap(tie(a_y, b_x), BIT_C)
    got = turn(from_cc)
    from_czl = swap(pair(context_keep[1:], got[1:]), BIT_ZL)
    context = [context_keep[0], got[0]]
    a_c.append(turn(from_a2c))
    from_b0c = swap(tie(b_own, a_c[2]), BIT_C)
    b_c = [turn(from_b0c)]
    from_b1c = swap(tie(b_x, b_c[0]), BIT_C)
    got = turn(from_czl)
    context += [got[0], got[1]]
    b_c.append(turn(from_b1c))
    from_b2c = swap(tie(b_y, b_c[1]), BIT_C)
    b_inner = jnp.transpose(tie(vec, b_c[1])[8:12].reshape(4, 32, shard), (1, 0, 2)).reshape(1, hidden)
    b_inner = turn(b_inner)
    cot_keep = lax.dynamic_index_in_dim(cotangent[:, 0], zh, 0, False)
    cot_give = turn(lax.dynamic_index_in_dim(cotangent[:, 0], 1 - zh, 0, False))
    from_cot = swap(cot_give, BIT_ZH)
    b_c.append(turn(from_b2c))
    a_xy = turn(from_axy)
    from_a3c = swap(a_xy, BIT_C)
    b_xy = turn(from_bxy)
    from_b3c = swap(b_xy, BIT_C)
    a_c.append(turn(from_a3c))
    b_c.append(turn(from_b3c))
    a_pieces = [a_own, a_x, a_y, a_xy, *a_c]
    b_pieces = [b_own, b_x, b_y, b_xy, *b_c]

    whole = [
        pltpu.VMEM((width, width), BF16),
        pltpu.VMEM((width, hidden), BF16),
        pltpu.VMEM((hidden, width), BF16),
        pltpu.SemaphoreType.DMA((192,)),
    ]
    results = call(
        forward_kernel,
        [
            ((own, width), BF16), ((own, width), F32), ((own, 128), F32), ((own, width), BF16),
            ((own, width), F32), ((own, 128), F32), ((own, hidden), BF16), ((own, hidden), F32),
        ],
        [place, *context, mine, turn(vec), b_inner, *a_pieces, *b_pieces],
        ["vmem"] * 7 + ["hbm"] * 16,
        whole,
        flops=4 * own * width * hidden * 2,
        traffic=4 * width * hidden * 2,
        name="forward",
    )
    second_out, second_normed, second_inverse, first_low, normed, inverse, active, slope = results
    second_normed = turn(second_normed)

    def to_place(kept, other):
        return join(zh, kept[None], other[None].astype(kept.dtype))[:, None]

    def split(both):
        half = both.shape[2] // 2
        return both[:, :, :half], both[:, :, half:]

    def first_hop(both):
        left, right = split(both)
        return swap(jnp.stack([left[1], left[3]]), BIT_X), swap(right[2:], BIT_Y)

    def second_hop(both, from_x, from_y):
        left, right = split(both)
        return (
            (add_low(left[0], from_x[0]), add_low(right[0], from_y[0])),
            swap(add_low(left[2], from_x[1]), BIT_Y),
            swap(add_low(right[1], from_y[1]), BIT_X),
        )

    def last_hop(owns, from_y, from_x):
        return jnp.concatenate([add_low(owns[0], from_y), add_low(owns[1], from_x)], 1)

    def zl_halves(array):
        half = array.shape[1] // 2
        one, two = array[:, :half], array[:, half:]
        return jnp.where(zl == 0, one, two), jnp.where(zl == 0, two, one)

    cot_other = turn(from_cot)
    b_shape, a_shape = ((4, 4, 4 * unit, cols), BF16), ((4, 4, 5 * unit, cols), BF16)
    b_give, b_keep, second_grad, outer_grad, sums_a = call(
        outer_grad_kernel,
        [b_shape, b_shape, ((own, width), F32), ((own, width), BF16), ((8, width), F32)],
        [place, cot_keep, cot_other, second_normed, second_inverse, vec, active],
        name="outer_grad",
    )
    b_all = add_low(b_keep, turn(swap(b_give, BIT_C)))
    from_bx1, from_by1 = first_hop(b_all)
    outer_grad = tie(outer_grad, b_all)
    results = call(
        middle_kernel,
        [
            ((own, hidden), BF16), ((own, width), F32), ((own, width), BF16), ((own, cut), BF16),
            ((own, cut), BF16), ((2, own, cut), BF16), ((8, width), F32), ((8, hidden), F32),
        ],
        [place, outer_grad, slope, second_grad, normed, inverse, vec, *a_pieces, *b_pieces],
        ["vmem"] * 6 + ["hbm"] * 16,
        whole,
        flops=4 * own * width * hidden,
        traffic=6 * width * hidden,
        name="middle",
    )
    inner_grad, first_grad, attended_grad, dc_own, dc_zl, dc_give, sums_c, sums_b = results
    a_give, a_keep = call(
        inner_grad_kernel,
        [a_shape, a_shape],
        [place, first_low, turn(inner_grad), attended_grad, *context],
        scratch=[pltpu.VMEM((width, own), BF16), pltpu.VMEM((4, own, cut), BF16)],
        name="inner_grad",
    )
    from_agive = swap(turn(a_give), BIT_C)
    from_dcc = swap(dc_give, BIT_C)
    got_x, got_y = turn(from_bx1), turn(from_by1)
    b_owns, from_by2, from_bx2 = second_hop(b_all, got_x, got_y)
    got = turn(from_dcc)
    dc_c = got[0]
    from_dczl = swap(jnp.stack([dc_zl, got[1]]), BIT_ZL)
    a_all = add_low(a_keep, turn(from_agive))
    from_ax1, from_ay1 = first_hop(a_all)
    b_own = last_hop(b_owns, turn(from_by2), turn(from_bx2))
    from_bzh = swap(b_own[2:], BIT_ZH)
    got = turn(from_dczl)
    dc = [tie(dc_own, b_own), got[0], dc_c, got[1]]
    grads, sums_d = call(
        attend_back_kernel,
        [((total, wide), BF16), ((8, wide), F32)],
        [place, queries, keys, values, context_wide, lse, *dc, docs],
        scratch=[
            pltpu.VMEM((HEAD, total), F32),
            pltpu.VMEM((8, total), F32),
            pltpu.VMEM((total, cut), BF16),
            pltpu.VMEM((total, 128), F32),
        ],
        flops=10 * total * total * cut * 4,
        traffic=8 * total * width,
        name="attend_back",
    )
    grads = turn(grads)
    from_out = swap(tie(second_out[rows:], grads), BIT_ZH)
    extra = jnp.concatenate(
        [
            sums_c[2:3], sums_c[0:2], sums_a[2:3], sums_a[0:2],
            jnp.transpose(sums_b[0].reshape(32, 4, shard), (1, 0, 2)).reshape(4, width),
            jnp.zeros((6, width), F32),
        ]
    )
    results = call(
        functools.partial(attend_weight_kernel, (3, 2, 1, 0)),
        [((4, unit, wide), BF16)] * 4 + [((own, width), F32), ((own, width), BF16), ((2, own, width), BF16)],
        [place, x_own, x_other, grads, *w_attend, sums_d, extra],
        scratch=[
            pltpu.VMEM((width, total), BF16),
            pltpu.VMEM((width, wide), BF16),
            pltpu.VMEM((width, 128), F32),
        ],
        flops=4 * total * width * 3 * cut,
        traffic=8 * total * width,
        name="attend_weight",
    )
    q_parts, (x_part, x_zl, x_give) = results[:4], results[4:]
    from_xgive = swap(turn(x_give), BIT_C)
    b_own = add_low(b_own[:2], turn(from_bzh))
    from_bzl = swap(b_own[1], BIT_ZL)
    got_x, got_y = turn(from_ax1), turn(from_ay1)
    a_owns, from_ay2, from_ax2 = second_hop(a_all, got_x, got_y)
    got = turn(from_xgive)
    x_zl = add_low(x_zl, got[1])
    x_part = x_part + got[0].astype(F32)
    from_xzl = swap(x_zl, BIT_ZL)
    outputs = to_place(second_out[:rows], turn(from_out))
    def core_halves(array, axis):
        half = array.shape[axis] // 2
        first_half = lax.slice_in_dim(array, 0, half, axis=axis)
        last_half = lax.slice_in_dim(array, half, 2 * half, axis=axis)
        return jnp.where(c == 0, first_half, last_half), jnp.where(c == 0, last_half, first_half)

    b_mine, b_theirs = core_halves(b_own[0].astype(F32) + turn(from_bzl).astype(F32), 0)
    from_bc = swap(low(b_theirs), BIT_C)
    a_own = last_hop(a_owns, turn(from_ay2), turn(from_ax2))
    a_halves = zl_halves(a_own[2:])
    from_az1 = swap(a_halves[1][::-1], BIT_ZL)
    from_q1 = swap(tie(q_parts[0], a_own), BIT_X)
    from_q2 = swap(tie(q_parts[2], a_own), BIT_X)
    a_far = add_low(a_halves[0], turn(from_az1))
    from_az2 = swap(a_far, BIT_ZH)
    x_grad = first_grad + (x_part + turn(from_xzl).astype(F32))
    outer_owned = join(c, b_mine, turn(from_bc).astype(F32), 1)
    q_far = add_low(q_parts[1], turn(from_q1))
    from_q3 = swap(q_far, BIT_Y)
    q_own = add_low(q_parts[3], turn(from_q2))
    q_own = add_low(q_own, turn(from_q3))
    from_qzh = swap(q_own[2:], BIT_ZH)
    got = turn(from_az2)
    empty = jnp.zeros_like(got)
    a_own = add_low(a_own[:2], join(zl, got, empty, 1))
    from_azl = swap(a_own[1], BIT_ZL)
    from_xzh = swap(low(tie(x_grad, a_own)[rows:]), BIT_ZH)
    q_own = add_low(q_own[:2], turn(from_qzh))
    from_qzl = swap(q_own[1], BIT_ZL)
    a_last = (a_own[0].astype(F32) + turn(from_azl).astype(F32)).reshape(5, unit, cols)
    a_mine, a_theirs = core_halves(a_last, 1)
    from_ac = swap(low(a_theirs), BIT_C)
    q_two = jnp.stack([q_own[0], turn(from_qzl)])
    q_mine, q_theirs = core_halves(q_two, 1)
    from_qc = swap(q_theirs, BIT_C)
    a_got = turn(from_ac).astype(F32)
    q_got = turn(from_qc)
    input_grad = to_place(x_grad[:rows], turn(from_xzh))

    groups = [q_mine[0], q_got[0], q_mine[1], q_got[1]]
    groups = [part.astype(F32) for part in groups]
    owned = (groups[0] + groups[1]) + (groups[2] + groups[3])
    owned = jnp.transpose(owned[:, 3 * cut : 3 * cut + 12])

    def attend_columns(n):
        parts = [part[:, cut * n : cut * (n + 1)] for part in groups]
        return join(zl, join(c, parts[0], parts[1], 1), join(c, parts[2], parts[3], 1), 1)

    def inner_columns(array):
        return jnp.transpose(array[:4], (1, 0, 2)).reshape(shard, 4 * cols)

    inner_owned = join(c, inner_columns(a_mine), inner_columns(a_got), 1)
    output_owned = join(c, a_mine[4], a_got[4], 1)
    return (
        outputs,
        input_grad,
        attend_columns(0),
        attend_columns(1),
        attend_columns(2),
        output_owned,
        owned[0],
        owned[1],
        owned[2],
        owned[3],
        owned[4],
        inner_owned,
        owned[8:12].reshape(-1),
        outer_owned,
        owned[5],
        owned[6],
        owned[7],
    )


def solution(mesh):
    fast = mesh.shape["dp"] == 4 and mesh.shape["sp"] == 8
    body = body_fast if fast else body_general
    in_specs = (
        P(None, "dp", "sp", None),
        P(None, "dp", "sp"),
        P(None, "dp", "sp", None),
        P(("dp", "sp"), None),
        P(("dp", "sp"), None),
        P(("dp", "sp"), None),
        P(("dp", "sp"), None),
        P(("dp", "sp")),
        P(("dp", "sp")),
        P(("dp", "sp")),
        P(("dp", "sp")),
        P(("dp", "sp")),
        P(("dp", "sp"), None),
        P(("dp", "sp")),
        P(("dp", "sp"), None),
        P(("dp", "sp")),
        P(("dp", "sp")),
        P(("dp", "sp")),
    )
    out_specs = (
        P(None, "dp", "sp", None),
        P(None, "dp", "sp", None),
        P(("dp", "sp"), None),
        P(("dp", "sp"), None),
        P(("dp", "sp"), None),
        P(("dp", "sp"), None),
        P(("dp", "sp")),
        P(("dp", "sp")),
        P(("dp", "sp")),
        P(("dp", "sp")),
        P(("dp", "sp")),
        P(("dp", "sp"), None),
        P(("dp", "sp")),
        P(("dp", "sp"), None),
        P(("dp", "sp")),
        P(("dp", "sp")),
        P(("dp", "sp")),
    )
    return jax.shard_map(body, mesh=mesh, in_specs=in_specs, out_specs=out_specs, check_vma=False)
```

```python
import functools

import jax
import jax.numpy as jnp
from jax import lax
from jax.experimental import pallas as pl
from jax.experimental.pallas import tpu as pltpu
from jax.sharding import PartitionSpec as P

HEADS = 12
HEAD = 64


EPS = 1e-12
NEG = -1e30


def product(left_matrix, right_matrix):
    return jnp.dot(left_matrix, right_matrix, preferred_element_type=jnp.float32)


def left_product(left_matrix, right_matrix):
    return lax.dot_general(
        left_matrix, right_matrix, (((0,), (0,)), ((), ())), preferred_element_type=jnp.float32
    )


def right_product(left_matrix, right_matrix):
    return lax.dot_general(
        left_matrix, right_matrix, (((1,), (1,)), ((), ())), preferred_element_type=jnp.float32
    )


def by_heads(matrix):
    return matrix.reshape(matrix.shape[0], HEADS, HEAD)


def norm_forward(summed, gain, shift):
    center = summed - jnp.mean(summed, -1, keepdims=True)
    inverse = lax.rsqrt(jnp.mean(center * center, -1, keepdims=True) + EPS)
    normed = center * inverse
    return (normed * gain + shift, normed, inverse)


def norm_backward(gradient, normed, inverse, gain):
    scaled = gradient * gain
    plain_mean = jnp.mean(scaled, -1, keepdims=True)
    cross_mean = jnp.mean(scaled * normed, -1, keepdims=True)
    return (
        (scaled - plain_mean - normed * cross_mean) * inverse,
        jnp.sum(gradient * normed, 0),
        jnp.sum(gradient, 0),
    )


def attend_forward(queries, key_rows, value_rows, seg_local, seg_all):
    row_count = queries.shape[0]
    scaling = HEAD ** (-0.5)
    query_heads = by_heads(queries)
    key_piece = lax.all_gather(key_rows, "sp", axis=0, tiled=True)
    value_piece = lax.all_gather(value_rows, "sp", axis=0, tiled=True)
    row_peak = jnp.full((HEADS, row_count), NEG, jnp.float32)
    same_doc = (seg_local[:, None] == seg_all[None, :])[None]
    scores = (
        jnp.einsum(
            "qhd,khd->hqk", query_heads, by_heads(key_piece), preferred_element_type=jnp.float32
        )
        * scaling
    )
    scores = jnp.where(same_doc, scores, NEG)
    new_peak = jnp.maximum(row_peak, jnp.max(scores, -1))
    weights = jnp.where(same_doc, jnp.exp(scores - new_peak[..., None]), 0.0)
    row_total = jnp.sum(weights, -1)
    summed = jnp.einsum(
        "hqk,khd->hqd",
        weights.astype(jnp.bfloat16),
        by_heads(value_piece),
        preferred_element_type=jnp.float32,
    )
    return (new_peak, row_total, summed)


def keys_backward(
    queries, key_rows, value_rows, context_grad, log_total, row_delta, seg_local, seg_all
):
    row_count, width = queries.shape
    scaling = HEAD ** (-0.5)
    query_heads = by_heads(queries)
    grad_heads = by_heads(context_grad)
    key_piece = lax.all_gather(key_rows, "sp", axis=0, tiled=True)
    value_piece = lax.all_gather(value_rows, "sp", axis=0, tiled=True)
    piece_rows = key_piece.shape[0]
    key_heads = by_heads(key_piece)
    same_doc = (seg_local[:, None] == seg_all[None, :])[None]
    scores = (
        jnp.einsum("qhd,khd->hqk", query_heads, key_heads, preferred_element_type=jnp.float32)
        * scaling
    )
    weights = jnp.where(same_doc, jnp.exp(scores - log_total[..., None]), 0.0)
    prob_grad = jnp.einsum(
        "qhd,khd->hqk", grad_heads, by_heads(value_piece), preferred_element_type=jnp.float32
    )
    score_grad = (weights * (prob_grad - row_delta[..., None])).astype(jnp.bfloat16)
    query_sum = jnp.einsum(
        "hqk,khd->hqd", score_grad, key_heads, preferred_element_type=jnp.float32
    )
    key_term = jnp.einsum(
        "hqk,qhd->khd", score_grad, query_heads, preferred_element_type=jnp.float32
    ).reshape(piece_rows, width)
    value_term = jnp.einsum(
        "hqk,qhd->khd", weights.astype(jnp.bfloat16), grad_heads, preferred_element_type=jnp.float32
    ).reshape(piece_rows, width)
    pair_sum = jnp.concatenate([key_term, value_term], 1)
    query_sum, pair_sum = (query_sum, pair_sum)
    pair_mine = lax.psum_scatter(pair_sum, "sp", scatter_dimension=0, tiled=True)
    query_sum = jnp.transpose(query_sum, (1, 0, 2)).reshape(row_count, width)
    return (query_sum, pair_mine[:, :width], pair_mine[:, width:])


def body_general(
    tokens,
    doc_ids,
    cotangent,
    query_weight,
    key_weight,
    value_weight,
    output_weight,
    query_bias,
    value_bias,
    output_bias,
    first_gain,
    first_shift,
    inner_weight,
    inner_bias,
    outer_weight,
    outer_bias,
    second_gain,
    second_shift,
):
    shards = (
        query_weight,
        key_weight,
        value_weight,
        output_weight,
        query_bias,
        value_bias,
        output_bias,
        first_gain,
        first_shift,
        inner_weight,
        inner_bias,
        outer_weight,
        outer_bias,
        second_gain,
        second_shift,
    )
    scaling = HEAD ** (-0.5)
    results = []
    input_grads = []
    totals = ()
    for micro in range(tokens.shape[0]):
        loaded = (
            lax.all_gather(shards[0], ("dp", "sp"), axis=0, tiled=True),
            lax.all_gather(shards[1], ("dp", "sp"), axis=0, tiled=True),
            lax.all_gather(shards[2], ("dp", "sp"), axis=0, tiled=True),
            lax.all_gather(shards[3], ("dp", "sp"), axis=0, tiled=True),
            lax.all_gather(shards[4], ("dp", "sp"), axis=0, tiled=True),
            lax.all_gather(shards[5], ("dp", "sp"), axis=0, tiled=True),
            lax.all_gather(shards[6], ("dp", "sp"), axis=0, tiled=True),
            lax.all_gather(shards[7], ("dp", "sp"), axis=0, tiled=True),
            lax.all_gather(shards[8], ("dp", "sp"), axis=0, tiled=True),
            lax.all_gather(shards[9], ("dp", "sp"), axis=0, tiled=True),
            lax.all_gather(shards[10], ("dp", "sp"), axis=0, tiled=True),
            lax.all_gather(shards[11], ("dp", "sp"), axis=0, tiled=True),
            lax.all_gather(shards[12], ("dp", "sp"), axis=0, tiled=True),
            lax.all_gather(shards[13], ("dp", "sp"), axis=0, tiled=True),
            lax.all_gather(shards[14], ("dp", "sp"), axis=0, tiled=True),
        )
        (
            w_query,
            w_key,
            w_value,
            w_output,
            b_query,
            b_value,
            b_output,
            g_first,
            s_first,
            w_inner,
            b_inner,
            w_outer,
            b_outer,
            g_second,
            s_second,
        ) = loaded
        inputs = tokens[micro, 0]
        seg_local = doc_ids[micro, 0]
        seg_all = lax.all_gather(seg_local, "sp", axis=0, tiled=True)
        row_count, width = inputs.shape
        queries = (product(inputs, w_query) + b_query).astype(jnp.bfloat16)
        key_rows = product(inputs, w_key).astype(jnp.bfloat16)
        value_rows = (product(inputs, w_value) + b_value).astype(jnp.bfloat16)
        row_peak, row_total, summed = attend_forward(
            queries, key_rows, value_rows, seg_local, seg_all
        )
        context_heads = summed / row_total[..., None]
        log_total = row_peak + jnp.log(row_total)
        context_low = (
            jnp.transpose(context_heads, (1, 0, 2)).reshape(row_count, width).astype(jnp.bfloat16)
        )
        attended = product(context_low, w_output) + b_output
        first_out, first_normed, first_inverse = norm_forward(
            inputs.astype(jnp.float32) + attended, g_first, s_first
        )
        first_low = first_out.astype(jnp.bfloat16)
        inner = product(first_low, w_inner) + b_inner
        active = jax.nn.gelu(inner, approximate=False).astype(jnp.bfloat16)
        outer = product(active, w_outer) + b_outer
        second_out, second_normed, second_inverse = norm_forward(
            first_out + outer, g_second, s_second
        )
        results.append(second_out.astype(jnp.bfloat16))
        loaded = (
            lax.all_gather(shards[0], ("dp", "sp"), axis=0, tiled=True),
            lax.all_gather(shards[1], ("dp", "sp"), axis=0, tiled=True),
            lax.all_gather(shards[2], ("dp", "sp"), axis=0, tiled=True),
            lax.all_gather(shards[3], ("dp", "sp"), axis=0, tiled=True),
            lax.all_gather(shards[4], ("dp", "sp"), axis=0, tiled=True),
            lax.all_gather(shards[5], ("dp", "sp"), axis=0, tiled=True),
            lax.all_gather(shards[6], ("dp", "sp"), axis=0, tiled=True),
            lax.all_gather(shards[7], ("dp", "sp"), axis=0, tiled=True),
            lax.all_gather(shards[8], ("dp", "sp"), axis=0, tiled=True),
            lax.all_gather(shards[9], ("dp", "sp"), axis=0, tiled=True),
            lax.all_gather(shards[10], ("dp", "sp"), axis=0, tiled=True),
            lax.all_gather(shards[11], ("dp", "sp"), axis=0, tiled=True),
            lax.all_gather(shards[12], ("dp", "sp"), axis=0, tiled=True),
            lax.all_gather(shards[13], ("dp", "sp"), axis=0, tiled=True),
            lax.all_gather(shards[14], ("dp", "sp"), axis=0, tiled=True),
        )
        (
            w_query,
            w_key,
            w_value,
            w_output,
            b_query,
            b_value,
            b_output,
            g_first,
            s_first,
            w_inner,
            b_inner,
            w_outer,
            b_outer,
            g_second,
            s_second,
        ) = loaded
        upstream = cotangent[micro, 0].astype(jnp.float32)
        second_grad, second_gain_grad, second_shift_grad = norm_backward(
            upstream, second_normed, second_inverse, g_second
        )
        outer_grad = second_grad.astype(jnp.bfloat16)
        outer_bias_grad = jnp.sum(outer_grad.astype(jnp.float32), 0)
        outer_weight_grad = left_product(active, outer_grad)
        active_grad = right_product(outer_grad, w_outer)
        _, gelu_pull = jax.vjp(lambda hidden: jax.nn.gelu(hidden, approximate=False), inner)
        inner_grad = gelu_pull(active_grad)[0].astype(jnp.bfloat16)
        inner_bias_grad = jnp.sum(inner_grad.astype(jnp.float32), 0)
        inner_weight_grad = left_product(first_low, inner_grad)
        first_incoming = second_grad + right_product(inner_grad, w_inner)
        first_grad, first_gain_grad, first_shift_grad = norm_backward(
            first_incoming, first_normed, first_inverse, g_first
        )
        attended_grad = first_grad.astype(jnp.bfloat16)
        output_bias_grad = jnp.sum(attended_grad.astype(jnp.float32), 0)
        output_weight_grad = left_product(context_low, attended_grad)
        context_grad = right_product(attended_grad, w_output).astype(jnp.bfloat16)
        row_delta = jnp.sum(jnp.transpose(by_heads(context_grad), (1, 0, 2)) * context_heads, -1)
        query_sum, key_sum, value_sum = keys_backward(
            queries, key_rows, value_rows, context_grad, log_total, row_delta, seg_local, seg_all
        )
        query_grad = (query_sum * scaling).astype(jnp.bfloat16)
        key_grad = (key_sum * scaling).astype(jnp.bfloat16)
        value_grad = value_sum.astype(jnp.bfloat16)
        query_bias_grad = jnp.sum(query_grad.astype(jnp.float32), 0)
        value_bias_grad = jnp.sum(value_grad.astype(jnp.float32), 0)
        query_weight_grad = left_product(inputs, query_grad)
        key_weight_grad = left_product(inputs, key_grad)
        value_weight_grad = left_product(inputs, value_grad)
        input_grads.append(
            first_grad
            + right_product(query_grad, w_query)
            + right_product(key_grad, w_key)
            + right_product(value_grad, w_value)
        )
        terms = (
            query_weight_grad,
            key_weight_grad,
            value_weight_grad,
            output_weight_grad,
            query_bias_grad,
            value_bias_grad,
            output_bias_grad,
            first_gain_grad,
            first_shift_grad,
            inner_weight_grad,
            inner_bias_grad,
            outer_weight_grad,
            outer_bias_grad,
            second_gain_grad,
            second_shift_grad,
        )
        if micro == 0:
            totals = terms
        else:
            totals = tuple((earlier + latest for earlier, latest in zip(totals, terms)))
    owned = lax.psum_scatter(totals, ("dp", "sp"), scatter_dimension=0, tiled=True)
    return (
        jnp.stack(results)[:, None],
        jnp.stack(input_grads)[:, None],
        owned[0],
        owned[1],
        owned[2],
        owned[3],
        owned[4],
        owned[5],
        owned[6],
        owned[7],
        owned[8],
        owned[9],
        owned[10],
        owned[11],
        owned[12],
        owned[13],
        owned[14],
    )


BIT_Y, BIT_X, BIT_ZH, BIT_ZL, BIT_C = 16, 8, 4, 2, 1
AXES = ("dp", "sp")
GAUSS = 0.3989422804014327
LIMITS = {
    "first": 2, "query": 2, "last": 4, "attend": 24, "forward": 20, "outer_grad": 12, "middle": 20, "inner_grad": 12,
    "attend_back": 24, "attend_weight": 20,
}
SIDE = 64
SCALE = 0.0
DOC_ROWS = 16
BF16, F32 = jnp.bfloat16, jnp.float32


def low(array):
    return array.astype(BF16)


def swap(array, mask, after=None):
    if after is not None:
        array, _ = lax.optimization_barrier((array, after))
    return lax.ppermute(array, AXES, [(i, i ^ mask) for i in range(32)])


class Turns:
    def __init__(self):
        self.last = None

    def __call__(self, array):
        if self.last is not None:
            array, _ = lax.optimization_barrier((array, self.last))
        self.last = array
        return array


def tie(array, other):
    return lax.optimization_barrier((array, other))[0]


def join(bit, own, other, axis=0):
    return jnp.where(
        bit == 0, jnp.concatenate([own, other], axis), jnp.concatenate([other, own], axis)
    )


def pair(own, other):
    return jnp.concatenate([own, other], 0)


def add_low(own, other):
    return low(own.astype(F32) + other.astype(F32))


def call(kernel, outs, operands, spaces=None, scratch=(), flops=0, traffic=0, name=None, out_spaces=None):
    whole = pl.BlockSpec(memory_space=pltpu.VMEM)
    specs = [pl.BlockSpec(memory_space=pltpu.SMEM)]
    operands = list(operands)
    for n, kind in enumerate(spaces or ["vmem"] * (len(operands) - 1), 1):
        specs.append(whole if kind == "vmem" else pl.BlockSpec(memory_space=pltpu.HBM))
        if kind == "hbm":
            operands[n] = pltpu.with_memory_space_constraint(operands[n], pltpu.HBM)
    return pl.pallas_call(
        kernel,
        out_shape=tuple(jax.ShapeDtypeStruct(shape, dtype) for shape, dtype in outs),
        in_specs=specs,
        out_specs=tuple(
            whole if kind == "vmem" else pl.BlockSpec(memory_space=pltpu.HBM)
            for kind in (out_spaces or ["vmem"] * len(outs))
        ),
        scratch_shapes=list(scratch),
        compiler_params=pltpu.CompilerParams(vmem_limit_bytes=LIMITS[name] * 1024 * 1024),
        cost_estimate=pl.CostEstimate(flops=int(flops * SCALE) + 1, transcendentals=0, bytes_accessed=int(traffic * SCALE) + 1),
        name=name,
    )(*operands)


def block_at(place, k):
    return (place[0] ^ (k // 2)) * 2 + (place[1] ^ (k % 2))


def unit_at(place, u):
    return (place[2] ^ (u // 2)) * 2 + (place[3] ^ (u % 2))


def first_kernel(place, tokens, docs, inner, outer, output, x_keep, x_give, keep, give, ids, sems):
    zh, c = place[2], place[4]
    rows, width = tokens.shape[1:]
    shard, cols = keep.shape[1:]
    started = [pltpu.make_async_copy(docs, ids, sems.at[0])]
    for flip in range(2):
        x_out, out = (x_keep, x_give)[flip], (keep, give)[flip]
        moves = [(tokens.at[zh ^ flip], x_out.at[pl.ds(0, rows), :])]
        half = c ^ flip
        for j in range(4):
            at = pl.ds(pl.multiple_of(half * (4 * cols) + j * cols, 128), cols)
            moves.append((inner.at[:, at], out.at[j]))
        at = pl.ds(pl.multiple_of(half * cols, 128), cols)
        for j in range(4):
            moves.append((outer.at[pl.ds(shard * j, shard), at], out.at[4 + j]))
        moves.append((output.at[:, at], out.at[8]))
        for source, target in moves:
            started.append(pltpu.make_async_copy(source, target, sems.at[len(started)]))
    for copy in started:
        copy.start()
    for copy in started:
        copy.wait()
    for flip, out in ((0, x_keep), (1, x_give)):
        line = ids[pl.ds(zh ^ flip, 1), :].astype(F32)
        line = jnp.concatenate([line, jnp.zeros((1, width - rows), F32)], 1)
        out[rows : rows + DOC_ROWS, :] = low(jnp.broadcast_to(line, (DOC_ROWS, width)))


def query_kernel(place, wq, wk, wv, smalls, q_keep, q_give, weights, blocks, side, sems):
    zl, c = place[3], place[4]
    shard, width = wq.shape
    cut = width // 4
    started = [
        pltpu.make_async_copy(w, weights.at[n], sems.at[n]) for n, w in enumerate((wq, wk, wv))
    ]
    for copy in started:
        copy.start()
    side[...] = jnp.zeros_like(side)
    side[SIDE : SIDE + 16, :] = smalls[...]
    columns = low(jnp.transpose(side[...]))[:shard, SIDE:]
    for copy in started:
        copy.wait()
    for p in range(4):
        at = slice(cut * p, cut * (p + 1))
        blocks[p] = jnp.concatenate([weights[0, :, at], weights[1, :, at], weights[2, :, at], columns], 1)
    for r in range(2):
        q_keep[r] = blocks[2 * (zl ^ r) + c]
        q_give[r] = blocks[2 * (zl ^ r) + (1 - c)]


PARTS = (((2, 0), (3, 0)), ((0, 0), (3, 1)), ((2, 1), (1, 0)), ((0, 1), (1, 1)))


def put_rows(out, k, u, start, value):
    half = out.shape[3]
    stop = start + value.shape[0]
    if start < half:
        part, n = PARTS[k][0]
        out[part, n, u, start : min(stop, half), :] = value[: min(stop, half) - start, :]
    if stop > half:
        part, n = PARTS[k][1]
        first = max(start, half)
        out[part, n, u, first - half : stop - half, :] = value[first - start :, :]


def head_copies(pieces, x_own, x_other, place, w, x, sems):
    size = pieces[0].shape[1]
    started = []
    for k, part in enumerate(pieces):
        for u in range(4):
            at = block_at(place, k) * (4 * size) + unit_at(place, u) * size
            target = w.at[pl.ds(pl.multiple_of(at, 16), size), :]
            started.append(pltpu.make_async_copy(part.at[u], target, sems.at[len(started)]))
    for n, part in enumerate((x_own, x_other)):
        started.append(pltpu.make_async_copy(part, x.at[n], sems.at[len(started)]))
    for copy in started:
        copy.start()
    return started


def attend_kernel(place, w0, w1, w2, w3, x_own, x_other, *refs):
    context_out, (qkv, wide, rows_of, vec_out) = refs[:2], refs[2:6]
    w, doc_col = refs[6:]
    size = w0.shape[1]
    for k, part in enumerate((w0, w1, w2, w3)):
        for u in range(4):
            at = block_at(place, k) * (4 * size) + unit_at(place, u) * size
            w[pl.ds(pl.multiple_of(at, 16), size), :] = part[u]
    cut = qkv.shape[2]
    heads = cut // HEAD
    group = place[5]
    tile = slice(3 * cut - SIDE, 3 * cut + SIDE)
    vec_out[...] = jnp.transpose(w[:, tile].astype(F32))[SIDE : SIDE + 16, :]
    biases = w[pl.ds(pl.multiple_of(group * cut, 64), cut), tile].astype(F32)
    biases = jnp.transpose(jnp.concatenate([biases, jnp.zeros((64, 2 * SIDE), F32)], 0))
    bq, bv = biases[SIDE : SIDE + 1, :cut], biases[SIDE + 1 : SIDE + 2, :cut]
    rows = x_own.shape[1] - DOC_ROWS
    ids = []
    for n in range(8):
        source = (x_own, x_other)[n // 4]
        part = product(source[n % 4, 0:rows, :], w[:, : 3 * cut])
        at = pl.ds(rows * n, rows)
        qkv[0, at, :] = low(part[:, :cut] + bq)
        qkv[1, at, :] = low(part[:, cut : 2 * cut])
        qkv[2, at, :] = low(part[:, 2 * cut :] + bv)
        ids.append(source[n % 4, rows : rows + 1, 0:128].astype(F32))
    doc_row = jnp.concatenate(ids, 1)
    rows_of[8:16, :] = jnp.broadcast_to(doc_row, (8, doc_row.shape[1]))
    turned = jnp.transpose(jnp.concatenate(ids + [jnp.zeros((120, 128), F32)], 0))
    for n in range(8):
        doc_col[pl.ds(rows * n, rows), :] = jnp.broadcast_to(turned[:, n : n + 1], (rows, 128))
    rows = 2 * rows
    lane = lax.broadcasted_iota(jnp.int32, (rows, 128), 1)
    for i in (2, 3, 0, 1):
        at = pl.ds(rows * i, rows)
        same = doc_col[at, 0:1] == doc_row
        pieces = []
        logs = jnp.zeros((rows, 128), F32)
        for h in range(heads):
            cols = slice(HEAD * h, HEAD * (h + 1))
            query = qkv[0, at, cols] * BF16(HEAD**-0.5)
            scores = right_product(query, qkv[1, :, cols])
            scores = jnp.where(same, scores, NEG)
            peak = jnp.max(scores, -1, keepdims=True)
            weights = jnp.exp(scores - peak)
            denom = jnp.sum(weights, -1, keepdims=True)
            summed = product(low(weights), qkv[2, :, cols])
            pieces.append(summed / denom)
            logs = jnp.where(lane == h, peak + jnp.log(denom), logs)
        context = jnp.concatenate(pieces, 1)
        wide[at, :] = context
        context_out[i // 2][i % 2] = low(context)
        rows_of[0:8, at] = jnp.transpose(logs)[:8, :]


def attend_back_kernel(
    place, qkv_in, wide_in, rows_in, g_own, g_zl, g_c, grads, sums, qkv, wide, rows_of, dq_acc, delta_ref, dc, doc_col, sems
):
    copies_in = [
        pltpu.make_async_copy(source, target, sems.at[n])
        for n, (source, target) in enumerate(((qkv_in, qkv), (wide_in, wide), (rows_in, rows_of)))
    ]
    for copy in copies_in:
        copy.start()
    for copy in copies_in:
        copy.wait()
    total, cut = wide.shape
    heads = cut // HEAD
    rows = total // 4
    scaling = HEAD**-0.5
    lane = lax.broadcasted_iota(jnp.int32, (rows, 128), 1)
    doc_row = rows_of[8:9, :]
    for n in range(total // 128):
        at = slice(128 * n, 128 * (n + 1))
        doc_col[at, :] = jnp.transpose(jnp.broadcast_to(rows_of[8:9, at], (128, 128)))
    for i in range(4):
        at = pl.ds(rows * i, rows)
        grad = (g_own[...], g_zl[0], g_c[0], g_zl[1])[i]
        dc[at, :] = grad
        prod = grad.astype(F32) * wide[at, :]
        cols = jnp.zeros((rows, 128), F32)
        for h in range(heads):
            piece = jnp.sum(prod[:, HEAD * h : HEAD * (h + 1)], -1, keepdims=True)
            cols = jnp.where(lane == h, piece, cols)
        delta_ref[:, at] = jnp.transpose(cols)[:8, :]
    for h in range(heads):
        cols = slice(HEAD * h, HEAD * (h + 1))
        query = qkv[0, :, cols]
        scaled = query * BF16(scaling)
        grad_rows = dc[:, cols]
        for i in range(4):
            at = pl.ds(rows * i, rows)
            key = qkv[1, at, cols]
            value = qkv[2, at, cols]
            same = doc_col[at, 0:1] == doc_row
            scores = jnp.where(same, right_product(key, scaled), NEG)
            probs = jnp.exp(scores - rows_of[h : h + 1, :])
            prob_grad = right_product(value, grad_rows)
            score_grad = low(probs * (prob_grad - delta_ref[h : h + 1, :]))
            grads[at, cut + HEAD * h : cut + HEAD * (h + 1)] = low(product(score_grad, query) * scaling)
            grads[at, 2 * cut + HEAD * h : 2 * cut + HEAD * (h + 1)] = low(product(low(probs), grad_rows))
            piece = left_product(key, score_grad)
            if i == 0:
                dq_acc[...] = piece
            else:
                dq_acc[...] += piece
        grads[:, cols] = low(jnp.transpose(dq_acc[...]) * scaling)
    grads[:, 3 * cut :] = jnp.zeros((total, SIDE), BF16)
    sums[0:1, :] = jnp.sum(grads[...].astype(F32), 0, keepdims=True)


def attend_weight_kernel(
    place, w0, w1, w2, w3, x_own, x_other, grads, sums, sums_a, sums_b, sums_c, *refs
):
    out, input_outs, (turned, w, x, side, tall, sems) = refs[0], refs[1:4], refs[4:]
    copies_in = head_copies((w0, w1, w2, w3), x_own, x_other, place, w, x, sems)
    rows = x.shape[2] - DOC_ROWS
    group = place[5]
    width = sums_a.shape[1]
    cut = width // 4
    early = jnp.concatenate([sums_c[2:3, :], sums_c[0:2, :], sums_a[2:3, :], sums_a[0:2, :]], 0)
    pad = jnp.concatenate(
        [jnp.zeros((SIDE + 2, width), F32), early, jnp.zeros((SIDE - 8, width), F32)], 0
    )
    side[...] = jnp.transpose(pad)
    own = jnp.concatenate([sums[0:1, :cut], sums[0:1, 2 * cut : 3 * cut]], 0)
    own = jnp.concatenate([own, jnp.zeros((2, 256 - cut), F32)], 1)
    own = jnp.concatenate([jnp.zeros((SIDE, 256), F32), own, jnp.zeros((SIDE - 2, 256), F32)], 0)
    at = pl.ds(pl.multiple_of(group * cut, 64), cut)
    side[at, :] += jnp.transpose(own)[:cut, :]
    tall[...] = jnp.transpose(jnp.broadcast_to(sums_b[0:1, :], (128, sums_b.shape[1])))
    shard = width // 32
    lane = lax.broadcasted_iota(jnp.int32, (shard, 128), 1)
    for n in range(32):
        at = slice(shard * n, shard * (n + 1))
        value = side[at, :]
        for q in range(4):
            start = 4 * shard * n + shard * q
            value = jnp.where(lane == SIDE + 8 + q, tall[start : start + shard, :], value)
        side[at, :] = value
    for copy in copies_in:
        copy.wait()
    for n in range(8):
        turned[:, pl.ds(rows * n, rows)] = jnp.transpose(x[n // 4, n % 4, 0:rows, :])
    size = w0.shape[1]
    for k in range(4):
        at = pl.ds(pl.multiple_of(block_at(place, k) * (4 * size), 64), 4 * size)
        piece = product(turned[at, :], grads[...])
        piece = jnp.concatenate([piece[:, : 3 * cut - SIDE], piece[:, 3 * cut - SIDE :] + side[at, :]], 1)
        for a in range(4):
            put_rows(out, k, unit_at(place, a), 0, low(piece[size * a : size * (a + 1), :]))
    for n in (2, 3, 1, 0):
        at = pl.ds(2 * rows * n, 2 * rows)
        part = right_product(grads[at, : 3 * cut], w[:, : 3 * cut])
        if n == 0:
            input_outs[0][...] = part
        elif n == 1:
            input_outs[1][...] = low(part)
        else:
            input_outs[2][n - 2] = low(part)


def last_kernel(place, q_mine, q_got, a_mine, a_got, wq, wk, wv, wo, wi, small, buf_q, buf_o, buf_i, sems):
    zl, c = place[3], place[4]
    shard, width = wq.shape
    cut = width // 4
    parts = [q_mine[0].astype(F32), q_got[0].astype(F32), q_mine[1].astype(F32), q_got[1].astype(F32)]

    def ordered(bit, own, other):
        return jnp.concatenate([jnp.where(bit == 0, own, other), jnp.where(bit == 0, other, own)], 1)

    for n in range(3):
        cols = [part[:, cut * n : cut * (n + 1)] for part in parts]
        near, far = ordered(c, cols[0], cols[1]), ordered(c, cols[2], cols[3])
        buf_q[n] = ordered(zl, near, far)
    started = [pltpu.make_async_copy(buf_q.at[n], out, sems.at[n]) for n, out in enumerate((wq, wk, wv))]
    mine = [a_mine[j] for j in range(5)]
    theirs = [a_got[j].astype(F32) for j in range(5)]
    buf_o[...] = ordered(c, mine[4], theirs[4])
    buf_i[...] = ordered(c, jnp.concatenate(mine[:4], 1), jnp.concatenate(theirs[:4], 1))
    started += [pltpu.make_async_copy(buf_o, wo, sems.at[3]), pltpu.make_async_copy(buf_i, wi, sems.at[4])]
    for copy in started:
        copy.start()
    tile = slice(3 * cut - SIDE, 3 * cut + SIDE)
    total = (parts[0][:, tile] + parts[1][:, tile]) + (parts[2][:, tile] + parts[3][:, tile])
    total = jnp.concatenate([total, jnp.zeros((128 - shard, 2 * SIDE), F32)], 0)
    small[...] = jnp.transpose(total)[SIDE : SIDE + 16, :]
    for copy in started:
        copy.wait()


def copies(pieces, whole, place, sems, base, column_blocks, first, row_count):
    c = place[4]
    started = []
    for half in range(2):
        for k in range(4):
            for u in range(4):
                for j in range(column_blocks):
                    source = pieces[half * 4 + k]
                    cols = source.shape[-1]
                    row = block_at(place, k) * (4 * row_count) + unit_at(place, u) * row_count
                    col = (c ^ half) * (column_blocks * cols) + j * cols
                    target = whole.at[
                        pl.ds(pl.multiple_of(row, 16), row_count), pl.ds(pl.multiple_of(col, 128), cols)
                    ]
                    if column_blocks > 1:
                        source = source.at[u, j]
                    else:
                        source = source.at[u, pl.ds(first, row_count), :]
                    started.append(pltpu.make_async_copy(source, target, sems.at[base + len(started)]))
    return started


def forward_kernel(place, c_own, c_c, c_zl, x_ref, vec, b_inner, *refs):
    a_p, b_p = refs[:8], refs[8:16]
    (out, n2_out, r2_out, h1b_out, n1_out, r1_out, g_out, gp_out) = refs[16:24]
    wo, wi, wu, sems = refs[24:]
    unit = wo.shape[0] // 16
    copy_o = copies(b_p, wo, place, sems, 0, 1, 4 * unit, unit)
    copy_i = copies(a_p, wi, place, sems, 32, 4, 0, unit)
    copy_u = copies(b_p, wu, place, sems, 160, 1, 0, 4 * unit)
    for copy in copy_o + copy_i + copy_u:
        copy.start()
    group = place[5]
    rows = x_ref.shape[1] - DOC_ROWS
    cut = c_own.shape[-1]
    for copy in copy_o:
        copy.wait()
    attended = vec[2:3, :]
    for mask in range(4):
        part = (c_own, c_c, c_zl, c_zl)[mask]
        at = pl.ds(pl.multiple_of((group ^ mask) * cut, 64), cut)
        attended = attended + product(part[mask // 3], wo[at, :])
    tokens = jnp.concatenate([x_ref[0, 0:rows, :], x_ref[1, 0:rows, :]], 0)
    first_out, normed, inverse = norm_forward(tokens.astype(F32) + attended, vec[3:4, :], vec[4:5, :])
    n1_out[...] = normed
    r1_out[...] = jnp.broadcast_to(inverse, r1_out.shape)
    h1b_out[...] = low(first_out)
    for copy in copy_i + copy_u:
        copy.wait()
    outer = vec[5:6, :]
    step = 512
    for j in range(wi.shape[1] // step):
        at = slice(step * j, step * (j + 1))
        hidden = product(h1b_out[...], wi[:, at]) + b_inner[:, at]
        half = 0.5 + 0.5 * lax.erf(hidden * (0.5**0.5))
        active = low(hidden * half)
        g_out[:, at] = active
        gp_out[:, at] = half + hidden * jnp.exp(hidden * hidden * -0.5) * GAUSS
        outer = outer + product(active, wu[at, :])
    second_out, normed, inverse = norm_forward(first_out + outer, vec[6:7, :], vec[7:8, :])
    out[...] = low(second_out)
    n2_out[...] = normed
    r2_out[...] = jnp.broadcast_to(inverse, r2_out.shape)


def outer_grad_kernel(
    place, cot_own, cot_other, n2, r2, vec, g_ref, give, keep, dz2_out, df_ref, sums
):
    c = place[4]
    upstream = jnp.concatenate([cot_own[...], cot_other[...]], 0).astype(F32)
    grad, gain_grad, shift_grad = norm_backward(upstream, n2[...], r2[:, 0:1], vec[6:7, :])
    dz2_out[...] = grad
    grad_low = low(grad)
    df_ref[...] = grad_low
    sums[0:1, :] = gain_grad[None]
    sums[1:2, :] = shift_grad[None]
    sums[2:3, :] = jnp.sum(grad_low.astype(F32), 0, keepdims=True)
    unit, cols = 2 * give.shape[3], give.shape[4]
    give_part = df_ref[:, pl.ds(pl.multiple_of((1 - c) * cols, 128), cols)]
    keep_part = df_ref[:, pl.ds(pl.multiple_of(c * cols, 128), cols)]
    both = jnp.concatenate([give_part, keep_part], 1)
    for k in range(4):
        at = pl.ds(pl.multiple_of(block_at(place, k) * (4 * unit), 128), 4 * unit)
        piece = low(left_product(g_ref[:, at], both))
        for a in range(4):
            at = slice(unit * a, unit * (a + 1))
            put_rows(give, k, unit_at(place, a), 0, piece[at, :cols])
            put_rows(keep, k, unit_at(place, a), 0, piece[at, cols:])


def middle_kernel(place, df_ref, gp_ref, dz2, n1, r1, vec, *refs):
    a_p, b_p = refs[:8], refs[8:16]
    du, grad_out, da, dc0, dc1, dc_give, sums, sums_b = refs[16:24]
    wo, wi, wu, sems = refs[24:]
    unit = wo.shape[0] // 16
    copy_o = copies(b_p, wo, place, sems, 0, 1, 4 * unit, unit)
    copy_i = copies(a_p, wi, place, sems, 32, 4, 0, unit)
    copy_u = copies(b_p, wu, place, sems, 160, 1, 0, 4 * unit)
    for copy in copy_u + copy_i + copy_o:
        copy.start()
    group = place[5]
    for copy in copy_u + copy_i:
        copy.wait()
    step = 512
    incoming = dz2[...]
    for j in range(wu.shape[0] // step):
        at = slice(step * j, step * (j + 1))
        grad = low(right_product(df_ref[...], wu[at, :]) * gp_ref[:, at])
        du[:, at] = grad
        sums_b[0:1, at] = jnp.sum(grad.astype(F32), 0, keepdims=True)
        incoming = incoming + right_product(grad, wi[:, at])
    for copy in copy_o:
        copy.wait()
    grad, gain_grad, shift_grad = norm_backward(incoming, n1[...], r1[:, 0:1], vec[3:4, :])
    grad_out[...] = grad
    grad_low = low(grad)
    da[...] = grad_low
    sums[0:1, :] = gain_grad[None]
    sums[1:2, :] = shift_grad[None]
    sums[2:3, :] = jnp.sum(grad_low.astype(F32), 0, keepdims=True)
    cut = dc0.shape[1]
    for mask in (1, 3, 0, 2):
        at = pl.ds(pl.multiple_of((group ^ mask) * cut, 64), cut)
        part = low(right_product(grad_low, wo[at, :]))
        if mask % 2:
            dc_give[mask // 2] = part
        else:
            (dc0, dc1)[mask // 2][...] = part


def inner_grad_kernel(place, h1b_ref, du, da, c_own, c_c, c_zl, give, keep, turned, cs):
    c, group = place[4], place[5]
    turned[...] = jnp.transpose(h1b_ref[...])
    for mask in range(4):
        cs[mask] = (c_own, c_c, c_zl, c_zl)[mask][mask // 3]
    unit, cols = 2 * give.shape[3] // 5, give.shape[4]
    blocks = 5
    wide = (blocks - 1) * cols
    for half in range(2):
        side = c ^ 1 ^ half
        right = du[:, pl.ds(pl.multiple_of(side * wide, 128), wide)]
        right_low = da[:, pl.ds(pl.multiple_of(side * cols, 128), cols)]
        for k in range(4):
            block = block_at(place, k)
            at = pl.ds(pl.multiple_of(block * (4 * unit), 64), 4 * unit)
            piece = low(product(turned[at, :], right))
            tail = low(left_product(cs[block ^ group], right_low))
            for a in range(4):
                u = unit_at(place, a)
                rows = slice(unit * a, unit * (a + 1))
                for j in range(blocks):
                    part = piece[rows, cols * j : cols * (j + 1)] if j < blocks - 1 else tail[rows, :]
                    put_rows((give, keep)[half], k, u, unit * j, part)


def body_fast(
    tokens,
    doc_ids,
    cotangent,
    query_weight,
    key_weight,
    value_weight,
    output_weight,
    query_bias,
    value_bias,
    output_bias,
    first_gain,
    first_shift,
    inner_weight,
    inner_bias,
    outer_weight,
    outer_bias,
    second_gain,
    second_shift,
):
    dp, sp = lax.axis_index("dp"), lax.axis_index("sp")
    y, x, zh, zl, c = dp // 2, dp % 2, sp // 4, (sp // 2) % 2, sp % 2
    place = jnp.stack([y, x, zh, zl, c, sp % 4]).astype(jnp.int32)
    width, hidden, rows = tokens.shape[-1], inner_weight.shape[1], tokens.shape[2]
    cut, shard = width // 4, query_weight.shape[0]
    unit = 2 * shard
    wide = 3 * cut + SIDE
    own, total = 2 * rows, 8 * rows
    turn = Turns()

    x_rows = rows + DOC_ROWS
    cols = hidden // 8
    x_keep, x_give, w_keep, w_give = call(
        first_kernel,
        [((x_rows, width), BF16)] * 2 + [((9, shard, cols), BF16)] * 2,
        [place, tokens[:, 0], doc_ids[:, 0], inner_weight, outer_weight, output_weight],
        ["hbm"] * 5,
        scratch=[pltpu.VMEM((2, rows), jnp.int32), pltpu.SemaphoreType.DMA((24,))],
        name="first",
    )
    from_xzh = swap(x_give, BIT_ZH)
    got = turn(swap(w_give, BIT_C))

    def zl_half(array):
        half = array.shape[1] // 2
        return lax.dynamic_slice_in_dim(array, zl * half, half, 1)

    def far_pair(own_half, other_half):
        turned = pair(other_half[1:], other_half[:1])
        return join(zl, own_half, turned, 1)

    a_unit = join(c, w_keep[:4], got[:4], 1)
    b_unit = jnp.concatenate(
        [
            join(c, w_keep[4:8].reshape(4 * shard, cols), got[4:8].reshape(4 * shard, cols)),
            join(c, w_keep[8], got[8]),
        ]
    )
    from_a2 = swap(a_unit[None], BIT_ZL)

    a_pair = pair(a_unit[None], turn(from_a2))
    from_a4 = swap(zl_half(a_pair), BIT_ZH)
    from_b2 = swap(b_unit[None], BIT_ZL, a_pair)
    b_pair = pair(b_unit[None], turn(from_b2))
    a_half = turn(from_a4)
    from_a5 = swap(a_half, BIT_ZL)
    from_b4 = swap(zl_half(b_pair), BIT_ZH, a_half)

    smalls = [
        query_bias, value_bias, output_bias, first_gain, first_shift,
        outer_bias, second_gain, second_shift,
    ] + [inner_bias[shard * q : shard * (q + 1)] for q in range(4)]
    smalls = list(lax.optimization_barrier((*smalls, a_half))[:-1])
    row = lax.broadcasted_iota(jnp.int32, (16, 128), 0)
    packed = jnp.zeros((16, 128), F32)
    for n, small in enumerate(smalls):
        wide_small = jnp.pad(small.astype(F32), (0, 128 - shard))
        packed = jnp.where(row == n, wide_small[None], packed)
    q_keep, q_give = call(
        query_kernel,
        [((2, shard, wide), BF16)] * 2,
        [place, tie(query_weight, a_half), key_weight, value_weight, packed],
        ["hbm"] * 3 + ["vmem"],
        scratch=[
            pltpu.VMEM((3, shard, width), BF16),
            pltpu.VMEM((4, shard, wide), BF16),
            pltpu.VMEM((128, 128), F32),
            pltpu.SemaphoreType.DMA((3,)),
        ],
        name="query",
    )
    mine = jnp.stack([x_keep, turn(from_xzh)])
    a_own = pair(a_pair, far_pair(a_half, turn(from_a5)))
    from_ax = swap(a_own, BIT_X)
    from_ay = swap(a_own, BIT_Y)
    from_qc = swap(turn(q_give), BIT_C)
    b_half = turn(from_b4)
    from_b5 = swap(b_half, BIT_ZL)
    q_unit = join(c, q_keep, turn(from_qc), 1)
    from_qzl = swap(q_unit[1], BIT_ZL)
    q_pair = jnp.stack([q_unit[0], turn(from_qzl)])
    from_qzh = swap(q_pair, BIT_ZH)
    b_own = pair(b_pair, far_pair(b_half, turn(from_b5)))
    from_xzl = swap(mine, BIT_ZL, b_own)

    def halves_of(array, axis):
        half = array.shape[axis] // 2
        return (
            lax.slice_in_dim(array, 0, half, axis=axis),
            lax.slice_in_dim(array, half, 2 * half, axis=axis),
        )

    def corner_hop(over_x, over_y, axis):
        return (
            swap(halves_of(over_y, axis)[0], BIT_X),
            swap(halves_of(over_x, axis)[1], BIT_Y),
        )

    a_y = turn(from_ay)
    a_x = turn(from_ax)
    from_axy = corner_hop(a_x, a_y, 1)
    q_own = pair(q_pair, turn(from_qzh))
    from_qy = swap(q_own, BIT_Y, a_y)
    from_qx = swap(q_own, BIT_X, a_x)
    x_own = pair(mine, turn(from_xzl))
    from_xc = swap(x_own, BIT_C)
    q_y = turn(from_qy)
    q_x = turn(from_qx)
    a_xy = jnp.concatenate([turn(from_axy[0]), turn(from_axy[1])], 1)
    x_other = turn(from_xc)
    from_qxy = corner_hop(q_x, q_y, 0)
    from_a0c = swap(a_own, BIT_C, x_other)
    a_c = [turn(from_a0c)]
    from_a1c = swap(a_x, BIT_C, a_c[0])
    a_c.append(turn(from_a1c))
    from_a2c = swap(a_y, BIT_C, a_c[1])
    q_xy = pair(turn(from_qxy[0]), turn(from_qxy[1]))
    from_bx = swap(b_own, BIT_X, q_xy)
    from_by = swap(b_own, BIT_Y, q_xy)
    a_c.append(turn(from_a2c))
    from_a3c = swap(a_xy, BIT_C, a_c[2])
    from_b0c = swap(b_own, BIT_C, a_c[2])
    w_attend = [q_own, q_x, q_y, q_xy]

    head_scratch = [pltpu.VMEM((width, wide), BF16), pltpu.VMEM((2, 4, x_rows, width), BF16)]
    saved = [((3, total, cut), BF16), ((total, cut), F32), ((16, total), F32)]
    results = call(
        attend_kernel,
        [((2, own, cut), BF16)] * 2 + saved + [((16, width), F32)],
        [place, *w_attend, x_own, tie(x_other, a_c[2])],
        scratch=[head_scratch[0], pltpu.VMEM((total, 128), F32)],
        name="attend",
    )
    context_keep, context_give, qkv, context_wide, rows_saved, vec = results
    context_give = turn(context_give)
    a_c.append(turn(from_a3c))
    b_c = [turn(from_b0c)]
    b_y = turn(from_by)
    b_x = turn(from_bx)
    from_bxy = corner_hop(b_x, b_y, 1)
    from_cc = swap(context_give, BIT_C, b_x)
    got = turn(from_cc)
    from_czl = swap(pair(context_keep[1:], got[1:]), BIT_ZL)
    context = [context_keep, got]
    b_inner = jnp.transpose(tie(vec, got)[8:12].reshape(4, 32, shard), (1, 0, 2)).reshape(1, hidden)
    b_inner = turn(b_inner)
    cot_keep = lax.dynamic_index_in_dim(cotangent[:, 0], zh, 0, False)
    cot_give = turn(lax.dynamic_index_in_dim(cotangent[:, 0], 1 - zh, 0, False))
    from_cot = swap(cot_give, BIT_ZH)
    from_b1c = swap(b_x, BIT_C, got)
    from_b2c = swap(b_y, BIT_C, got)
    b_c.append(turn(from_b1c))
    context.append(turn(from_czl))
    b_xy = jnp.concatenate([turn(from_bxy[0]), turn(from_bxy[1])], 1)
    from_b3c = swap(b_xy, BIT_C)
    b_c.append(turn(from_b2c))
    b_c.append(turn(from_b3c))
    a_pieces = [a_own, a_x, a_y, a_xy, *a_c]
    b_pieces = [b_own, b_x, b_y, b_xy, *b_c]

    whole = [
        pltpu.VMEM((width, width), BF16),
        pltpu.VMEM((width, hidden), BF16),
        pltpu.VMEM((hidden, width), BF16),
        pltpu.SemaphoreType.DMA((192,)),
    ]
    results = call(
        forward_kernel,
        [
            ((own, width), BF16), ((own, width), F32), ((own, 128), F32), ((own, width), BF16),
            ((own, width), F32), ((own, 128), F32), ((own, hidden), BF16), ((own, hidden), F32),
        ],
        [place, *context, mine, turn(vec), b_inner, *a_pieces, *b_pieces],
        ["vmem"] * 6 + ["hbm"] * 16,
        whole,
        flops=4 * own * width * hidden * 2,
        traffic=4 * width * hidden * 2,
        name="forward",
    )
    second_out, second_normed, second_inverse, first_low, normed, inverse, active, slope = results
    second_normed = turn(second_normed)

    def to_place(kept, other):
        return join(zh, kept[None], other[None].astype(kept.dtype))[:, None]

    def parts_sum(keep, got):
        return [add_low(keep[n], got[n]) for n in range(4)]

    def first_hop(parts, after=None):
        return swap(parts[0], BIT_X, after), swap(parts[1], BIT_Y, after)

    def second_hop(parts, from_x, from_y):
        left, right = add_low(parts[2], from_x), add_low(parts[3], from_y)
        return (left[0], right[0]), swap(left[1], BIT_Y), swap(right[1], BIT_X)

    def last_hop(owns, from_y, from_x):
        return jnp.concatenate([add_low(owns[0], from_y), add_low(owns[1], from_x)], 1)

    def zl_halves(array):
        half = array.shape[1] // 2
        one, two = array[:, :half], array[:, half:]
        return jnp.where(zl == 0, one, two), jnp.where(zl == 0, two, one)

    cot_other = turn(from_cot)
    b_shape, a_shape = ((4, 2, 4, 2 * unit, cols), BF16), ((4, 2, 4, 5 * unit // 2, cols), BF16)
    b_give, b_keep, second_grad, outer_grad, sums_a = call(
        outer_grad_kernel,
        [b_shape, b_shape, ((own, width), F32), ((own, width), BF16), ((8, width), F32)],
        [place, cot_keep, cot_other, second_normed, second_inverse, vec, active],
        name="outer_grad",
    )
    from_out = swap(second_out[rows:], BIT_ZH)
    b_all = parts_sum(b_keep, turn(swap(b_give, BIT_C)))
    from_bx1, from_by1 = first_hop(b_all)
    outer_grad = tie(outer_grad, b_all[1])
    results = call(
        middle_kernel,
        [
            ((own, hidden), BF16), ((own, width), F32), ((own, width), BF16), ((own, cut), BF16),
            ((own, cut), BF16), ((2, own, cut), BF16), ((8, width), F32), ((8, hidden), F32),
        ],
        [place, outer_grad, slope, second_grad, normed, inverse, vec, *a_pieces, *b_pieces],
        ["vmem"] * 6 + ["hbm"] * 16,
        whole,
        flops=4 * own * width * hidden,
        traffic=6 * width * hidden,
        name="middle",
    )
    inner_grad, first_grad, attended_grad, dc_own, dc_zl, dc_give, sums_c, sums_b = results
    inner_grad = turn(inner_grad)
    got_x, got_y = turn(from_bx1), turn(from_by1)
    b_owns, from_by2, from_bx2 = second_hop(b_all, got_x, got_y)
    dc_c = turn(swap(dc_give, BIT_C))
    outputs = to_place(second_out[:rows], turn(from_out))
    from_dczl = swap(jnp.stack([dc_zl, dc_c[1]]), BIT_ZL)
    a_give, a_keep = call(
        inner_grad_kernel,
        [a_shape, a_shape],
        [place, tie(first_low, dc_c), inner_grad, attended_grad, *context],
        scratch=[pltpu.VMEM((width, own), BF16), pltpu.VMEM((4, own, cut), BF16)],
        name="inner_grad",
    )
    b_own = last_hop(b_owns, turn(from_by2), turn(from_bx2))
    dc_far = turn(from_dczl)
    from_agive = swap(turn(a_give), BIT_C)
    from_bzh = swap(b_own[2:], BIT_ZH, a_give)
    a_all = parts_sum(a_keep, turn(from_agive))
    from_ax1, from_ay1 = first_hop(a_all)
    dc = [tie(dc_own, a_all[1]), dc_far, dc_c]
    grads, sums_d = call(
        attend_back_kernel,
        [((total, wide), BF16), ((8, wide), F32)],
        [place, qkv, context_wide, rows_saved, *dc],
        ["hbm"] * 3 + ["vmem"] * 3,
        scratch=[pltpu.VMEM(*shape) for shape in saved]
        + [
            pltpu.VMEM((HEAD, total), F32),
            pltpu.VMEM((8, total), F32),
            pltpu.VMEM((total, cut), BF16),
            pltpu.VMEM((total, 128), F32),
            pltpu.SemaphoreType.DMA((3,)),
        ],
        name="attend_back",
    )
    grads = turn(grads)
    got_x, got_y = turn(from_ax1), turn(from_ay1)
    a_owns, from_ay2, from_ax2 = second_hop(a_all, got_x, got_y)
    grads = tie(grads, got_y)
    results = call(
        attend_weight_kernel,
        [((4, 2, 4, shard, wide), BF16), ((own, width), F32), ((own, width), BF16), ((2, own, width), BF16)],
        [place, *w_attend, x_own, x_other, grads, sums_d, sums_a, sums_b, sums_c],
        ["hbm"] * 6 + ["vmem"] * 5,
        scratch=[pltpu.VMEM((width, total), BF16)]
        + head_scratch
        + [pltpu.VMEM((width, 128), F32), pltpu.VMEM((hidden, 128), F32), pltpu.SemaphoreType.DMA((24,))],
        name="attend_weight",
    )
    q_all, x_part, x_zl, x_give = results
    a_own = last_hop(a_owns, turn(from_ay2), turn(from_ax2))
    a_halves = zl_halves(a_own[2:])
    from_az1 = swap(jnp.concatenate([a_halves[1][1:], a_halves[1][:1]]), BIT_ZL)
    from_xgive = swap(turn(x_give), BIT_C)
    from_qx1, from_qy1 = first_hop(q_all, a_own)
    b_own = add_low(b_own[:2], turn(from_bzh))
    a_far = add_low(a_halves[0], turn(from_az1))
    from_az2 = swap(a_far, BIT_ZH)
    got = turn(from_xgive)
    x_zl = add_low(x_zl, got[1])
    x_part = x_part + got[0].astype(F32)
    from_xzl = swap(x_zl, BIT_ZL)
    got_x, got_y = turn(from_qx1), turn(from_qy1)
    q_owns, from_qy2, from_qx2 = second_hop(q_all, got_x, got_y)

    def core_halves(array, axis):
        half = array.shape[axis] // 2
        first_half = lax.slice_in_dim(array, 0, half, axis=axis)
        last_half = lax.slice_in_dim(array, half, 2 * half, axis=axis)
        return jnp.where(c == 0, first_half, last_half), jnp.where(c == 0, last_half, first_half)

    x_far = turn(from_xzl)
    x_grad = first_grad + (x_part + x_far.astype(F32))
    from_xzh = swap(low(x_grad[rows:]), BIT_ZH)
    from_bzl = swap(b_own[1], BIT_ZL, x_far)
    got = turn(from_az2)
    empty = jnp.zeros_like(got)
    a_own = add_low(a_own[:2], join(zl, got, empty, 1))
    from_azl = swap(a_own[1], BIT_ZL)
    q_own = last_hop(q_owns, turn(from_qy2), turn(from_qx2))
    from_qzh = swap(q_own[2:], BIT_ZH)
    b_mine, b_theirs = core_halves(b_own[0].astype(F32) + turn(from_bzl).astype(F32), 0)
    from_bc = swap(low(b_theirs), BIT_C)
    q_own = add_low(q_own[:2], turn(from_qzh))
    from_qzl = swap(q_own[1], BIT_ZL)
    outer_owned = join(c, b_mine, turn(from_bc).astype(F32), 1)
    a_last = (a_own[0].astype(F32) + turn(from_azl).astype(F32)).reshape(5, unit, cols)
    a_mine, a_theirs = core_halves(a_last, 1)
    from_ac = swap(low(a_theirs), BIT_C)
    q_two = jnp.stack([q_own[0], turn(from_qzl)])
    q_mine, q_theirs = core_halves(q_two, 1)
    from_qc = swap(q_theirs, BIT_C)
    input_grad = to_place(x_grad[:rows], turn(from_xzh))
    a_got = turn(from_ac)
    q_got = turn(from_qc)
    results = call(
        last_kernel,
        [((shard, width), F32)] * 4 + [((shard, hidden), F32), ((16, 128), F32)],
        [place, q_mine, q_got, a_mine, a_got],
        scratch=[
            pltpu.VMEM((3, shard, width), F32),
            pltpu.VMEM((shard, width), F32),
            pltpu.VMEM((shard, hidden), F32),
            pltpu.SemaphoreType.DMA((5,)),
        ],
        out_spaces=["hbm"] * 5 + ["vmem"],
        name="last",
    )
    query_owned, key_owned, value_owned, output_owned, inner_owned, owned = results
    owned = owned[:12, :shard]
    return (
        outputs,
        input_grad,
        query_owned,
        key_owned,
        value_owned,
        output_owned,
        owned[0],
        owned[1],
        owned[2],
        owned[3],
        owned[4],
        inner_owned,
        owned[8:12].reshape(-1),
        outer_owned,
        owned[5],
        owned[6],
        owned[7],
    )


def solution(mesh):
    fast = mesh.shape["dp"] == 4 and mesh.shape["sp"] == 8
    body = body_fast if fast else body_general
    in_specs = (
        P(None, "dp", "sp", None),
        P(None, "dp", "sp"),
        P(None, "dp", "sp", None),
        P(("dp", "sp"), None),
        P(("dp", "sp"), None),
        P(("dp", "sp"), None),
        P(("dp", "sp"), None),
        P(("dp", "sp")),
        P(("dp", "sp")),
        P(("dp", "sp")),
        P(("dp", "sp")),
        P(("dp", "sp")),
        P(("dp", "sp"), None),
        P(("dp", "sp")),
        P(("dp", "sp"), None),
        P(("dp", "sp")),
        P(("dp", "sp")),
        P(("dp", "sp")),
    )
    out_specs = (
        P(None, "dp", "sp", None),
        P(None, "dp", "sp", None),
        P(("dp", "sp"), None),
        P(("dp", "sp"), None),
        P(("dp", "sp"), None),
        P(("dp", "sp"), None),
        P(("dp", "sp")),
        P(("dp", "sp")),
        P(("dp", "sp")),
        P(("dp", "sp")),
        P(("dp", "sp")),
        P(("dp", "sp"), None),
        P(("dp", "sp")),
        P(("dp", "sp"), None),
        P(("dp", "sp")),
        P(("dp", "sp")),
        P(("dp", "sp")),
    )
    return jax.shard_map(body, mesh=mesh, in_specs=in_specs, out_specs=out_specs, check_vma=False)
```

```python
import functools

import jax
import jax.numpy as jnp
from jax import lax
from jax.experimental import pallas as pl
from jax.experimental.pallas import tpu as pltpu
from jax.sharding import PartitionSpec as P

HEADS = 12
HEAD = 64


EPS = 1e-12
NEG = -1e30


def product(left_matrix, right_matrix):
    return jnp.dot(left_matrix, right_matrix, preferred_element_type=jnp.float32)


def left_product(left_matrix, right_matrix):
    return lax.dot_general(
        left_matrix, right_matrix, (((0,), (0,)), ((), ())), preferred_element_type=jnp.float32
    )


def right_product(left_matrix, right_matrix):
    return lax.dot_general(
        left_matrix, right_matrix, (((1,), (1,)), ((), ())), preferred_element_type=jnp.float32
    )


def by_heads(matrix):
    return matrix.reshape(matrix.shape[0], HEADS, HEAD)


def norm_forward(summed, gain, shift):
    center = summed - jnp.mean(summed, -1, keepdims=True)
    inverse = lax.rsqrt(jnp.mean(center * center, -1, keepdims=True) + EPS)
    normed = center * inverse
    return (normed * gain + shift, normed, inverse)


def norm_backward(gradient, normed, inverse, gain):
    scaled = gradient * gain
    plain_mean = jnp.mean(scaled, -1, keepdims=True)
    cross_mean = jnp.mean(scaled * normed, -1, keepdims=True)
    return (
        (scaled - plain_mean - normed * cross_mean) * inverse,
        jnp.sum(gradient * normed, 0),
        jnp.sum(gradient, 0),
    )


def attend_forward(queries, key_rows, value_rows, seg_local, seg_all):
    row_count = queries.shape[0]
    scaling = HEAD ** (-0.5)
    query_heads = by_heads(queries)
    key_piece = lax.all_gather(key_rows, "sp", axis=0, tiled=True)
    value_piece = lax.all_gather(value_rows, "sp", axis=0, tiled=True)
    row_peak = jnp.full((HEADS, row_count), NEG, jnp.float32)
    same_doc = (seg_local[:, None] == seg_all[None, :])[None]
    scores = (
        jnp.einsum(
            "qhd,khd->hqk", query_heads, by_heads(key_piece), preferred_element_type=jnp.float32
        )
        * scaling
    )
    scores = jnp.where(same_doc, scores, NEG)
    new_peak = jnp.maximum(row_peak, jnp.max(scores, -1))
    weights = jnp.where(same_doc, jnp.exp(scores - new_peak[..., None]), 0.0)
    row_total = jnp.sum(weights, -1)
    summed = jnp.einsum(
        "hqk,khd->hqd",
        weights.astype(jnp.bfloat16),
        by_heads(value_piece),
        preferred_element_type=jnp.float32,
    )
    return (new_peak, row_total, summed)


def keys_backward(
    queries, key_rows, value_rows, context_grad, log_total, row_delta, seg_local, seg_all
):
    row_count, width = queries.shape
    scaling = HEAD ** (-0.5)
    query_heads = by_heads(queries)
    grad_heads = by_heads(context_grad)
    key_piece = lax.all_gather(key_rows, "sp", axis=0, tiled=True)
    value_piece = lax.all_gather(value_rows, "sp", axis=0, tiled=True)
    piece_rows = key_piece.shape[0]
    key_heads = by_heads(key_piece)
    same_doc = (seg_local[:, None] == seg_all[None, :])[None]
    scores = (
        jnp.einsum("qhd,khd->hqk", query_heads, key_heads, preferred_element_type=jnp.float32)
        * scaling
    )
    weights = jnp.where(same_doc, jnp.exp(scores - log_total[..., None]), 0.0)
    prob_grad = jnp.einsum(
        "qhd,khd->hqk", grad_heads, by_heads(value_piece), preferred_element_type=jnp.float32
    )
    score_grad = (weights * (prob_grad - row_delta[..., None])).astype(jnp.bfloat16)
    query_sum = jnp.einsum(
        "hqk,khd->hqd", score_grad, key_heads, preferred_element_type=jnp.float32
    )
    key_term = jnp.einsum(
        "hqk,qhd->khd", score_grad, query_heads, preferred_element_type=jnp.float32
    ).reshape(piece_rows, width)
    value_term = jnp.einsum(
        "hqk,qhd->khd", weights.astype(jnp.bfloat16), grad_heads, preferred_element_type=jnp.float32
    ).reshape(piece_rows, width)
    pair_sum = jnp.concatenate([key_term, value_term], 1)
    query_sum, pair_sum = (query_sum, pair_sum)
    pair_mine = lax.psum_scatter(pair_sum, "sp", scatter_dimension=0, tiled=True)
    query_sum = jnp.transpose(query_sum, (1, 0, 2)).reshape(row_count, width)
    return (query_sum, pair_mine[:, :width], pair_mine[:, width:])


def body_general(
    tokens,
    doc_ids,
    cotangent,
    query_weight,
    key_weight,
    value_weight,
    output_weight,
    query_bias,
    value_bias,
    output_bias,
    first_gain,
    first_shift,
    inner_weight,
    inner_bias,
    outer_weight,
    outer_bias,
    second_gain,
    second_shift,
):
    shards = (
        query_weight,
        key_weight,
        value_weight,
        output_weight,
        query_bias,
        value_bias,
        output_bias,
        first_gain,
        first_shift,
        inner_weight,
        inner_bias,
        outer_weight,
        outer_bias,
        second_gain,
        second_shift,
    )
    scaling = HEAD ** (-0.5)
    results = []
    input_grads = []
    totals = ()
    for micro in range(tokens.shape[0]):
        loaded = (
            lax.all_gather(shards[0], ("dp", "sp"), axis=0, tiled=True),
            lax.all_gather(shards[1], ("dp", "sp"), axis=0, tiled=True),
            lax.all_gather(shards[2], ("dp", "sp"), axis=0, tiled=True),
            lax.all_gather(shards[3], ("dp", "sp"), axis=0, tiled=True),
            lax.all_gather(shards[4], ("dp", "sp"), axis=0, tiled=True),
            lax.all_gather(shards[5], ("dp", "sp"), axis=0, tiled=True),
            lax.all_gather(shards[6], ("dp", "sp"), axis=0, tiled=True),
            lax.all_gather(shards[7], ("dp", "sp"), axis=0, tiled=True),
            lax.all_gather(shards[8], ("dp", "sp"), axis=0, tiled=True),
            lax.all_gather(shards[9], ("dp", "sp"), axis=0, tiled=True),
            lax.all_gather(shards[10], ("dp", "sp"), axis=0, tiled=True),
            lax.all_gather(shards[11], ("dp", "sp"), axis=0, tiled=True),
            lax.all_gather(shards[12], ("dp", "sp"), axis=0, tiled=True),
            lax.all_gather(shards[13], ("dp", "sp"), axis=0, tiled=True),
            lax.all_gather(shards[14], ("dp", "sp"), axis=0, tiled=True),
        )
        (
            w_query,
            w_key,
            w_value,
            w_output,
            b_query,
            b_value,
            b_output,
            g_first,
            s_first,
            w_inner,
            b_inner,
            w_outer,
            b_outer,
            g_second,
            s_second,
        ) = loaded
        inputs = tokens[micro, 0]
        seg_local = doc_ids[micro, 0]
        seg_all = lax.all_gather(seg_local, "sp", axis=0, tiled=True)
        row_count, width = inputs.shape
        queries = (product(inputs, w_query) + b_query).astype(jnp.bfloat16)
        key_rows = product(inputs, w_key).astype(jnp.bfloat16)
        value_rows = (product(inputs, w_value) + b_value).astype(jnp.bfloat16)
        row_peak, row_total, summed = attend_forward(
            queries, key_rows, value_rows, seg_local, seg_all
        )
        context_heads = summed / row_total[..., None]
        log_total = row_peak + jnp.log(row_total)
        context_low = (
            jnp.transpose(context_heads, (1, 0, 2)).reshape(row_count, width).astype(jnp.bfloat16)
        )
        attended = product(context_low, w_output) + b_output
        first_out, first_normed, first_inverse = norm_forward(
            inputs.astype(jnp.float32) + attended, g_first, s_first
        )
        first_low = first_out.astype(jnp.bfloat16)
        inner = product(first_low, w_inner) + b_inner
        active = jax.nn.gelu(inner, approximate=False).astype(jnp.bfloat16)
        outer = product(active, w_outer) + b_outer
        second_out, second_normed, second_inverse = norm_forward(
            first_out + outer, g_second, s_second
        )
        results.append(second_out.astype(jnp.bfloat16))
        loaded = (
            lax.all_gather(shards[0], ("dp", "sp"), axis=0, tiled=True),
            lax.all_gather(shards[1], ("dp", "sp"), axis=0, tiled=True),
            lax.all_gather(shards[2], ("dp", "sp"), axis=0, tiled=True),
            lax.all_gather(shards[3], ("dp", "sp"), axis=0, tiled=True),
            lax.all_gather(shards[4], ("dp", "sp"), axis=0, tiled=True),
            lax.all_gather(shards[5], ("dp", "sp"), axis=0, tiled=True),
            lax.all_gather(shards[6], ("dp", "sp"), axis=0, tiled=True),
            lax.all_gather(shards[7], ("dp", "sp"), axis=0, tiled=True),
            lax.all_gather(shards[8], ("dp", "sp"), axis=0, tiled=True),
            lax.all_gather(shards[9], ("dp", "sp"), axis=0, tiled=True),
            lax.all_gather(shards[10], ("dp", "sp"), axis=0, tiled=True),
            lax.all_gather(shards[11], ("dp", "sp"), axis=0, tiled=True),
            lax.all_gather(shards[12], ("dp", "sp"), axis=0, tiled=True),
            lax.all_gather(shards[13], ("dp", "sp"), axis=0, tiled=True),
            lax.all_gather(shards[14], ("dp", "sp"), axis=0, tiled=True),
        )
        (
            w_query,
            w_key,
            w_value,
            w_output,
            b_query,
            b_value,
            b_output,
            g_first,
            s_first,
            w_inner,
            b_inner,
            w_outer,
            b_outer,
            g_second,
            s_second,
        ) = loaded
        upstream = cotangent[micro, 0].astype(jnp.float32)
        second_grad, second_gain_grad, second_shift_grad = norm_backward(
            upstream, second_normed, second_inverse, g_second
        )
        outer_grad = second_grad.astype(jnp.bfloat16)
        outer_bias_grad = jnp.sum(outer_grad.astype(jnp.float32), 0)
        outer_weight_grad = left_product(active, outer_grad)
        active_grad = right_product(outer_grad, w_outer)
        _, gelu_pull = jax.vjp(lambda hidden: jax.nn.gelu(hidden, approximate=False), inner)
        inner_grad = gelu_pull(active_grad)[0].astype(jnp.bfloat16)
        inner_bias_grad = jnp.sum(inner_grad.astype(jnp.float32), 0)
        inner_weight_grad = left_product(first_low, inner_grad)
        first_incoming = second_grad + right_product(inner_grad, w_inner)
        first_grad, first_gain_grad, first_shift_grad = norm_backward(
            first_incoming, first_normed, first_inverse, g_first
        )
        attended_grad = first_grad.astype(jnp.bfloat16)
        output_bias_grad = jnp.sum(attended_grad.astype(jnp.float32), 0)
        output_weight_grad = left_product(context_low, attended_grad)
        context_grad = right_product(attended_grad, w_output).astype(jnp.bfloat16)
        row_delta = jnp.sum(jnp.transpose(by_heads(context_grad), (1, 0, 2)) * context_heads, -1)
        query_sum, key_sum, value_sum = keys_backward(
            queries, key_rows, value_rows, context_grad, log_total, row_delta, seg_local, seg_all
        )
        query_grad = (query_sum * scaling).astype(jnp.bfloat16)
        key_grad = (key_sum * scaling).astype(jnp.bfloat16)
        value_grad = value_sum.astype(jnp.bfloat16)
        query_bias_grad = jnp.sum(query_grad.astype(jnp.float32), 0)
        value_bias_grad = jnp.sum(value_grad.astype(jnp.float32), 0)
        query_weight_grad = left_product(inputs, query_grad)
        key_weight_grad = left_product(inputs, key_grad)
        value_weight_grad = left_product(inputs, value_grad)
        input_grads.append(
            first_grad
            + right_product(query_grad, w_query)
            + right_product(key_grad, w_key)
            + right_product(value_grad, w_value)
        )
        terms = (
            query_weight_grad,
            key_weight_grad,
            value_weight_grad,
            output_weight_grad,
            query_bias_grad,
            value_bias_grad,
            output_bias_grad,
            first_gain_grad,
            first_shift_grad,
            inner_weight_grad,
            inner_bias_grad,
            outer_weight_grad,
            outer_bias_grad,
            second_gain_grad,
            second_shift_grad,
        )
        if micro == 0:
            totals = terms
        else:
            totals = tuple((earlier + latest for earlier, latest in zip(totals, terms)))
    owned = lax.psum_scatter(totals, ("dp", "sp"), scatter_dimension=0, tiled=True)
    return (
        jnp.stack(results)[:, None],
        jnp.stack(input_grads)[:, None],
        owned[0],
        owned[1],
        owned[2],
        owned[3],
        owned[4],
        owned[5],
        owned[6],
        owned[7],
        owned[8],
        owned[9],
        owned[10],
        owned[11],
        owned[12],
        owned[13],
        owned[14],
    )


BIT_Y, BIT_X, BIT_ZH, BIT_ZL, BIT_C = 16, 8, 4, 2, 1
AXES = ("dp", "sp")
GAUSS = 0.3989422804014327
LIMITS = {
    "first": 2, "query": 2, "last": 4, "attend": 24, "forward": 20, "outer_grad": 12, "middle": 20, "inner_grad": 12,
    "attend_back": 24, "attend_weight": 20,
}
SIDE = 64
SCALE = 0.0
DOC_ROWS = 16
BF16, F32 = jnp.bfloat16, jnp.float32


def low(array):
    return array.astype(BF16)


def swap(array, mask, after=None):
    if after is not None:
        array, _ = lax.optimization_barrier((array, after))
    return lax.ppermute(array, AXES, [(i, i ^ mask) for i in range(32)])


class Turns:
    def __init__(self):
        self.last = None

    def __call__(self, array):
        if self.last is not None:
            array, _ = lax.optimization_barrier((array, self.last))
        self.last = array
        return array


def tie(array, other):
    return lax.optimization_barrier((array, other))[0]


def join(bit, own, other, axis=0):
    return jnp.where(
        bit == 0, jnp.concatenate([own, other], axis), jnp.concatenate([other, own], axis)
    )


def pair(own, other):
    return jnp.concatenate([own, other], 0)


def add_low(own, other):
    return low(own.astype(F32) + other.astype(F32))


def call(kernel, outs, operands, spaces=None, scratch=(), flops=0, traffic=0, name=None, out_spaces=None):
    whole = pl.BlockSpec(memory_space=pltpu.VMEM)
    specs = [pl.BlockSpec(memory_space=pltpu.SMEM)]
    operands = list(operands)
    for n, kind in enumerate(spaces or ["vmem"] * (len(operands) - 1), 1):
        specs.append(whole if kind == "vmem" else pl.BlockSpec(memory_space=pltpu.HBM))
        if kind == "hbm":
            operands[n] = pltpu.with_memory_space_constraint(operands[n], pltpu.HBM)
    return pl.pallas_call(
        kernel,
        out_shape=tuple(jax.ShapeDtypeStruct(shape, dtype) for shape, dtype in outs),
        in_specs=specs,
        out_specs=tuple(
            whole if kind == "vmem" else pl.BlockSpec(memory_space=pltpu.HBM)
            for kind in (out_spaces or ["vmem"] * len(outs))
        ),
        scratch_shapes=list(scratch),
        compiler_params=pltpu.CompilerParams(vmem_limit_bytes=LIMITS[name] * 1024 * 1024),
        cost_estimate=pl.CostEstimate(flops=int(flops * SCALE) + 1, transcendentals=0, bytes_accessed=int(traffic * SCALE) + 1),
        name=name,
    )(*operands)


def block_at(place, k):
    return (place[0] ^ (k // 2)) * 2 + (place[1] ^ (k % 2))


def unit_at(place, u):
    return (place[2] ^ (u // 2)) * 2 + (place[3] ^ (u % 2))


def first_kernel(place, tokens, docs, inner, outer, output, x_keep, x_give, keep, give, ids, sems):
    zh, c = place[2], place[4]
    rows, width = tokens.shape[1:]
    shard, cols = keep.shape[1:]
    started = [pltpu.make_async_copy(docs, ids, sems.at[0])]
    for flip in range(2):
        x_out, out = (x_keep, x_give)[flip], (keep, give)[flip]
        moves = [(tokens.at[zh ^ flip], x_out.at[pl.ds(0, rows), :])]
        half = c ^ flip
        for j in range(4):
            at = pl.ds(pl.multiple_of(half * (4 * cols) + j * cols, 128), cols)
            moves.append((inner.at[:, at], out.at[j]))
        at = pl.ds(pl.multiple_of(half * cols, 128), cols)
        for j in range(4):
            moves.append((outer.at[pl.ds(shard * j, shard), at], out.at[4 + j]))
        moves.append((output.at[:, at], out.at[8]))
        for source, target in moves:
            started.append(pltpu.make_async_copy(source, target, sems.at[len(started)]))
    for copy in started:
        copy.start()
    for copy in started:
        copy.wait()
    for flip, out in ((0, x_keep), (1, x_give)):
        line = ids[pl.ds(zh ^ flip, 1), :].astype(F32)
        line = jnp.concatenate([line, jnp.zeros((1, width - rows), F32)], 1)
        out[rows : rows + DOC_ROWS, :] = low(jnp.broadcast_to(line, (DOC_ROWS, width)))


def query_kernel(place, wq, wk, wv, smalls, q_keep, q_give, weights, blocks, side, sems):
    zl, c = place[3], place[4]
    shard, width = wq.shape
    cut = width // 4
    started = [
        pltpu.make_async_copy(w, weights.at[n], sems.at[n]) for n, w in enumerate((wq, wk, wv))
    ]
    for copy in started:
        copy.start()
    side[...] = jnp.zeros_like(side)
    side[SIDE : SIDE + 16, :] = smalls[...]
    columns = low(jnp.transpose(side[...]))[:shard, SIDE:]
    for copy in started:
        copy.wait()
    for p in range(4):
        at = slice(cut * p, cut * (p + 1))
        blocks[p] = jnp.concatenate([weights[0, :, at], weights[1, :, at], weights[2, :, at], columns], 1)
    for r in range(2):
        q_keep[r] = blocks[2 * (zl ^ r) + c]
        q_give[r] = blocks[2 * (zl ^ r) + (1 - c)]


PARTS = (((2, 0), (3, 0)), ((0, 0), (3, 1)), ((2, 1), (1, 0)), ((0, 1), (1, 1)))


def put_rows(outs, k, u, start, value):
    half = outs[0].shape[3]
    stop = start + value.shape[0]
    if start < half:
        part, n = PARTS[k][0]
        out = outs[part // 2]
        out[part % 2, n, u, start : min(stop, half), :] = value[: min(stop, half) - start, :]
    if stop > half:
        part, n = PARTS[k][1]
        out = outs[part // 2]
        first = max(start, half)
        out[part % 2, n, u, first - half : stop - half, :] = value[first - start :, :]


def head_copies(pieces, place, w, sems, base):
    size = pieces[0].shape[1]
    started = []
    for k, part in enumerate(pieces):
        for u in range(4):
            at = block_at(place, k) * (4 * size) + unit_at(place, u) * size
            target = w.at[pl.ds(pl.multiple_of(at, 16), size), :]
            started.append(pltpu.make_async_copy(part.at[u], target, sems.at[base + len(started)]))
    return started


def attend_kernel(place, w0, w1, w2, w3, x_own, x_other, *refs):
    context_out, (qkv, wide, rows_of, vec_out) = refs[:2], refs[2:6]
    w, doc_col = refs[6:]
    size = w0.shape[1]
    for k, part in enumerate((w0, w1, w2, w3)):
        for u in range(4):
            at = block_at(place, k) * (4 * size) + unit_at(place, u) * size
            w[pl.ds(pl.multiple_of(at, 16), size), :] = part[u]
    cut = qkv.shape[2]
    heads = cut // HEAD
    group = place[5]
    tile = slice(3 * cut - SIDE, 3 * cut + SIDE)
    vec_out[...] = jnp.transpose(w[:, tile].astype(F32))[SIDE : SIDE + 16, :]
    biases = w[pl.ds(pl.multiple_of(group * cut, 64), cut), tile].astype(F32)
    biases = jnp.transpose(jnp.concatenate([biases, jnp.zeros((64, 2 * SIDE), F32)], 0))
    bq, bv = biases[SIDE : SIDE + 1, :cut], biases[SIDE + 1 : SIDE + 2, :cut]
    rows = x_own.shape[1] - DOC_ROWS
    ids = []
    for n in range(8):
        source = (x_own, x_other)[n // 4]
        part = product(source[n % 4, 0:rows, :], w[:, : 3 * cut])
        at = pl.ds(rows * n, rows)
        qkv[0, at, :] = low(part[:, :cut] + bq)
        qkv[1, at, :] = low(part[:, cut : 2 * cut])
        qkv[2, at, :] = low(part[:, 2 * cut :] + bv)
        ids.append(source[n % 4, rows : rows + 1, 0:128].astype(F32))
    doc_row = jnp.concatenate(ids, 1)
    rows_of[8:16, :] = jnp.broadcast_to(doc_row, (8, doc_row.shape[1]))
    turned = jnp.transpose(jnp.concatenate(ids + [jnp.zeros((120, 128), F32)], 0))
    for n in range(8):
        doc_col[pl.ds(rows * n, rows), :] = jnp.broadcast_to(turned[:, n : n + 1], (rows, 128))
    rows = 2 * rows
    lane = lax.broadcasted_iota(jnp.int32, (rows, 128), 1)
    for i in (2, 3, 0, 1):
        at = pl.ds(rows * i, rows)
        same = doc_col[at, 0:1] == doc_row
        pieces = []
        logs = jnp.zeros((rows, 128), F32)
        for h in range(heads):
            cols = slice(HEAD * h, HEAD * (h + 1))
            query = qkv[0, at, cols] * BF16(HEAD**-0.5)
            scores = right_product(query, qkv[1, :, cols])
            scores = jnp.where(same, scores, NEG)
            peak = jnp.max(scores, -1, keepdims=True)
            weights = jnp.exp(scores - peak)
            denom = jnp.sum(weights, -1, keepdims=True)
            summed = product(low(weights), qkv[2, :, cols])
            pieces.append(summed / denom)
            logs = jnp.where(lane == h, peak + jnp.log(denom), logs)
        context = jnp.concatenate(pieces, 1)
        wide[at, :] = context
        context_out[i // 2][i % 2] = low(context)
        rows_of[0:8, at] = jnp.transpose(logs)[:8, :]


def attend_back_kernel(
    place, qkv_in, wide_in, rows_in, w0, w1, w2, w3, g_own, g_zl, g_c, grads, sums, x_part, x_zl, x_give,
    qkv, wide, rows_of, dq_acc, delta_ref, dc, doc_col, w, sems
):
    copies_in = [
        pltpu.make_async_copy(source, target, sems.at[n])
        for n, (source, target) in enumerate(((qkv_in, qkv), (wide_in, wide), (rows_in, rows_of)))
    ]
    weight_copies = head_copies((w0, w1, w2, w3), place, w, sems, 3)
    for copy in copies_in + weight_copies:
        copy.start()
    for copy in copies_in:
        copy.wait()
    total, cut = wide.shape
    heads = cut // HEAD
    rows = total // 4
    scaling = HEAD**-0.5
    lane = lax.broadcasted_iota(jnp.int32, (rows, 128), 1)
    doc_row = rows_of[8:9, :]
    for n in range(total // 128):
        at = slice(128 * n, 128 * (n + 1))
        doc_col[at, :] = jnp.transpose(jnp.broadcast_to(rows_of[8:9, at], (128, 128)))
    for i in range(4):
        at = pl.ds(rows * i, rows)
        grad = (g_own[...], g_zl[0], g_c[0], g_zl[1])[i]
        dc[at, :] = grad
        prod = grad.astype(F32) * wide[at, :]
        cols = jnp.zeros((rows, 128), F32)
        for h in range(heads):
            piece = jnp.sum(prod[:, HEAD * h : HEAD * (h + 1)], -1, keepdims=True)
            cols = jnp.where(lane == h, piece, cols)
        delta_ref[:, at] = jnp.transpose(cols)[:8, :]
    for h in range(heads):
        cols = slice(HEAD * h, HEAD * (h + 1))
        query = qkv[0, :, cols]
        scaled = query * BF16(scaling)
        grad_rows = dc[:, cols]
        for i in range(4):
            at = pl.ds(rows * i, rows)
            key = qkv[1, at, cols]
            value = qkv[2, at, cols]
            same = doc_col[at, 0:1] == doc_row
            scores = jnp.where(same, right_product(key, scaled), NEG)
            probs = jnp.exp(scores - rows_of[h : h + 1, :])
            prob_grad = right_product(value, grad_rows)
            score_grad = low(probs * (prob_grad - delta_ref[h : h + 1, :]))
            grads[at, cut + HEAD * h : cut + HEAD * (h + 1)] = low(product(score_grad, query) * scaling)
            grads[at, 2 * cut + HEAD * h : 2 * cut + HEAD * (h + 1)] = low(product(low(probs), grad_rows))
            piece = left_product(key, score_grad)
            if i == 0:
                dq_acc[...] = piece
            else:
                dq_acc[...] += piece
        grads[:, cols] = low(jnp.transpose(dq_acc[...]) * scaling)
    grads[:, 3 * cut :] = jnp.zeros((total, SIDE), BF16)
    for copy in weight_copies:
        copy.wait()
    for n in (2, 3, 1, 0):
        at = pl.ds(rows * n, rows)
        part = right_product(grads[at, : 3 * cut], w[:, : 3 * cut])
        if n == 0:
            x_part[...] = part
        elif n == 1:
            x_zl[...] = low(part)
        else:
            x_give[n - 2] = low(part)
    sums[0:1, :] = jnp.sum(grads[...].astype(F32), 0, keepdims=True)


def attend_weight_kernel(
    place, x_own, x_other, grads, sums, sums_a, sums_b, sums_c, *refs
):
    outs, (turned, x, side, tall, sems) = refs[:2], refs[2:]
    copies_in = [
        pltpu.make_async_copy(part, x.at[n], sems.at[n]) for n, part in enumerate((x_own, x_other))
    ]
    for copy in copies_in:
        copy.start()
    rows = x.shape[2] - DOC_ROWS
    group = place[5]
    width = sums_a.shape[1]
    cut = width // 4
    early = jnp.concatenate([sums_c[2:3, :], sums_c[0:2, :], sums_a[2:3, :], sums_a[0:2, :]], 0)
    pad = jnp.concatenate(
        [jnp.zeros((SIDE + 2, width), F32), early, jnp.zeros((SIDE - 8, width), F32)], 0
    )
    side[...] = jnp.transpose(pad)
    own = jnp.concatenate([sums[0:1, :cut], sums[0:1, 2 * cut : 3 * cut]], 0)
    own = jnp.concatenate([own, jnp.zeros((2, 256 - cut), F32)], 1)
    own = jnp.concatenate([jnp.zeros((SIDE, 256), F32), own, jnp.zeros((SIDE - 2, 256), F32)], 0)
    at = pl.ds(pl.multiple_of(group * cut, 64), cut)
    side[at, :] += jnp.transpose(own)[:cut, :]
    tall[...] = jnp.transpose(jnp.broadcast_to(sums_b[0:1, :], (128, sums_b.shape[1])))
    shard = width // 32
    lane = lax.broadcasted_iota(jnp.int32, (shard, 128), 1)
    for n in range(32):
        at = slice(shard * n, shard * (n + 1))
        value = side[at, :]
        for q in range(4):
            start = 4 * shard * n + shard * q
            value = jnp.where(lane == SIDE + 8 + q, tall[start : start + shard, :], value)
        side[at, :] = value
    for copy in copies_in:
        copy.wait()
    for n in range(8):
        turned[:, pl.ds(rows * n, rows)] = jnp.transpose(x[n // 4, n % 4, 0:rows, :])
    size = 2 * outs[0].shape[3]
    for k in range(4):
        at = pl.ds(pl.multiple_of(block_at(place, k) * (4 * size), 64), 4 * size)
        piece = product(turned[at, :], grads[...])
        piece = jnp.concatenate([piece[:, : 3 * cut - SIDE], piece[:, 3 * cut - SIDE :] + side[at, :]], 1)
        for a in range(4):
            put_rows(outs, k, unit_at(place, a), 0, low(piece[size * a : size * (a + 1), :]))


def last_kernel(place, q_mine, q_got, a_mine, a_got, wq, wk, wv, wo, wi, small, buf_q, buf_o, buf_i, sems):
    zl, c = place[3], place[4]
    shard, width = wq.shape
    cut = width // 4
    parts = [q_mine[0].astype(F32), q_got[0].astype(F32), q_mine[1].astype(F32), q_got[1].astype(F32)]

    def ordered(bit, own, other):
        return jnp.concatenate([jnp.where(bit == 0, own, other), jnp.where(bit == 0, other, own)], 1)

    for n in range(3):
        cols = [part[:, cut * n : cut * (n + 1)] for part in parts]
        near, far = ordered(c, cols[0], cols[1]), ordered(c, cols[2], cols[3])
        buf_q[n] = ordered(zl, near, far)
    started = [pltpu.make_async_copy(buf_q.at[n], out, sems.at[n]) for n, out in enumerate((wq, wk, wv))]
    mine = [a_mine[j] for j in range(5)]
    theirs = [a_got[j].astype(F32) for j in range(5)]
    buf_o[...] = ordered(c, mine[4], theirs[4])
    buf_i[...] = ordered(c, jnp.concatenate(mine[:4], 1), jnp.concatenate(theirs[:4], 1))
    started += [pltpu.make_async_copy(buf_o, wo, sems.at[3]), pltpu.make_async_copy(buf_i, wi, sems.at[4])]
    for copy in started:
        copy.start()
    tile = slice(3 * cut - SIDE, 3 * cut + SIDE)
    total = (parts[0][:, tile] + parts[1][:, tile]) + (parts[2][:, tile] + parts[3][:, tile])
    total = jnp.concatenate([total, jnp.zeros((128 - shard, 2 * SIDE), F32)], 0)
    small[...] = jnp.transpose(total)[SIDE : SIDE + 16, :]
    for copy in started:
        copy.wait()


def copies(pieces, whole, place, sems, base, column_blocks, first, row_count):
    c = place[4]
    started = []
    for half in range(2):
        for k in range(4):
            for u in range(4):
                for j in range(column_blocks):
                    source = pieces[half * 4 + k]
                    cols = source.shape[-1]
                    row = block_at(place, k) * (4 * row_count) + unit_at(place, u) * row_count
                    col = (c ^ half) * (column_blocks * cols) + j * cols
                    target = whole.at[
                        pl.ds(pl.multiple_of(row, 16), row_count), pl.ds(pl.multiple_of(col, 128), cols)
                    ]
                    if column_blocks > 1:
                        source = source.at[u, j]
                    else:
                        source = source.at[u, pl.ds(first, row_count), :]
                    started.append(pltpu.make_async_copy(source, target, sems.at[base + len(started)]))
    return started


def forward_kernel(place, c_own, c_c, c_zl, x_ref, vec, b_inner, *refs):
    a_p, b_p = refs[:8], refs[8:16]
    (out, n2_out, r2_out, h1b_out, n1_out, r1_out, g_out, gp_out) = refs[16:24]
    wo, wi, wu, sems = refs[24:]
    unit = wo.shape[0] // 16
    copy_o = copies(b_p, wo, place, sems, 0, 1, 4 * unit, unit)
    copy_i = copies(a_p, wi, place, sems, 32, 4, 0, unit)
    copy_u = copies(b_p, wu, place, sems, 160, 1, 0, 4 * unit)
    for copy in copy_o + copy_i + copy_u:
        copy.start()
    group = place[5]
    rows = x_ref.shape[1] - DOC_ROWS
    cut = c_own.shape[-1]
    for copy in copy_o:
        copy.wait()
    attended = vec[2:3, :]
    for mask in range(4):
        part = (c_own, c_c, c_zl, c_zl)[mask]
        at = pl.ds(pl.multiple_of((group ^ mask) * cut, 64), cut)
        attended = attended + product(part[mask // 3], wo[at, :])
    tokens = jnp.concatenate([x_ref[0, 0:rows, :], x_ref[1, 0:rows, :]], 0)
    first_out, normed, inverse = norm_forward(tokens.astype(F32) + attended, vec[3:4, :], vec[4:5, :])
    n1_out[...] = normed
    r1_out[...] = jnp.broadcast_to(inverse, r1_out.shape)
    h1b_out[...] = low(first_out)
    for copy in copy_i + copy_u:
        copy.wait()
    outer = vec[5:6, :]
    step = 512
    for j in range(wi.shape[1] // step):
        at = slice(step * j, step * (j + 1))
        hidden = product(h1b_out[...], wi[:, at]) + b_inner[:, at]
        half = 0.5 + 0.5 * lax.erf(hidden * (0.5**0.5))
        active = low(hidden * half)
        g_out[:, at] = active
        gp_out[:, at] = half + hidden * jnp.exp(hidden * hidden * -0.5) * GAUSS
        outer = outer + product(active, wu[at, :])
    second_out, normed, inverse = norm_forward(first_out + outer, vec[6:7, :], vec[7:8, :])
    out[...] = low(second_out)
    n2_out[...] = normed
    r2_out[...] = jnp.broadcast_to(inverse, r2_out.shape)


def outer_grad_kernel(
    place, cot_own, cot_other, n2, r2, vec, g_ref, give, give_rest, keep, keep_rest, dz2_out, df_ref, sums
):
    c = place[4]
    upstream = jnp.concatenate([cot_own[...], cot_other[...]], 0).astype(F32)
    grad, gain_grad, shift_grad = norm_backward(upstream, n2[...], r2[:, 0:1], vec[6:7, :])
    dz2_out[...] = grad
    grad_low = low(grad)
    df_ref[...] = grad_low
    sums[0:1, :] = gain_grad[None]
    sums[1:2, :] = shift_grad[None]
    sums[2:3, :] = jnp.sum(grad_low.astype(F32), 0, keepdims=True)
    unit, cols = 2 * give.shape[3], give.shape[4]
    give_part = df_ref[:, pl.ds(pl.multiple_of((1 - c) * cols, 128), cols)]
    keep_part = df_ref[:, pl.ds(pl.multiple_of(c * cols, 128), cols)]
    both = jnp.concatenate([give_part, keep_part], 1)
    for k in range(4):
        at = pl.ds(pl.multiple_of(block_at(place, k) * (4 * unit), 128), 4 * unit)
        piece = low(left_product(g_ref[:, at], both))
        for a in range(4):
            at = slice(unit * a, unit * (a + 1))
            put_rows((give, give_rest), k, unit_at(place, a), 0, piece[at, :cols])
            put_rows((keep, keep_rest), k, unit_at(place, a), 0, piece[at, cols:])


def middle_kernel(place, df_ref, gp_ref, dz2, n1, r1, vec, *refs):
    a_p, b_p = refs[:8], refs[8:16]
    du, grad_out, da, dc0, dc1, dc_give, sums, sums_b = refs[16:24]
    wo, wi, wu, sems = refs[24:]
    unit = wo.shape[0] // 16
    copy_o = copies(b_p, wo, place, sems, 0, 1, 4 * unit, unit)
    copy_i = copies(a_p, wi, place, sems, 32, 4, 0, unit)
    copy_u = copies(b_p, wu, place, sems, 160, 1, 0, 4 * unit)
    for copy in copy_u + copy_i + copy_o:
        copy.start()
    group = place[5]
    for copy in copy_u + copy_i:
        copy.wait()
    step = 512
    incoming = dz2[...]
    for j in range(wu.shape[0] // step):
        at = slice(step * j, step * (j + 1))
        grad = low(right_product(df_ref[...], wu[at, :]) * gp_ref[:, at])
        du[:, at] = grad
        sums_b[0:1, at] = jnp.sum(grad.astype(F32), 0, keepdims=True)
        incoming = incoming + right_product(grad, wi[:, at])
    for copy in copy_o:
        copy.wait()
    grad, gain_grad, shift_grad = norm_backward(incoming, n1[...], r1[:, 0:1], vec[3:4, :])
    grad_out[...] = grad
    grad_low = low(grad)
    da[...] = grad_low
    sums[0:1, :] = gain_grad[None]
    sums[1:2, :] = shift_grad[None]
    sums[2:3, :] = jnp.sum(grad_low.astype(F32), 0, keepdims=True)
    cut = dc0.shape[1]
    for mask in (1, 3, 0, 2):
        at = pl.ds(pl.multiple_of((group ^ mask) * cut, 64), cut)
        part = low(right_product(grad_low, wo[at, :]))
        if mask % 2:
            dc_give[mask // 2] = part
        else:
            (dc0, dc1)[mask // 2][...] = part


def inner_grad_kernel(place, h1b_ref, du, da, c_own, c_c, c_zl, give, give_rest, keep, keep_rest, turned, cs):
    c, group = place[4], place[5]
    turned[...] = jnp.transpose(h1b_ref[...])
    for mask in range(4):
        cs[mask] = (c_own, c_c, c_zl, c_zl)[mask][mask // 3]
    unit, cols = 2 * give.shape[3] // 5, give.shape[4]
    blocks = 5
    wide = (blocks - 1) * cols
    for half in range(2):
        side = c ^ 1 ^ half
        right = du[:, pl.ds(pl.multiple_of(side * wide, 128), wide)]
        right_low = da[:, pl.ds(pl.multiple_of(side * cols, 128), cols)]
        for k in range(4):
            block = block_at(place, k)
            at = pl.ds(pl.multiple_of(block * (4 * unit), 64), 4 * unit)
            piece = low(product(turned[at, :], right))
            tail = low(left_product(cs[block ^ group], right_low))
            for a in range(4):
                u = unit_at(place, a)
                rows = slice(unit * a, unit * (a + 1))
                for j in range(blocks):
                    part = piece[rows, cols * j : cols * (j + 1)] if j < blocks - 1 else tail[rows, :]
                    outs = (keep, keep_rest) if half else (give, give_rest)
                    put_rows(outs, k, u, unit * j, part)


def body_fast(
    tokens,
    doc_ids,
    cotangent,
    query_weight,
    key_weight,
    value_weight,
    output_weight,
    query_bias,
    value_bias,
    output_bias,
    first_gain,
    first_shift,
    inner_weight,
    inner_bias,
    outer_weight,
    outer_bias,
    second_gain,
    second_shift,
):
    dp, sp = lax.axis_index("dp"), lax.axis_index("sp")
    y, x, zh, zl, c = dp // 2, dp % 2, sp // 4, (sp // 2) % 2, sp % 2
    place = jnp.stack([y, x, zh, zl, c, sp % 4]).astype(jnp.int32)
    width, hidden, rows = tokens.shape[-1], inner_weight.shape[1], tokens.shape[2]
    cut, shard = width // 4, query_weight.shape[0]
    unit = 2 * shard
    wide = 3 * cut + SIDE
    own, total = 2 * rows, 8 * rows
    turn = Turns()

    x_rows = rows + DOC_ROWS
    cols = hidden // 8
    x_keep, x_give, w_keep, w_give = call(
        first_kernel,
        [((x_rows, width), BF16)] * 2 + [((9, shard, cols), BF16)] * 2,
        [place, tokens[:, 0], doc_ids[:, 0], inner_weight, outer_weight, output_weight],
        ["hbm"] * 5,
        scratch=[pltpu.VMEM((2, rows), jnp.int32), pltpu.SemaphoreType.DMA((24,))],
        name="first",
    )
    from_xzh = swap(x_give, BIT_ZH)
    got = turn(swap(w_give, BIT_C))

    def zl_half(array):
        half = array.shape[1] // 2
        return lax.dynamic_slice_in_dim(array, zl * half, half, 1)

    def far_pair(own_half, other_half):
        turned = pair(other_half[1:], other_half[:1])
        return join(zl, own_half, turned, 1)

    a_unit = join(c, w_keep[:4], got[:4], 1)
    b_unit = jnp.concatenate(
        [
            join(c, w_keep[4:8].reshape(4 * shard, cols), got[4:8].reshape(4 * shard, cols)),
            join(c, w_keep[8], got[8]),
        ]
    )
    from_a2 = swap(a_unit[None], BIT_ZL)

    a_pair = pair(a_unit[None], turn(from_a2))
    from_a4 = swap(zl_half(a_pair), BIT_ZH)
    from_b2 = swap(b_unit[None], BIT_ZL, a_pair)
    b_pair = pair(b_unit[None], turn(from_b2))
    a_half = turn(from_a4)
    from_a5 = swap(a_half, BIT_ZL)
    from_b4 = swap(zl_half(b_pair), BIT_ZH, a_half)

    smalls = [
        query_bias, value_bias, output_bias, first_gain, first_shift,
        outer_bias, second_gain, second_shift,
    ] + [inner_bias[shard * q : shard * (q + 1)] for q in range(4)]
    smalls = list(lax.optimization_barrier((*smalls, a_half))[:-1])
    row = lax.broadcasted_iota(jnp.int32, (16, 128), 0)
    packed = jnp.zeros((16, 128), F32)
    for n, small in enumerate(smalls):
        wide_small = jnp.pad(small.astype(F32), (0, 128 - shard))
        packed = jnp.where(row == n, wide_small[None], packed)
    q_keep, q_give = call(
        query_kernel,
        [((2, shard, wide), BF16)] * 2,
        [place, tie(query_weight, a_half), key_weight, value_weight, packed],
        ["hbm"] * 3 + ["vmem"],
        scratch=[
            pltpu.VMEM((3, shard, width), BF16),
            pltpu.VMEM((4, shard, wide), BF16),
            pltpu.VMEM((128, 128), F32),
            pltpu.SemaphoreType.DMA((3,)),
        ],
        name="query",
    )
    mine = jnp.stack([x_keep, turn(from_xzh)])
    a_own = pair(a_pair, far_pair(a_half, turn(from_a5)))
    from_ax = swap(a_own, BIT_X)
    from_ay = swap(a_own, BIT_Y)
    from_qc = swap(turn(q_give), BIT_C)
    b_half = turn(from_b4)
    from_b5 = swap(b_half, BIT_ZL)
    q_unit = join(c, q_keep, turn(from_qc), 1)
    from_qzl = swap(q_unit[1], BIT_ZL)
    q_pair = jnp.stack([q_unit[0], turn(from_qzl)])
    from_qzh = swap(q_pair, BIT_ZH)
    b_own = pair(b_pair, far_pair(b_half, turn(from_b5)))
    from_xzl = swap(mine, BIT_ZL, b_own)

    def halves_of(array, axis):
        half = array.shape[axis] // 2
        return (
            lax.slice_in_dim(array, 0, half, axis=axis),
            lax.slice_in_dim(array, half, 2 * half, axis=axis),
        )

    def corner_hop(over_x, over_y, axis):
        return (
            swap(halves_of(over_y, axis)[0], BIT_X),
            swap(halves_of(over_x, axis)[1], BIT_Y),
        )

    a_y = turn(from_ay)
    a_x = turn(from_ax)
    from_axy = corner_hop(a_x, a_y, 1)
    q_own = pair(q_pair, turn(from_qzh))
    from_qy = swap(q_own, BIT_Y, a_y)
    from_qx = swap(q_own, BIT_X, a_x)
    x_own = pair(mine, turn(from_xzl))
    from_xc = swap(x_own, BIT_C)
    q_y = turn(from_qy)
    q_x = turn(from_qx)
    a_xy = jnp.concatenate([turn(from_axy[0]), turn(from_axy[1])], 1)
    x_other = turn(from_xc)
    from_qxy = corner_hop(q_x, q_y, 0)
    from_a0c = swap(a_own, BIT_C, q_x)
    from_a1c = swap(a_x, BIT_C, q_x)
    q_xy = pair(turn(from_qxy[0]), turn(from_qxy[1]))
    from_bx = swap(b_own, BIT_X, q_xy)
    from_by = swap(b_own, BIT_Y, q_xy)
    a_c = [turn(from_a0c), turn(from_a1c)]
    w_attend = [q_own, q_x, q_y, q_xy]

    head_scratch = [pltpu.VMEM((width, wide), BF16), pltpu.VMEM((2, 4, x_rows, width), BF16)]
    saved = [((3, total, cut), BF16), ((total, cut), F32), ((16, total), F32)]
    results = call(
        attend_kernel,
        [((2, own, cut), BF16)] * 2 + saved + [((16, width), F32)],
        [place, *w_attend, x_own, tie(x_other, a_c[1])],
        scratch=[head_scratch[0], pltpu.VMEM((total, 128), F32)],
        name="attend",
    )
    context_keep, context_give, qkv, context_wide, rows_saved, vec = results
    from_cc = swap(turn(context_give), BIT_C)
    got = turn(from_cc)
    from_czl = swap(pair(context_keep[1:], got[1:]), BIT_ZL)
    context = [context_keep, got]
    b_y = turn(from_by)
    b_x = turn(from_bx)
    from_bxy = corner_hop(b_x, b_y, 1)
    from_a2c = swap(a_y, BIT_C, b_x)
    from_a3c = swap(a_xy, BIT_C, b_x)
    a_c.append(turn(from_a2c))
    a_c.append(turn(from_a3c))
    from_b0c = swap(b_own, BIT_C, a_c[3])
    from_b1c = swap(b_x, BIT_C, a_c[3])
    b_inner = jnp.transpose(tie(vec, got)[8:12].reshape(4, 32, shard), (1, 0, 2)).reshape(1, hidden)
    b_inner = turn(b_inner)
    cot_keep = lax.dynamic_index_in_dim(cotangent[:, 0], zh, 0, False)
    cot_give = turn(lax.dynamic_index_in_dim(cotangent[:, 0], 1 - zh, 0, False))
    from_cot = swap(cot_give, BIT_ZH)
    b_c = [turn(from_b0c), turn(from_b1c)]
    from_b2c = swap(b_y, BIT_C, b_c[1])
    context.append(turn(from_czl))
    b_c.append(turn(from_b2c))
    b_xy = jnp.concatenate([turn(from_bxy[0]), turn(from_bxy[1])], 1)
    from_b3c = swap(b_xy, BIT_C)
    b_c.append(turn(from_b3c))
    a_pieces = [a_own, a_x, a_y, a_xy, *a_c]
    b_pieces = [b_own, b_x, b_y, b_xy, *b_c]

    whole = [
        pltpu.VMEM((width, width), BF16),
        pltpu.VMEM((width, hidden), BF16),
        pltpu.VMEM((hidden, width), BF16),
        pltpu.SemaphoreType.DMA((192,)),
    ]
    results = call(
        forward_kernel,
        [
            ((own, width), BF16), ((own, width), F32), ((own, 128), F32), ((own, width), BF16),
            ((own, width), F32), ((own, 128), F32), ((own, hidden), BF16), ((own, hidden), F32),
        ],
        [place, *context, mine, turn(vec), b_inner, *a_pieces, *b_pieces],
        ["vmem"] * 6 + ["hbm"] * 16,
        whole,
        flops=4 * own * width * hidden * 2,
        traffic=4 * width * hidden * 2,
        name="forward",
    )
    second_out, second_normed, second_inverse, first_low, normed, inverse, active, slope = results
    second_normed = turn(second_normed)

    def to_place(kept, other):
        return join(zh, kept[None], other[None].astype(kept.dtype))[:, None]

    def first_hop(parts, after=None):
        return swap(parts[0], BIT_X, after), swap(parts[1], BIT_Y, after)

    def second_hop(rest, from_x, from_y):
        left, right = add_low(rest[0], from_x), add_low(rest[1], from_y)
        return (left[0], right[0]), swap(left[1], BIT_Y), swap(right[1], BIT_X)

    def last_hop(owns, from_y, from_x):
        return jnp.concatenate([add_low(owns[0], from_y), add_low(owns[1], from_x)], 1)

    def zl_halves(array):
        half = array.shape[1] // 2
        one, two = array[:, :half], array[:, half:]
        return jnp.where(zl == 0, one, two), jnp.where(zl == 0, two, one)

    cot_other = turn(from_cot)
    b_shape, a_shape = ((2, 2, 4, 2 * unit, cols), BF16), ((2, 2, 4, 5 * unit // 2, cols), BF16)
    b_give, b_give_rest, b_keep, b_keep_rest, second_grad, outer_grad, sums_a = call(
        outer_grad_kernel,
        [b_shape, b_shape, b_shape, b_shape, ((own, width), F32), ((own, width), BF16), ((8, width), F32)],
        [place, cot_keep, cot_other, second_normed, second_inverse, vec, active],
        name="outer_grad",
    )
    got = turn(swap(b_give, BIT_C))
    b_first = [add_low(b_keep[0], got[0]), add_low(b_keep[1], got[1])]
    from_bx1, from_by1 = first_hop(b_first)
    from_brest = swap(b_give_rest, BIT_C, got)
    outer_grad = tie(outer_grad, b_first[1])
    results = call(
        middle_kernel,
        [
            ((own, hidden), BF16), ((own, width), F32), ((own, width), BF16), ((own, cut), BF16),
            ((own, cut), BF16), ((2, own, cut), BF16), ((8, width), F32), ((8, hidden), F32),
        ],
        [place, outer_grad, slope, second_grad, normed, inverse, vec, *a_pieces, *b_pieces],
        ["vmem"] * 6 + ["hbm"] * 16,
        whole,
        flops=4 * own * width * hidden,
        traffic=6 * width * hidden,
        name="middle",
    )
    inner_grad, first_grad, attended_grad, dc_own, dc_zl, dc_give, sums_c, sums_b = results
    inner_grad = turn(inner_grad)
    a_give, a_give_rest, a_keep, a_keep_rest = call(
        inner_grad_kernel,
        [a_shape] * 4,
        [place, first_low, inner_grad, attended_grad, *context],
        scratch=[pltpu.VMEM((width, own), BF16), pltpu.VMEM((4, own, cut), BF16)],
        name="inner_grad",
    )
    a_give = turn(a_give)
    got_x, got_y = turn(from_bx1), turn(from_by1)
    b_rest = add_low(b_keep_rest, turn(from_brest))
    from_dcc = swap(dc_give, BIT_C, got_y)
    from_out = swap(second_out[rows:], BIT_ZH, got_y)
    b_owns, from_by2, from_bx2 = second_hop(b_rest, got_x, got_y)
    from_agive = swap(a_give, BIT_C, got_y)
    dc_c = turn(from_dcc)
    from_dczl = swap(jnp.stack([dc_zl, dc_c[1]]), BIT_ZL)
    from_arest = swap(a_give_rest, BIT_C, dc_c)
    got = turn(from_agive)
    a_first = [add_low(a_keep[0], got[0]), add_low(a_keep[1], got[1])]
    from_ax1, from_ay1 = first_hop(a_first)
    a_rest = add_low(a_keep_rest, turn(from_arest))
    dc = [dc_own, turn(from_dczl), dc_c]
    results = call(
        attend_back_kernel,
        [
            ((total, wide), BF16), ((8, wide), F32),
            ((own, width), F32), ((own, width), BF16), ((2, own, width), BF16),
        ],
        [place, qkv, context_wide, rows_saved, *w_attend, *dc],
        ["hbm"] * 7 + ["vmem"] * 3,
        scratch=[pltpu.VMEM(*shape) for shape in saved]
        + [
            pltpu.VMEM((HEAD, total), F32),
            pltpu.VMEM((8, total), F32),
            pltpu.VMEM((total, cut), BF16),
            pltpu.VMEM((total, 128), F32),
            head_scratch[0],
            pltpu.SemaphoreType.DMA((20,)),
        ],
        name="attend_back",
    )
    grads, sums_d, x_part, x_zl, x_give = results
    grads = turn(grads)
    outputs = to_place(second_out[:rows], turn(from_out))
    b_own = last_hop(b_owns, turn(from_by2), turn(from_bx2))
    from_bzh = swap(b_own[2:], BIT_ZH)
    got_x, got_y = turn(from_ax1), turn(from_ay1)
    a_owns, from_ay2, from_ax2 = second_hop(a_rest, got_x, got_y)
    from_xgive = swap(x_give, BIT_C, got_y)
    got = turn(from_xgive)
    x_zl = add_low(x_zl, got[1])
    x_part = x_part + got[0].astype(F32)
    from_xzl = swap(x_zl, BIT_ZL)
    grads = tie(grads, got)
    q_first, q_rest = call(
        attend_weight_kernel,
        [((2, 2, 4, shard, wide), BF16)] * 2,
        [place, x_own, x_other, grads, sums_d, sums_a, sums_b, sums_c],
        ["hbm"] * 2 + ["vmem"] * 5,
        scratch=[
            pltpu.VMEM((width, total), BF16),
            head_scratch[1],
            pltpu.VMEM((width, 128), F32),
            pltpu.VMEM((hidden, 128), F32),
            pltpu.SemaphoreType.DMA((2,)),
        ],
        name="attend_weight",
    )
    q_first = turn(q_first)
    a_own = last_hop(a_owns, turn(from_ay2), turn(from_ax2))
    a_halves = zl_halves(a_own[2:])
    b_own = add_low(b_own[:2], turn(from_bzh))
    from_az1 = swap(jnp.concatenate([a_halves[1][1:], a_halves[1][:1]]), BIT_ZL)
    from_qx1, from_qy1 = first_hop(q_first, a_own)
    a_far = add_low(a_halves[0], turn(from_az1))
    from_az2 = swap(a_far, BIT_ZH)
    got_x, got_y = turn(from_qx1), turn(from_qy1)
    q_owns, from_qy2, from_qx2 = second_hop(q_rest, got_x, got_y)
    from_bzl = swap(b_own[1], BIT_ZL, got_y)
    x_far = turn(from_xzl)
    x_grad = first_grad + (x_part + x_far.astype(F32))
    from_xzh = swap(low(x_grad[rows:]), BIT_ZH)

    def core_halves(array, axis):
        half = array.shape[axis] // 2
        first_half = lax.slice_in_dim(array, 0, half, axis=axis)
        last_half = lax.slice_in_dim(array, half, 2 * half, axis=axis)
        return jnp.where(c == 0, first_half, last_half), jnp.where(c == 0, last_half, first_half)

    q_own = last_hop(q_owns, turn(from_qy2), turn(from_qx2))
    from_qzh = swap(q_own[2:], BIT_ZH)
    got = turn(from_az2)
    empty = jnp.zeros_like(got)
    a_own = add_low(a_own[:2], join(zl, got, empty, 1))
    from_azl = swap(a_own[1], BIT_ZL)
    b_mine, b_theirs = core_halves(b_own[0].astype(F32) + turn(from_bzl).astype(F32), 0)
    from_bc = swap(low(b_theirs), BIT_C)
    q_own = add_low(q_own[:2], turn(from_qzh))
    from_qzl = swap(q_own[1], BIT_ZL)
    a_last = (a_own[0].astype(F32) + turn(from_azl).astype(F32)).reshape(5, unit, cols)
    a_mine, a_theirs = core_halves(a_last, 1)
    from_ac = swap(low(a_theirs), BIT_C)
    outer_owned = join(c, b_mine, turn(from_bc).astype(F32), 1)
    q_two = jnp.stack([q_own[0], turn(from_qzl)])
    q_mine, q_theirs = core_halves(q_two, 1)
    from_qc = swap(q_theirs, BIT_C)
    input_grad = to_place(x_grad[:rows], turn(from_xzh))
    a_got = turn(from_ac)
    q_got = turn(from_qc)
    results = call(
        last_kernel,
        [((shard, width), F32)] * 4 + [((shard, hidden), F32), ((16, 128), F32)],
        [place, q_mine, q_got, a_mine, a_got],
        scratch=[
            pltpu.VMEM((3, shard, width), F32),
            pltpu.VMEM((shard, width), F32),
            pltpu.VMEM((shard, hidden), F32),
            pltpu.SemaphoreType.DMA((5,)),
        ],
        out_spaces=["hbm"] * 5 + ["vmem"],
        name="last",
    )
    query_owned, key_owned, value_owned, output_owned, inner_owned, owned = results
    owned = owned[:12, :shard]
    return (
        outputs,
        input_grad,
        query_owned,
        key_owned,
        value_owned,
        output_owned,
        owned[0],
        owned[1],
        owned[2],
        owned[3],
        owned[4],
        inner_owned,
        owned[8:12].reshape(-1),
        outer_owned,
        owned[5],
        owned[6],
        owned[7],
    )


def solution(mesh):
    fast = mesh.shape["dp"] == 4 and mesh.shape["sp"] == 8
    body = body_fast if fast else body_general
    in_specs = (
        P(None, "dp", "sp", None),
        P(None, "dp", "sp"),
        P(None, "dp", "sp", None),
        P(("dp", "sp"), None),
        P(("dp", "sp"), None),
        P(("dp", "sp"), None),
        P(("dp", "sp"), None),
        P(("dp", "sp")),
        P(("dp", "sp")),
        P(("dp", "sp")),
        P(("dp", "sp")),
        P(("dp", "sp")),
        P(("dp", "sp"), None),
        P(("dp", "sp")),
        P(("dp", "sp"), None),
        P(("dp", "sp")),
        P(("dp", "sp")),
        P(("dp", "sp")),
    )
    out_specs = (
        P(None, "dp", "sp", None),
        P(None, "dp", "sp", None),
        P(("dp", "sp"), None),
        P(("dp", "sp"), None),
        P(("dp", "sp"), None),
        P(("dp", "sp"), None),
        P(("dp", "sp")),
        P(("dp", "sp")),
        P(("dp", "sp")),
        P(("dp", "sp")),
        P(("dp", "sp")),
        P(("dp", "sp"), None),
        P(("dp", "sp")),
        P(("dp", "sp"), None),
        P(("dp", "sp")),
        P(("dp", "sp")),
        P(("dp", "sp")),
    )
    return jax.shard_map(body, mesh=mesh, in_specs=in_specs, out_specs=out_specs, check_vma=False)
```

```python
import functools

import jax
import jax.numpy as jnp
from jax import lax
from jax.experimental import pallas as pl
from jax.experimental.pallas import tpu as pltpu
from jax.sharding import PartitionSpec as P

HEADS = 12
HEAD = 64


EPS = 1e-12
NEG = -1e30


def product(left_matrix, right_matrix):
    return jnp.dot(left_matrix, right_matrix, preferred_element_type=jnp.float32)


def left_product(left_matrix, right_matrix):
    return lax.dot_general(
        left_matrix, right_matrix, (((0,), (0,)), ((), ())), preferred_element_type=jnp.float32
    )


def right_product(left_matrix, right_matrix):
    return lax.dot_general(
        left_matrix, right_matrix, (((1,), (1,)), ((), ())), preferred_element_type=jnp.float32
    )


def by_heads(matrix):
    return matrix.reshape(matrix.shape[0], HEADS, HEAD)


def norm_forward(summed, gain, shift):
    center = summed - jnp.mean(summed, -1, keepdims=True)
    inverse = lax.rsqrt(jnp.mean(center * center, -1, keepdims=True) + EPS)
    normed = center * inverse
    return (normed * gain + shift, normed, inverse)


def norm_backward(gradient, normed, inverse, gain):
    scaled = gradient * gain
    plain_mean = jnp.mean(scaled, -1, keepdims=True)
    cross_mean = jnp.mean(scaled * normed, -1, keepdims=True)
    return (
        (scaled - plain_mean - normed * cross_mean) * inverse,
        jnp.sum(gradient * normed, 0),
        jnp.sum(gradient, 0),
    )


def attend_forward(queries, key_rows, value_rows, seg_local, seg_all):
    row_count = queries.shape[0]
    scaling = HEAD ** (-0.5)
    query_heads = by_heads(queries)
    key_piece = lax.all_gather(key_rows, "sp", axis=0, tiled=True)
    value_piece = lax.all_gather(value_rows, "sp", axis=0, tiled=True)
    row_peak = jnp.full((HEADS, row_count), NEG, jnp.float32)
    same_doc = (seg_local[:, None] == seg_all[None, :])[None]
    scores = (
        jnp.einsum(
            "qhd,khd->hqk", query_heads, by_heads(key_piece), preferred_element_type=jnp.float32
        )
        * scaling
    )
    scores = jnp.where(same_doc, scores, NEG)
    new_peak = jnp.maximum(row_peak, jnp.max(scores, -1))
    weights = jnp.where(same_doc, jnp.exp(scores - new_peak[..., None]), 0.0)
    row_total = jnp.sum(weights, -1)
    summed = jnp.einsum(
        "hqk,khd->hqd",
        weights.astype(jnp.bfloat16),
        by_heads(value_piece),
        preferred_element_type=jnp.float32,
    )
    return (new_peak, row_total, summed)


def keys_backward(
    queries, key_rows, value_rows, context_grad, log_total, row_delta, seg_local, seg_all
):
    row_count, width = queries.shape
    scaling = HEAD ** (-0.5)
    query_heads = by_heads(queries)
    grad_heads = by_heads(context_grad)
    key_piece = lax.all_gather(key_rows, "sp", axis=0, tiled=True)
    value_piece = lax.all_gather(value_rows, "sp", axis=0, tiled=True)
    piece_rows = key_piece.shape[0]
    key_heads = by_heads(key_piece)
    same_doc = (seg_local[:, None] == seg_all[None, :])[None]
    scores = (
        jnp.einsum("qhd,khd->hqk", query_heads, key_heads, preferred_element_type=jnp.float32)
        * scaling
    )
    weights = jnp.where(same_doc, jnp.exp(scores - log_total[..., None]), 0.0)
    prob_grad = jnp.einsum(
        "qhd,khd->hqk", grad_heads, by_heads(value_piece), preferred_element_type=jnp.float32
    )
    score_grad = (weights * (prob_grad - row_delta[..., None])).astype(jnp.bfloat16)
    query_sum = jnp.einsum(
        "hqk,khd->hqd", score_grad, key_heads, preferred_element_type=jnp.float32
    )
    key_term = jnp.einsum(
        "hqk,qhd->khd", score_grad, query_heads, preferred_element_type=jnp.float32
    ).reshape(piece_rows, width)
    value_term = jnp.einsum(
        "hqk,qhd->khd", weights.astype(jnp.bfloat16), grad_heads, preferred_element_type=jnp.float32
    ).reshape(piece_rows, width)
    pair_sum = jnp.concatenate([key_term, value_term], 1)
    query_sum, pair_sum = (query_sum, pair_sum)
    pair_mine = lax.psum_scatter(pair_sum, "sp", scatter_dimension=0, tiled=True)
    query_sum = jnp.transpose(query_sum, (1, 0, 2)).reshape(row_count, width)
    return (query_sum, pair_mine[:, :width], pair_mine[:, width:])


def body_general(
    tokens,
    doc_ids,
    cotangent,
    query_weight,
    key_weight,
    value_weight,
    output_weight,
    query_bias,
    value_bias,
    output_bias,
    first_gain,
    first_shift,
    inner_weight,
    inner_bias,
    outer_weight,
    outer_bias,
    second_gain,
    second_shift,
):
    shards = (
        query_weight,
        key_weight,
        value_weight,
        output_weight,
        query_bias,
        value_bias,
        output_bias,
        first_gain,
        first_shift,
        inner_weight,
        inner_bias,
        outer_weight,
        outer_bias,
        second_gain,
        second_shift,
    )
    scaling = HEAD ** (-0.5)
    results = []
    input_grads = []
    totals = ()
    for micro in range(tokens.shape[0]):
        loaded = (
            lax.all_gather(shards[0], ("dp", "sp"), axis=0, tiled=True),
            lax.all_gather(shards[1], ("dp", "sp"), axis=0, tiled=True),
            lax.all_gather(shards[2], ("dp", "sp"), axis=0, tiled=True),
            lax.all_gather(shards[3], ("dp", "sp"), axis=0, tiled=True),
            lax.all_gather(shards[4], ("dp", "sp"), axis=0, tiled=True),
            lax.all_gather(shards[5], ("dp", "sp"), axis=0, tiled=True),
            lax.all_gather(shards[6], ("dp", "sp"), axis=0, tiled=True),
            lax.all_gather(shards[7], ("dp", "sp"), axis=0, tiled=True),
            lax.all_gather(shards[8], ("dp", "sp"), axis=0, tiled=True),
            lax.all_gather(shards[9], ("dp", "sp"), axis=0, tiled=True),
            lax.all_gather(shards[10], ("dp", "sp"), axis=0, tiled=True),
            lax.all_gather(shards[11], ("dp", "sp"), axis=0, tiled=True),
            lax.all_gather(shards[12], ("dp", "sp"), axis=0, tiled=True),
            lax.all_gather(shards[13], ("dp", "sp"), axis=0, tiled=True),
            lax.all_gather(shards[14], ("dp", "sp"), axis=0, tiled=True),
        )
        (
            w_query,
            w_key,
            w_value,
            w_output,
            b_query,
            b_value,
            b_output,
            g_first,
            s_first,
            w_inner,
            b_inner,
            w_outer,
            b_outer,
            g_second,
            s_second,
        ) = loaded
        inputs = tokens[micro, 0]
        seg_local = doc_ids[micro, 0]
        seg_all = lax.all_gather(seg_local, "sp", axis=0, tiled=True)
        row_count, width = inputs.shape
        queries = (product(inputs, w_query) + b_query).astype(jnp.bfloat16)
        key_rows = product(inputs, w_key).astype(jnp.bfloat16)
        value_rows = (product(inputs, w_value) + b_value).astype(jnp.bfloat16)
        row_peak, row_total, summed = attend_forward(
            queries, key_rows, value_rows, seg_local, seg_all
        )
        context_heads = summed / row_total[..., None]
        log_total = row_peak + jnp.log(row_total)
        context_low = (
            jnp.transpose(context_heads, (1, 0, 2)).reshape(row_count, width).astype(jnp.bfloat16)
        )
        attended = product(context_low, w_output) + b_output
        first_out, first_normed, first_inverse = norm_forward(
            inputs.astype(jnp.float32) + attended, g_first, s_first
        )
        first_low = first_out.astype(jnp.bfloat16)
        inner = product(first_low, w_inner) + b_inner
        active = jax.nn.gelu(inner, approximate=False).astype(jnp.bfloat16)
        outer = product(active, w_outer) + b_outer
        second_out, second_normed, second_inverse = norm_forward(
            first_out + outer, g_second, s_second
        )
        results.append(second_out.astype(jnp.bfloat16))
        loaded = (
            lax.all_gather(shards[0], ("dp", "sp"), axis=0, tiled=True),
            lax.all_gather(shards[1], ("dp", "sp"), axis=0, tiled=True),
            lax.all_gather(shards[2], ("dp", "sp"), axis=0, tiled=True),
            lax.all_gather(shards[3], ("dp", "sp"), axis=0, tiled=True),
            lax.all_gather(shards[4], ("dp", "sp"), axis=0, tiled=True),
            lax.all_gather(shards[5], ("dp", "sp"), axis=0, tiled=True),
            lax.all_gather(shards[6], ("dp", "sp"), axis=0, tiled=True),
            lax.all_gather(shards[7], ("dp", "sp"), axis=0, tiled=True),
            lax.all_gather(shards[8], ("dp", "sp"), axis=0, tiled=True),
            lax.all_gather(shards[9], ("dp", "sp"), axis=0, tiled=True),
            lax.all_gather(shards[10], ("dp", "sp"), axis=0, tiled=True),
            lax.all_gather(shards[11], ("dp", "sp"), axis=0, tiled=True),
            lax.all_gather(shards[12], ("dp", "sp"), axis=0, tiled=True),
            lax.all_gather(shards[13], ("dp", "sp"), axis=0, tiled=True),
            lax.all_gather(shards[14], ("dp", "sp"), axis=0, tiled=True),
        )
        (
            w_query,
            w_key,
            w_value,
            w_output,
            b_query,
            b_value,
            b_output,
            g_first,
            s_first,
            w_inner,
            b_inner,
            w_outer,
            b_outer,
            g_second,
            s_second,
        ) = loaded
        upstream = cotangent[micro, 0].astype(jnp.float32)
        second_grad, second_gain_grad, second_shift_grad = norm_backward(
            upstream, second_normed, second_inverse, g_second
        )
        outer_grad = second_grad.astype(jnp.bfloat16)
        outer_bias_grad = jnp.sum(outer_grad.astype(jnp.float32), 0)
        outer_weight_grad = left_product(active, outer_grad)
        active_grad = right_product(outer_grad, w_outer)
        _, gelu_pull = jax.vjp(lambda hidden: jax.nn.gelu(hidden, approximate=False), inner)
        inner_grad = gelu_pull(active_grad)[0].astype(jnp.bfloat16)
        inner_bias_grad = jnp.sum(inner_grad.astype(jnp.float32), 0)
        inner_weight_grad = left_product(first_low, inner_grad)
        first_incoming = second_grad + right_product(inner_grad, w_inner)
        first_grad, first_gain_grad, first_shift_grad = norm_backward(
            first_incoming, first_normed, first_inverse, g_first
        )
        attended_grad = first_grad.astype(jnp.bfloat16)
        output_bias_grad = jnp.sum(attended_grad.astype(jnp.float32), 0)
        output_weight_grad = left_product(context_low, attended_grad)
        context_grad = right_product(attended_grad, w_output).astype(jnp.bfloat16)
        row_delta = jnp.sum(jnp.transpose(by_heads(context_grad), (1, 0, 2)) * context_heads, -1)
        query_sum, key_sum, value_sum = keys_backward(
            queries, key_rows, value_rows, context_grad, log_total, row_delta, seg_local, seg_all
        )
        query_grad = (query_sum * scaling).astype(jnp.bfloat16)
        key_grad = (key_sum * scaling).astype(jnp.bfloat16)
        value_grad = value_sum.astype(jnp.bfloat16)
        query_bias_grad = jnp.sum(query_grad.astype(jnp.float32), 0)
        value_bias_grad = jnp.sum(value_grad.astype(jnp.float32), 0)
        query_weight_grad = left_product(inputs, query_grad)
        key_weight_grad = left_product(inputs, key_grad)
        value_weight_grad = left_product(inputs, value_grad)
        input_grads.append(
            first_grad
            + right_product(query_grad, w_query)
            + right_product(key_grad, w_key)
            + right_product(value_grad, w_value)
        )
        terms = (
            query_weight_grad,
            key_weight_grad,
            value_weight_grad,
            output_weight_grad,
            query_bias_grad,
            value_bias_grad,
            output_bias_grad,
            first_gain_grad,
            first_shift_grad,
            inner_weight_grad,
            inner_bias_grad,
            outer_weight_grad,
            outer_bias_grad,
            second_gain_grad,
            second_shift_grad,
        )
        if micro == 0:
            totals = terms
        else:
            totals = tuple((earlier + latest for earlier, latest in zip(totals, terms)))
    owned = lax.psum_scatter(totals, ("dp", "sp"), scatter_dimension=0, tiled=True)
    return (
        jnp.stack(results)[:, None],
        jnp.stack(input_grads)[:, None],
        owned[0],
        owned[1],
        owned[2],
        owned[3],
        owned[4],
        owned[5],
        owned[6],
        owned[7],
        owned[8],
        owned[9],
        owned[10],
        owned[11],
        owned[12],
        owned[13],
        owned[14],
    )


BIT_Y, BIT_X, BIT_ZH, BIT_ZL, BIT_C = 16, 8, 4, 2, 1
AXES = ("dp", "sp")
GAUSS = 0.3989422804014327
LIMITS = {
    "first": 2, "query": 2, "last": 4, "attend": 24, "forward": 20, "outer_grad": 12, "middle": 20, "inner_grad": 12,
    "attend_back": 24, "attend_weight": 20,
}
SIDE = 64
SCALE = 0.0
DOC_ROWS = 16
BF16, F32 = jnp.bfloat16, jnp.float32


def low(array):
    return array.astype(BF16)


def swap(array, mask, after=None):
    if after is not None:
        array, _ = lax.optimization_barrier((array, after))
    return lax.ppermute(array, AXES, [(i, i ^ mask) for i in range(32)])


class Turns:
    def __init__(self):
        self.last = None

    def __call__(self, array):
        if self.last is not None:
            array, _ = lax.optimization_barrier((array, self.last))
        self.last = array
        return array


def tie(array, other):
    return lax.optimization_barrier((array, other))[0]


def join(bit, own, other, axis=0):
    return jnp.where(
        bit == 0, jnp.concatenate([own, other], axis), jnp.concatenate([other, own], axis)
    )


def pair(own, other):
    return jnp.concatenate([own, other], 0)


def add_low(own, other):
    return low(own.astype(F32) + other.astype(F32))


def call(kernel, outs, operands, spaces=None, scratch=(), flops=0, traffic=0, name=None, out_spaces=None):
    whole = pl.BlockSpec(memory_space=pltpu.VMEM)
    specs = [pl.BlockSpec(memory_space=pltpu.SMEM)]
    operands = list(operands)
    for n, kind in enumerate(spaces or ["vmem"] * (len(operands) - 1), 1):
        space = pl.ANY if kind == "any" else pltpu.HBM
        specs.append(whole if kind == "vmem" else pl.BlockSpec(memory_space=space))
        if kind == "hbm":
            operands[n] = pltpu.with_memory_space_constraint(operands[n], pltpu.HBM)
    return pl.pallas_call(
        kernel,
        out_shape=tuple(jax.ShapeDtypeStruct(shape, dtype) for shape, dtype in outs),
        in_specs=specs,
        out_specs=tuple(
            whole if kind == "vmem" else pl.BlockSpec(memory_space=pltpu.HBM)
            for kind in (out_spaces or ["vmem"] * len(outs))
        ),
        scratch_shapes=list(scratch),
        compiler_params=pltpu.CompilerParams(vmem_limit_bytes=LIMITS[name] * 1024 * 1024),
        cost_estimate=pl.CostEstimate(flops=int(flops * SCALE) + 1, transcendentals=0, bytes_accessed=int(traffic * SCALE) + 1),
        name=name,
    )(*operands)


def block_at(place, k):
    return (place[0] ^ (k // 2)) * 2 + (place[1] ^ (k % 2))


def unit_at(place, u):
    return (place[2] ^ (u // 2)) * 2 + (place[3] ^ (u % 2))


def first_kernel(place, tokens, docs, inner, outer, output, x_keep, x_give, keep, give, ids, sems):
    zh, c = place[2], place[4]
    rows, width = tokens.shape[1:]
    shard, cols = keep.shape[1:]
    started = [pltpu.make_async_copy(docs, ids, sems.at[0])]
    for flip in range(2):
        x_out, out = (x_keep, x_give)[flip], (keep, give)[flip]
        moves = [(tokens.at[zh ^ flip], x_out.at[pl.ds(0, rows), :])]
        half = c ^ flip
        for j in range(4):
            at = pl.ds(pl.multiple_of(half * (4 * cols) + j * cols, 128), cols)
            moves.append((inner.at[:, at], out.at[j]))
        at = pl.ds(pl.multiple_of(half * cols, 128), cols)
        for j in range(4):
            moves.append((outer.at[pl.ds(shard * j, shard), at], out.at[4 + j]))
        moves.append((output.at[:, at], out.at[8]))
        for source, target in moves:
            started.append(pltpu.make_async_copy(source, target, sems.at[len(started)]))
    for copy in started:
        copy.start()
    for copy in started:
        copy.wait()
    for flip, out in ((0, x_keep), (1, x_give)):
        line = ids[pl.ds(zh ^ flip, 1), :].astype(F32)
        line = jnp.concatenate([line, jnp.zeros((1, width - rows), F32)], 1)
        out[rows : rows + DOC_ROWS, :] = low(jnp.broadcast_to(line, (DOC_ROWS, width)))


def query_kernel(place, wq, wk, wv, smalls, q_keep, q_give, weights, blocks, side, sems):
    zl, c = place[3], place[4]
    shard, width = wq.shape
    cut = width // 4
    started = [
        pltpu.make_async_copy(w, weights.at[n], sems.at[n]) for n, w in enumerate((wq, wk, wv))
    ]
    for copy in started:
        copy.start()
    side[...] = jnp.zeros_like(side)
    side[SIDE : SIDE + 16, :] = smalls[...]
    columns = low(jnp.transpose(side[...]))[:shard, SIDE:]
    for copy in started:
        copy.wait()
    for p in range(4):
        at = slice(cut * p, cut * (p + 1))
        blocks[p] = jnp.concatenate([weights[0, :, at], weights[1, :, at], weights[2, :, at], columns], 1)
    for r in range(2):
        q_keep[r] = blocks[2 * (zl ^ r) + c]
        q_give[r] = blocks[2 * (zl ^ r) + (1 - c)]


PARTS = (((2, 0), (3, 0)), ((0, 0), (3, 1)), ((2, 1), (1, 0)), ((0, 1), (1, 1)))


def put_rows(outs, k, u, start, value):
    half = outs[0].shape[3]
    stop = start + value.shape[0]
    if start < half:
        part, n = PARTS[k][0]
        out = outs[part // 2]
        out[part % 2, n, u, start : min(stop, half), :] = value[: min(stop, half) - start, :]
    if stop > half:
        part, n = PARTS[k][1]
        out = outs[part // 2]
        first = max(start, half)
        out[part % 2, n, u, first - half : stop - half, :] = value[first - start :, :]


def head_copies(pieces, place, w, sems, base):
    size = pieces[0].shape[1]
    started = []
    for k, part in enumerate(pieces):
        for u in range(4):
            at = block_at(place, k) * (4 * size) + unit_at(place, u) * size
            target = w.at[pl.ds(pl.multiple_of(at, 16), size), :]
            started.append(pltpu.make_async_copy(part.at[u], target, sems.at[base + len(started)]))
    return started


def attend_kernel(place, w0, w1, w2, w3, x_own, x_other, *refs):
    context_out, (qkv, wide, rows_of, vec_out) = refs[:2], refs[2:6]
    w, doc_col = refs[6:]
    size = w0.shape[1]
    for k, part in enumerate((w0, w1, w2, w3)):
        for u in range(4):
            at = block_at(place, k) * (4 * size) + unit_at(place, u) * size
            w[pl.ds(pl.multiple_of(at, 16), size), :] = part[u]
    cut = qkv.shape[2]
    heads = cut // HEAD
    group = place[5]
    tile = slice(3 * cut - SIDE, 3 * cut + SIDE)
    vec_out[...] = jnp.transpose(w[:, tile].astype(F32))[SIDE : SIDE + 16, :]
    biases = w[pl.ds(pl.multiple_of(group * cut, 64), cut), tile].astype(F32)
    biases = jnp.transpose(jnp.concatenate([biases, jnp.zeros((64, 2 * SIDE), F32)], 0))
    bq, bv = biases[SIDE : SIDE + 1, :cut], biases[SIDE + 1 : SIDE + 2, :cut]
    rows = x_own.shape[1] - DOC_ROWS
    ids = []
    for n in range(8):
        source = (x_own, x_other)[n // 4]
        part = product(source[n % 4, 0:rows, :], w[:, : 3 * cut])
        at = pl.ds(rows * n, rows)
        qkv[0, at, :] = low(part[:, :cut] + bq)
        qkv[1, at, :] = low(part[:, cut : 2 * cut])
        qkv[2, at, :] = low(part[:, 2 * cut :] + bv)
        ids.append(source[n % 4, rows : rows + 1, 0:128].astype(F32))
    doc_row = jnp.concatenate(ids, 1)
    rows_of[8:16, :] = jnp.broadcast_to(doc_row, (8, doc_row.shape[1]))
    turned = jnp.transpose(jnp.concatenate(ids + [jnp.zeros((120, 128), F32)], 0))
    for n in range(8):
        doc_col[pl.ds(rows * n, rows), :] = jnp.broadcast_to(turned[:, n : n + 1], (rows, 128))
    rows = 2 * rows
    lane = lax.broadcasted_iota(jnp.int32, (rows, 128), 1)
    for i in (2, 3, 0, 1):
        at = pl.ds(rows * i, rows)
        same = doc_col[at, 0:1] == doc_row
        pieces = []
        logs = jnp.zeros((rows, 128), F32)
        for h in range(heads):
            cols = slice(HEAD * h, HEAD * (h + 1))
            query = qkv[0, at, cols] * BF16(HEAD**-0.5)
            scores = right_product(query, qkv[1, :, cols])
            scores = jnp.where(same, scores, NEG)
            peak = jnp.max(scores, -1, keepdims=True)
            weights = jnp.exp(scores - peak)
            denom = jnp.sum(weights, -1, keepdims=True)
            summed = product(low(weights), qkv[2, :, cols])
            pieces.append(summed / denom)
            logs = jnp.where(lane == h, peak + jnp.log(denom), logs)
        context = jnp.concatenate(pieces, 1)
        wide[at, :] = context
        context_out[i // 2][i % 2] = low(context)
        rows_of[0:8, at] = jnp.transpose(logs)[:8, :]


def attend_back_kernel(
    place, qkv_in, wide_in, rows_in, w0, w1, w2, w3, g_own, g_zl, g_c, grads, sums, x_part, x_zl, x_give,
    qkv, wide, rows_of, dq_acc, delta_ref, dc, doc_col, w, sems
):
    copies_in = [
        pltpu.make_async_copy(source, target, sems.at[n])
        for n, (source, target) in enumerate(((qkv_in, qkv), (wide_in, wide), (rows_in, rows_of)))
    ]
    weight_copies = head_copies((w0, w1, w2, w3), place, w, sems, 3)
    for copy in copies_in + weight_copies:
        copy.start()
    for copy in copies_in:
        copy.wait()
    total, cut = wide.shape
    heads = cut // HEAD
    rows = total // 4
    scaling = HEAD**-0.5
    lane = lax.broadcasted_iota(jnp.int32, (rows, 128), 1)
    doc_row = rows_of[8:9, :]
    for n in range(total // 128):
        at = slice(128 * n, 128 * (n + 1))
        doc_col[at, :] = jnp.transpose(jnp.broadcast_to(rows_of[8:9, at], (128, 128)))
    for i in range(4):
        at = pl.ds(rows * i, rows)
        grad = (g_own[...], g_zl[0], g_c[0], g_zl[1])[i]
        dc[at, :] = grad
        prod = grad.astype(F32) * wide[at, :]
        cols = jnp.zeros((rows, 128), F32)
        for h in range(heads):
            piece = jnp.sum(prod[:, HEAD * h : HEAD * (h + 1)], -1, keepdims=True)
            cols = jnp.where(lane == h, piece, cols)
        delta_ref[:, at] = jnp.transpose(cols)[:8, :]
    for h in range(heads):
        cols = slice(HEAD * h, HEAD * (h + 1))
        query = qkv[0, :, cols]
        scaled = query * BF16(scaling)
        grad_rows = dc[:, cols]
        for i in range(4):
            at = pl.ds(rows * i, rows)
            key = qkv[1, at, cols]
            value = qkv[2, at, cols]
            same = doc_col[at, 0:1] == doc_row
            scores = jnp.where(same, right_product(key, scaled), NEG)
            probs = jnp.exp(scores - rows_of[h : h + 1, :])
            prob_grad = right_product(value, grad_rows)
            score_grad = low(probs * (prob_grad - delta_ref[h : h + 1, :]))
            grads[at, cut + HEAD * h : cut + HEAD * (h + 1)] = low(product(score_grad, query) * scaling)
            grads[at, 2 * cut + HEAD * h : 2 * cut + HEAD * (h + 1)] = low(product(low(probs), grad_rows))
            piece = left_product(key, score_grad)
            if i == 0:
                dq_acc[...] = piece
            else:
                dq_acc[...] += piece
        grads[:, cols] = low(jnp.transpose(dq_acc[...]) * scaling)
    grads[:, 3 * cut :] = jnp.zeros((total, SIDE), BF16)
    for copy in weight_copies:
        copy.wait()
    for n in (2, 3, 1, 0):
        at = pl.ds(rows * n, rows)
        part = right_product(grads[at, : 3 * cut], w[:, : 3 * cut])
        if n == 0:
            x_part[...] = part
        elif n == 1:
            x_zl[...] = low(part)
        else:
            x_give[n - 2] = low(part)
    sums[0:1, :] = jnp.sum(grads[...].astype(F32), 0, keepdims=True)


def attend_weight_kernel(
    place, x_own, x_other, grads, sums, sums_a, sums_b, sums_c, *refs
):
    outs, (turned, x, side, tall, sems) = refs[:2], refs[2:]
    copies_in = [
        pltpu.make_async_copy(part, x.at[n], sems.at[n]) for n, part in enumerate((x_own, x_other))
    ]
    for copy in copies_in:
        copy.start()
    rows = x.shape[2] - DOC_ROWS
    group = place[5]
    width = sums_a.shape[1]
    cut = width // 4
    early = jnp.concatenate([sums_c[2:3, :], sums_c[0:2, :], sums_a[2:3, :], sums_a[0:2, :]], 0)
    pad = jnp.concatenate(
        [jnp.zeros((SIDE + 2, width), F32), early, jnp.zeros((SIDE - 8, width), F32)], 0
    )
    side[...] = jnp.transpose(pad)
    own = jnp.concatenate([sums[0:1, :cut], sums[0:1, 2 * cut : 3 * cut]], 0)
    own = jnp.concatenate([own, jnp.zeros((2, 256 - cut), F32)], 1)
    own = jnp.concatenate([jnp.zeros((SIDE, 256), F32), own, jnp.zeros((SIDE - 2, 256), F32)], 0)
    at = pl.ds(pl.multiple_of(group * cut, 64), cut)
    side[at, :] += jnp.transpose(own)[:cut, :]
    tall[...] = jnp.transpose(jnp.broadcast_to(sums_b[0:1, :], (128, sums_b.shape[1])))
    shard = width // 32
    lane = lax.broadcasted_iota(jnp.int32, (shard, 128), 1)
    for n in range(32):
        at = slice(shard * n, shard * (n + 1))
        value = side[at, :]
        for q in range(4):
            start = 4 * shard * n + shard * q
            value = jnp.where(lane == SIDE + 8 + q, tall[start : start + shard, :], value)
        side[at, :] = value
    for copy in copies_in:
        copy.wait()
    for n in range(8):
        turned[:, pl.ds(rows * n, rows)] = jnp.transpose(x[n // 4, n % 4, 0:rows, :])
    size = 2 * outs[0].shape[3]
    for k in range(4):
        at = pl.ds(pl.multiple_of(block_at(place, k) * (4 * size), 64), 4 * size)
        piece = product(turned[at, :], grads[...])
        piece = jnp.concatenate([piece[:, : 3 * cut - SIDE], piece[:, 3 * cut - SIDE :] + side[at, :]], 1)
        for a in range(4):
            put_rows(outs, k, unit_at(place, a), 0, low(piece[size * a : size * (a + 1), :]))


def last_kernel(place, q_mine, q_got, a_mine, a_got, wq, wk, wv, wo, wi, small, buf_q, buf_o, buf_i, sems):
    zl, c = place[3], place[4]
    shard, width = wq.shape
    cut = width // 4
    parts = [q_mine[0].astype(F32), q_got[0].astype(F32), q_mine[1].astype(F32), q_got[1].astype(F32)]

    def ordered(bit, own, other):
        return jnp.concatenate([jnp.where(bit == 0, own, other), jnp.where(bit == 0, other, own)], 1)

    for n in range(3):
        cols = [part[:, cut * n : cut * (n + 1)] for part in parts]
        near, far = ordered(c, cols[0], cols[1]), ordered(c, cols[2], cols[3])
        buf_q[n] = ordered(zl, near, far)
    started = [pltpu.make_async_copy(buf_q.at[n], out, sems.at[n]) for n, out in enumerate((wq, wk, wv))]
    mine = [a_mine[j] for j in range(5)]
    theirs = [a_got[j].astype(F32) for j in range(5)]
    buf_o[...] = ordered(c, mine[4], theirs[4])
    buf_i[...] = ordered(c, jnp.concatenate(mine[:4], 1), jnp.concatenate(theirs[:4], 1))
    started += [pltpu.make_async_copy(buf_o, wo, sems.at[3]), pltpu.make_async_copy(buf_i, wi, sems.at[4])]
    for copy in started:
        copy.start()
    tile = slice(3 * cut - SIDE, 3 * cut + SIDE)
    total = (parts[0][:, tile] + parts[1][:, tile]) + (parts[2][:, tile] + parts[3][:, tile])
    total = jnp.concatenate([total, jnp.zeros((128 - shard, 2 * SIDE), F32)], 0)
    small[...] = jnp.transpose(total)[SIDE : SIDE + 16, :]
    for copy in started:
        copy.wait()


def copies(pieces, whole, place, sems, base, column_blocks, first, row_count):
    c = place[4]
    started = []
    for half in range(2):
        for k in range(4):
            for u in range(4):
                for j in range(column_blocks):
                    source = pieces[half * 4 + k]
                    cols = source.shape[-1]
                    row = block_at(place, k) * (4 * row_count) + unit_at(place, u) * row_count
                    col = (c ^ half) * (column_blocks * cols) + j * cols
                    target = whole.at[
                        pl.ds(pl.multiple_of(row, 16), row_count), pl.ds(pl.multiple_of(col, 128), cols)
                    ]
                    if column_blocks > 1:
                        source = source.at[u, j]
                    else:
                        source = source.at[u, pl.ds(first, row_count), :]
                    started.append(pltpu.make_async_copy(source, target, sems.at[base + len(started)]))
    return started


def forward_kernel(place, c_own, c_c, c_zl, x_ref, vec, b_inner, *refs):
    a_p, b_p = refs[:8], refs[8:16]
    (out, n2_out, r2_out, h1b_out, n1_out, r1_out, g_out, gp_out) = refs[16:24]
    wo, wi, wu, sems = refs[24:]
    unit = wo.shape[0] // 16
    copy_o = copies(b_p, wo, place, sems, 0, 1, 4 * unit, unit)
    copy_i = copies(a_p, wi, place, sems, 32, 4, 0, unit)
    copy_u = copies(b_p, wu, place, sems, 160, 1, 0, 4 * unit)
    for copy in copy_o + copy_i + copy_u:
        copy.start()
    group = place[5]
    rows = x_ref.shape[1] - DOC_ROWS
    cut = c_own.shape[-1]
    for copy in copy_o:
        copy.wait()
    attended = vec[2:3, :]
    for mask in range(4):
        part = (c_own, c_c, c_zl, c_zl)[mask]
        at = pl.ds(pl.multiple_of((group ^ mask) * cut, 64), cut)
        attended = attended + product(part[mask // 3], wo[at, :])
    tokens = jnp.concatenate([x_ref[0, 0:rows, :], x_ref[1, 0:rows, :]], 0)
    first_out, normed, inverse = norm_forward(tokens.astype(F32) + attended, vec[3:4, :], vec[4:5, :])
    n1_out[...] = normed
    r1_out[...] = jnp.broadcast_to(inverse, r1_out.shape)
    h1b_out[...] = low(first_out)
    for copy in copy_i + copy_u:
        copy.wait()
    outer = vec[5:6, :]
    step = 512
    for j in range(wi.shape[1] // step):
        at = slice(step * j, step * (j + 1))
        hidden = product(h1b_out[...], wi[:, at]) + b_inner[:, at]
        half = 0.5 + 0.5 * lax.erf(hidden * (0.5**0.5))
        active = low(hidden * half)
        g_out[:, at] = active
        gp_out[:, at] = half + hidden * jnp.exp(hidden * hidden * -0.5) * GAUSS
        outer = outer + product(active, wu[at, :])
    second_out, normed, inverse = norm_forward(first_out + outer, vec[6:7, :], vec[7:8, :])
    out[...] = low(second_out)
    n2_out[...] = normed
    r2_out[...] = jnp.broadcast_to(inverse, r2_out.shape)


def outer_grad_kernel(
    place, cot_own, cot_other, n2, r2, vec, g_ref, give, give_rest, keep, keep_rest, dz2_out, df_ref, sums
):
    c = place[4]
    upstream = jnp.concatenate([cot_own[...], cot_other[...]], 0).astype(F32)
    grad, gain_grad, shift_grad = norm_backward(upstream, n2[...], r2[:, 0:1], vec[6:7, :])
    dz2_out[...] = grad
    grad_low = low(grad)
    df_ref[...] = grad_low
    sums[0:1, :] = gain_grad[None]
    sums[1:2, :] = shift_grad[None]
    sums[2:3, :] = jnp.sum(grad_low.astype(F32), 0, keepdims=True)
    unit, cols = 2 * give.shape[3], give.shape[4]
    give_part = df_ref[:, pl.ds(pl.multiple_of((1 - c) * cols, 128), cols)]
    keep_part = df_ref[:, pl.ds(pl.multiple_of(c * cols, 128), cols)]
    both = jnp.concatenate([give_part, keep_part], 1)
    for k in range(4):
        at = pl.ds(pl.multiple_of(block_at(place, k) * (4 * unit), 128), 4 * unit)
        piece = low(left_product(g_ref[:, at], both))
        for a in range(4):
            at = slice(unit * a, unit * (a + 1))
            put_rows((give, give_rest), k, unit_at(place, a), 0, piece[at, :cols])
            put_rows((keep, keep_rest), k, unit_at(place, a), 0, piece[at, cols:])


def middle_kernel(place, df_ref, gp_ref, dz2, n1, r1, vec, *refs):
    a_p, b_p = refs[:8], refs[8:16]
    du, grad_out, da, dc0, dc1, dc_give, sums, sums_b = refs[16:24]
    wo, wi, wu, sems = refs[24:]
    unit = wo.shape[0] // 16
    copy_o = copies(b_p, wo, place, sems, 0, 1, 4 * unit, unit)
    copy_i = copies(a_p, wi, place, sems, 32, 4, 0, unit)
    copy_u = copies(b_p, wu, place, sems, 160, 1, 0, 4 * unit)
    for copy in copy_u + copy_i + copy_o:
        copy.start()
    group = place[5]
    for copy in copy_u + copy_i:
        copy.wait()
    step = 512
    incoming = dz2[...]
    for j in range(wu.shape[0] // step):
        at = slice(step * j, step * (j + 1))
        grad = low(right_product(df_ref[...], wu[at, :]) * gp_ref[:, at])
        du[:, at] = grad
        sums_b[0:1, at] = jnp.sum(grad.astype(F32), 0, keepdims=True)
        incoming = incoming + right_product(grad, wi[:, at])
    for copy in copy_o:
        copy.wait()
    grad, gain_grad, shift_grad = norm_backward(incoming, n1[...], r1[:, 0:1], vec[3:4, :])
    grad_out[...] = grad
    grad_low = low(grad)
    da[...] = grad_low
    sums[0:1, :] = gain_grad[None]
    sums[1:2, :] = shift_grad[None]
    sums[2:3, :] = jnp.sum(grad_low.astype(F32), 0, keepdims=True)
    cut = dc0.shape[1]
    for mask in (1, 3, 0, 2):
        at = pl.ds(pl.multiple_of((group ^ mask) * cut, 64), cut)
        part = low(right_product(grad_low, wo[at, :]))
        if mask % 2:
            dc_give[mask // 2] = part
        else:
            (dc0, dc1)[mask // 2][...] = part


def inner_grad_kernel(place, h1b_ref, du, da, c_own, c_c, c_zl, give, give_rest, keep, keep_rest, turned, cs):
    c, group = place[4], place[5]
    turned[...] = jnp.transpose(h1b_ref[...])
    for mask in range(4):
        cs[mask] = (c_own, c_c, c_zl, c_zl)[mask][mask // 3]
    unit, cols = 2 * give.shape[3] // 5, give.shape[4]
    blocks = 5
    wide = (blocks - 1) * cols
    for half in range(2):
        side = c ^ 1 ^ half
        right = du[:, pl.ds(pl.multiple_of(side * wide, 128), wide)]
        right_low = da[:, pl.ds(pl.multiple_of(side * cols, 128), cols)]
        for k in range(4):
            block = block_at(place, k)
            at = pl.ds(pl.multiple_of(block * (4 * unit), 64), 4 * unit)
            piece = low(product(turned[at, :], right))
            tail = low(left_product(cs[block ^ group], right_low))
            for a in range(4):
                u = unit_at(place, a)
                rows = slice(unit * a, unit * (a + 1))
                for j in range(blocks):
                    part = piece[rows, cols * j : cols * (j + 1)] if j < blocks - 1 else tail[rows, :]
                    outs = (keep, keep_rest) if half else (give, give_rest)
                    put_rows(outs, k, u, unit * j, part)


def body_fast(
    tokens,
    doc_ids,
    cotangent,
    query_weight,
    key_weight,
    value_weight,
    output_weight,
    query_bias,
    value_bias,
    output_bias,
    first_gain,
    first_shift,
    inner_weight,
    inner_bias,
    outer_weight,
    outer_bias,
    second_gain,
    second_shift,
):
    dp, sp = lax.axis_index("dp"), lax.axis_index("sp")
    y, x, zh, zl, c = dp // 2, dp % 2, sp // 4, (sp // 2) % 2, sp % 2
    place = jnp.stack([y, x, zh, zl, c, sp % 4]).astype(jnp.int32)
    width, hidden, rows = tokens.shape[-1], inner_weight.shape[1], tokens.shape[2]
    cut, shard = width // 4, query_weight.shape[0]
    unit = 2 * shard
    wide = 3 * cut + SIDE
    own, total = 2 * rows, 8 * rows
    turn = Turns()

    x_rows = rows + DOC_ROWS
    cols = hidden // 8
    x_keep, x_give, w_keep, w_give = call(
        first_kernel,
        [((x_rows, width), BF16)] * 2 + [((9, shard, cols), BF16)] * 2,
        [place, tokens[:, 0], doc_ids[:, 0], inner_weight, outer_weight, output_weight],
        ["hbm"] * 5,
        scratch=[pltpu.VMEM((2, rows), jnp.int32), pltpu.SemaphoreType.DMA((24,))],
        name="first",
    )
    from_xzh = swap(x_give, BIT_ZH)
    got = turn(swap(w_give, BIT_C))

    def zl_half(array):
        half = array.shape[1] // 2
        return lax.dynamic_slice_in_dim(array, zl * half, half, 1)

    def far_pair(own_half, other_half):
        turned = pair(other_half[1:], other_half[:1])
        return join(zl, own_half, turned, 1)

    a_unit = join(c, w_keep[:4], got[:4], 1)
    b_unit = jnp.concatenate(
        [
            join(c, w_keep[4:8].reshape(4 * shard, cols), got[4:8].reshape(4 * shard, cols)),
            join(c, w_keep[8], got[8]),
        ]
    )
    from_a2 = swap(a_unit[None], BIT_ZL)

    a_pair = pair(a_unit[None], turn(from_a2))
    from_a4 = swap(zl_half(a_pair), BIT_ZH)
    from_b2 = swap(b_unit[None], BIT_ZL, a_pair)
    b_pair = pair(b_unit[None], turn(from_b2))
    a_half = turn(from_a4)
    from_a5 = swap(a_half, BIT_ZL)
    from_b4 = swap(zl_half(b_pair), BIT_ZH, a_half)

    smalls = [
        query_bias, value_bias, output_bias, first_gain, first_shift,
        outer_bias, second_gain, second_shift,
    ] + [inner_bias[shard * q : shard * (q + 1)] for q in range(4)]
    smalls = list(lax.optimization_barrier((*smalls, a_half))[:-1])
    row = lax.broadcasted_iota(jnp.int32, (16, 128), 0)
    packed = jnp.zeros((16, 128), F32)
    for n, small in enumerate(smalls):
        wide_small = jnp.pad(small.astype(F32), (0, 128 - shard))
        packed = jnp.where(row == n, wide_small[None], packed)
    q_keep, q_give = call(
        query_kernel,
        [((2, shard, wide), BF16)] * 2,
        [place, tie(query_weight, a_half), key_weight, value_weight, packed],
        ["hbm"] * 3 + ["vmem"],
        scratch=[
            pltpu.VMEM((3, shard, width), BF16),
            pltpu.VMEM((4, shard, wide), BF16),
            pltpu.VMEM((128, 128), F32),
            pltpu.SemaphoreType.DMA((3,)),
        ],
        name="query",
    )
    mine = jnp.stack([x_keep, turn(from_xzh)])
    a_own = pair(a_pair, far_pair(a_half, turn(from_a5)))
    from_ax = swap(a_own, BIT_X)
    from_ay = swap(a_own, BIT_Y)
    from_qc = swap(turn(q_give), BIT_C)
    b_half = turn(from_b4)
    from_b5 = swap(b_half, BIT_ZL)
    q_unit = join(c, q_keep, turn(from_qc), 1)
    from_qzl = swap(q_unit[1], BIT_ZL)
    q_pair = jnp.stack([q_unit[0], turn(from_qzl)])
    from_qzh = swap(q_pair, BIT_ZH)
    b_own = pair(b_pair, far_pair(b_half, turn(from_b5)))
    from_xzl = swap(mine, BIT_ZL, b_own)

    def halves_of(array, axis):
        half = array.shape[axis] // 2
        return (
            lax.slice_in_dim(array, 0, half, axis=axis),
            lax.slice_in_dim(array, half, 2 * half, axis=axis),
        )

    def corner_hop(over_x, over_y, axis, after=None):
        return (
            swap(halves_of(over_y, axis)[0], BIT_X, after),
            swap(halves_of(over_x, axis)[1], BIT_Y, after),
        )

    a_y = turn(from_ay)
    a_x = turn(from_ax)
    q_own = pair(q_pair, turn(from_qzh))
    from_qy = swap(q_own, BIT_Y, a_y)
    from_qx = swap(q_own, BIT_X, a_x)
    x_own = pair(mine, turn(from_xzl))
    from_xc = swap(x_own, BIT_C)
    q_y = turn(from_qy)
    q_x = turn(from_qx)
    x_other = turn(from_xc)
    from_qxy = corner_hop(q_x, q_y, 0)
    from_a0c = swap(a_own, BIT_C, q_x)
    from_a1c = swap(a_x, BIT_C, q_x)
    q_xy = pair(turn(from_qxy[0]), turn(from_qxy[1]))
    from_bx = swap(b_own, BIT_X, q_xy)
    from_by = swap(b_own, BIT_Y, q_xy)
    a_c = [turn(from_a0c), turn(from_a1c)]
    from_a2c = swap(a_y, BIT_C, a_c[1])
    from_b0c = swap(b_own, BIT_C, a_c[1])
    w_attend = [q_own, q_x, q_y, q_xy]

    head_scratch = [pltpu.VMEM((width, wide), BF16), pltpu.VMEM((2, 4, x_rows, width), BF16)]
    saved = [((3, total, cut), BF16), ((total, cut), F32), ((16, total), F32)]
    results = call(
        attend_kernel,
        [((2, own, cut), BF16)] * 2 + saved + [((16, width), F32)],
        [place, *w_attend, x_own, tie(x_other, a_c[1])],
        scratch=[head_scratch[0], pltpu.VMEM((total, 128), F32)],
        name="attend",
    )
    context_keep, context_give, qkv, context_wide, rows_saved, vec = results
    context_give = turn(context_give)
    a_c.append(turn(from_a2c))
    b_c = [turn(from_b0c)]
    got = turn(swap(context_give, BIT_C, b_c[0]))
    from_czl = swap(pair(context_keep[1:], got[1:]), BIT_ZL)
    context = [context_keep, got]
    b_y = turn(from_by)
    b_x = turn(from_bx)
    from_bxy = swap(b_x, BIT_Y)
    from_axy = swap(a_y, BIT_X, b_x)
    from_b1c = swap(b_x, BIT_C, b_y)
    from_b2c = swap(b_y, BIT_C, b_x)
    context.append(turn(from_czl))
    b_c.append(turn(from_b1c))
    b_c.append(turn(from_b2c))
    b_inner = jnp.transpose(tie(vec, got)[8:12].reshape(4, 32, shard), (1, 0, 2)).reshape(1, hidden)
    b_inner = turn(b_inner)
    cot_keep = lax.dynamic_index_in_dim(cotangent[:, 0], zh, 0, False)
    cot_give = turn(lax.dynamic_index_in_dim(cotangent[:, 0], 1 - zh, 0, False))
    from_cot = swap(cot_give, BIT_ZH)
    a_xy = turn(from_axy)
    from_a3c = swap(a_xy, BIT_C)
    b_xy = turn(from_bxy)
    from_b3c = swap(b_xy, BIT_C)
    a_c.append(turn(from_a3c))
    b_c.append(turn(from_b3c))
    a_pieces = [a_own, a_x, a_y, a_xy, *a_c]
    b_pieces = [b_own, b_x, b_y, b_xy, *b_c]

    whole = [
        pltpu.VMEM((width, width), BF16),
        pltpu.VMEM((width, hidden), BF16),
        pltpu.VMEM((hidden, width), BF16),
        pltpu.SemaphoreType.DMA((192,)),
    ]
    results = call(
        forward_kernel,
        [
            ((own, width), BF16), ((own, width), F32), ((own, 128), F32), ((own, width), BF16),
            ((own, width), F32), ((own, 128), F32), ((own, hidden), BF16), ((own, hidden), F32),
        ],
        [place, *context, mine, turn(vec), b_inner, *a_pieces, *b_pieces],
        ["vmem"] * 6 + (["hbm"] * 7 + ["any"]) * 2,
        whole,
        flops=4 * own * width * hidden * 2,
        traffic=4 * width * hidden * 2,
        name="forward",
    )
    second_out, second_normed, second_inverse, first_low, normed, inverse, active, slope = results
    second_normed = turn(second_normed)

    def to_place(kept, other):
        return join(zh, kept[None], other[None].astype(kept.dtype))[:, None]

    def first_hop(parts, after=None):
        return swap(parts[0], BIT_X, after), swap(parts[1], BIT_Y, after)

    def second_hop(rest, from_x, from_y):
        left, right = add_low(rest[0], from_x), add_low(rest[1], from_y)
        return (left[0], right[0]), swap(left[1], BIT_Y), swap(right[1], BIT_X)

    def last_hop(owns, from_y, from_x):
        return jnp.concatenate([add_low(owns[0], from_y), add_low(owns[1], from_x)], 1)

    def zl_halves(array):
        half = array.shape[1] // 2
        one, two = array[:, :half], array[:, half:]
        return jnp.where(zl == 0, one, two), jnp.where(zl == 0, two, one)

    cot_other = turn(from_cot)
    b_shape, a_shape = ((2, 2, 4, 2 * unit, cols), BF16), ((2, 2, 4, 5 * unit // 2, cols), BF16)
    b_give, b_give_rest, b_keep, b_keep_rest, second_grad, outer_grad, sums_a = call(
        outer_grad_kernel,
        [b_shape, b_shape, b_shape, b_shape, ((own, width), F32), ((own, width), BF16), ((8, width), F32)],
        [place, cot_keep, cot_other, second_normed, second_inverse, vec, active],
        name="outer_grad",
    )
    got = turn(swap(b_give, BIT_C))
    b_first = [add_low(b_keep[0], got[0]), add_low(b_keep[1], got[1])]
    from_bx1, from_by1 = first_hop(b_first)
    from_brest = swap(b_give_rest, BIT_C, got)
    outer_grad = tie(outer_grad, b_first[1])
    results = call(
        middle_kernel,
        [
            ((own, hidden), BF16), ((own, width), F32), ((own, width), BF16), ((own, cut), BF16),
            ((own, cut), BF16), ((2, own, cut), BF16), ((8, width), F32), ((8, hidden), F32),
        ],
        [place, outer_grad, slope, second_grad, normed, inverse, vec, *a_pieces, *b_pieces],
        ["vmem"] * 6 + ["hbm"] * 16,
        whole,
        flops=4 * own * width * hidden,
        traffic=6 * width * hidden,
        name="middle",
    )
    inner_grad, first_grad, attended_grad, dc_own, dc_zl, dc_give, sums_c, sums_b = results
    inner_grad = turn(inner_grad)
    a_give, a_give_rest, a_keep, a_keep_rest = call(
        inner_grad_kernel,
        [a_shape] * 4,
        [place, first_low, inner_grad, attended_grad, *context],
        scratch=[pltpu.VMEM((width, own), BF16), pltpu.VMEM((4, own, cut), BF16)],
        name="inner_grad",
    )
    a_give = turn(a_give)
    got_x, got_y = turn(from_bx1), turn(from_by1)
    b_rest = add_low(b_keep_rest, turn(from_brest))
    from_dcc = swap(dc_give, BIT_C, got_y)
    from_out = swap(second_out[rows:], BIT_ZH, got_y)
    b_owns, from_by2, from_bx2 = second_hop(b_rest, got_x, got_y)
    from_agive = swap(a_give, BIT_C, got_y)
    dc_c = turn(from_dcc)
    from_dczl = swap(jnp.stack([dc_zl, dc_c[1]]), BIT_ZL)
    from_arest = swap(a_give_rest, BIT_C, dc_c)
    got = turn(from_agive)
    a_first = [add_low(a_keep[0], got[0]), add_low(a_keep[1], got[1])]
    from_ax1, from_ay1 = first_hop(a_first)
    a_rest = add_low(a_keep_rest, turn(from_arest))
    dc = [dc_own, turn(from_dczl), dc_c]
    results = call(
        attend_back_kernel,
        [
            ((total, wide), BF16), ((8, wide), F32),
            ((own, width), F32), ((own, width), BF16), ((2, own, width), BF16),
        ],
        [place, qkv, context_wide, rows_saved, *w_attend, *dc],
        ["hbm"] * 7 + ["vmem"] * 3,
        scratch=[pltpu.VMEM(*shape) for shape in saved]
        + [
            pltpu.VMEM((HEAD, total), F32),
            pltpu.VMEM((8, total), F32),
            pltpu.VMEM((total, cut), BF16),
            pltpu.VMEM((total, 128), F32),
            head_scratch[0],
            pltpu.SemaphoreType.DMA((20,)),
        ],
        name="attend_back",
    )
    grads, sums_d, x_part, x_zl, x_give = results
    grads = turn(grads)
    outputs = to_place(second_out[:rows], turn(from_out))
    b_own = last_hop(b_owns, turn(from_by2), turn(from_bx2))
    from_bzh = swap(b_own[2:], BIT_ZH)
    got_x, got_y = turn(from_ax1), turn(from_ay1)
    a_owns, from_ay2, from_ax2 = second_hop(a_rest, got_x, got_y)
    from_xgive = swap(x_give, BIT_C, got_y)
    got = turn(from_xgive)
    x_zl = add_low(x_zl, got[1])
    x_part = x_part + got[0].astype(F32)
    from_xzl = swap(x_zl, BIT_ZL)
    grads = tie(grads, got)
    q_first, q_rest = call(
        attend_weight_kernel,
        [((2, 2, 4, shard, wide), BF16)] * 2,
        [place, x_own, x_other, grads, sums_d, sums_a, sums_b, sums_c],
        ["hbm"] * 2 + ["vmem"] * 5,
        scratch=[
            pltpu.VMEM((width, total), BF16),
            head_scratch[1],
            pltpu.VMEM((width, 128), F32),
            pltpu.VMEM((hidden, 128), F32),
            pltpu.SemaphoreType.DMA((2,)),
        ],
        name="attend_weight",
    )
    q_first = turn(q_first)
    a_own = last_hop(a_owns, turn(from_ay2), turn(from_ax2))
    a_halves = zl_halves(a_own[2:])
    b_own = add_low(b_own[:2], turn(from_bzh))
    from_az1 = swap(jnp.concatenate([a_halves[1][1:], a_halves[1][:1]]), BIT_ZL)
    from_qx1, from_qy1 = first_hop(q_first, a_own)
    a_far = add_low(a_halves[0], turn(from_az1))
    from_az2 = swap(a_far, BIT_ZH)
    got_x, got_y = turn(from_qx1), turn(from_qy1)
    q_owns, from_qy2, from_qx2 = second_hop(q_rest, got_x, got_y)
    from_bzl = swap(b_own[1], BIT_ZL, got_y)
    x_far = turn(from_xzl)
    x_grad = first_grad + (x_part + x_far.astype(F32))
    from_xzh = swap(low(x_grad[rows:]), BIT_ZH)

    def core_halves(array, axis):
        half = array.shape[axis] // 2
        first_half = lax.slice_in_dim(array, 0, half, axis=axis)
        last_half = lax.slice_in_dim(array, half, 2 * half, axis=axis)
        return jnp.where(c == 0, first_half, last_half), jnp.where(c == 0, last_half, first_half)

    q_own = last_hop(q_owns, turn(from_qy2), turn(from_qx2))
    from_qzh = swap(q_own[2:], BIT_ZH)
    got = turn(from_az2)
    empty = jnp.zeros_like(got)
    a_own = add_low(a_own[:2], join(zl, got, empty, 1))
    from_azl = swap(a_own[1], BIT_ZL)
    b_mine, b_theirs = core_halves(b_own[0].astype(F32) + turn(from_bzl).astype(F32), 0)
    from_bc = swap(low(b_theirs), BIT_C)
    q_own = add_low(q_own[:2], turn(from_qzh))
    from_qzl = swap(q_own[1], BIT_ZL)
    a_last = (a_own[0].astype(F32) + turn(from_azl).astype(F32)).reshape(5, unit, cols)
    a_mine, a_theirs = core_halves(a_last, 1)
    from_ac = swap(low(a_theirs), BIT_C)
    outer_owned = join(c, b_mine, turn(from_bc).astype(F32), 1)
    q_two = jnp.stack([q_own[0], turn(from_qzl)])
    q_mine, q_theirs = core_halves(q_two, 1)
    from_qc = swap(q_theirs, BIT_C)
    input_grad = to_place(x_grad[:rows], turn(from_xzh))
    a_got = turn(from_ac)
    q_got = turn(from_qc)
    results = call(
        last_kernel,
        [((shard, width), F32)] * 4 + [((shard, hidden), F32), ((16, 128), F32)],
        [place, q_mine, q_got, a_mine, a_got],
        scratch=[
            pltpu.VMEM((3, shard, width), F32),
            pltpu.VMEM((shard, width), F32),
            pltpu.VMEM((shard, hidden), F32),
            pltpu.SemaphoreType.DMA((5,)),
        ],
        out_spaces=["hbm"] * 5 + ["vmem"],
        name="last",
    )
    query_owned, key_owned, value_owned, output_owned, inner_owned, owned = results
    owned = owned[:12, :shard]
    return (
        outputs,
        input_grad,
        query_owned,
        key_owned,
        value_owned,
        output_owned,
        owned[0],
        owned[1],
        owned[2],
        owned[3],
        owned[4],
        inner_owned,
        owned[8:12].reshape(-1),
        outer_owned,
        owned[5],
        owned[6],
        owned[7],
    )


def solution(mesh):
    fast = mesh.shape["dp"] == 4 and mesh.shape["sp"] == 8
    body = body_fast if fast else body_general
    in_specs = (
        P(None, "dp", "sp", None),
        P(None, "dp", "sp"),
        P(None, "dp", "sp", None),
        P(("dp", "sp"), None),
        P(("dp", "sp"), None),
        P(("dp", "sp"), None),
        P(("dp", "sp"), None),
        P(("dp", "sp")),
        P(("dp", "sp")),
        P(("dp", "sp")),
        P(("dp", "sp")),
        P(("dp", "sp")),
        P(("dp", "sp"), None),
        P(("dp", "sp")),
        P(("dp", "sp"), None),
        P(("dp", "sp")),
        P(("dp", "sp")),
        P(("dp", "sp")),
    )
    out_specs = (
        P(None, "dp", "sp", None),
        P(None, "dp", "sp", None),
        P(("dp", "sp"), None),
        P(("dp", "sp"), None),
        P(("dp", "sp"), None),
        P(("dp", "sp"), None),
        P(("dp", "sp")),
        P(("dp", "sp")),
        P(("dp", "sp")),
        P(("dp", "sp")),
        P(("dp", "sp")),
        P(("dp", "sp"), None),
        P(("dp", "sp")),
        P(("dp", "sp"), None),
        P(("dp", "sp")),
        P(("dp", "sp")),
        P(("dp", "sp")),
    )
    return jax.shard_map(body, mesh=mesh, in_specs=in_specs, out_specs=out_specs, check_vma=False)
```
